32 devices in a mesh: row: 8 (over z, y), col: 4 (over x, core).
Axes of the slice: x: 2, y: 2, z: 4, core: 2. Of those that a mesh axis runs over, the one named last changes fastest.
Arguments:
- inv_interior: bfloat16 [64, 1024, 1024], P(('row', 'col')), may hold values from -1 to 3
- coupling: bfloat16 [64, 1024, 512], P(('row', 'col')), may hold values from -0.375 to 0.375
- boundary_stiff: bfloat16 [64, 512, 512], P(('row', 'col')), may hold values from -6 to 6
- mass_interior: float32 [64, 1024], P(('row', 'col')), may hold values from 0.5 to 2
- mass_boundary: float32 [64, 512], P(('row', 'col')), may hold values from 0.5 to 2
- block_map: int32 [64, 4], P(('row', 'col')), may hold values from 0 to 127, as said below
- modes: bfloat16 [16384, 1024], P('col', 'row'), may hold values from -0.046875 to 0.046875
Outputs:
- iface_stiff: bfloat16 [16384, 16384], P('row', 'col')
- iface_mass: bfloat16 [16384, 16384], P('row', 'col')
- reduced_stiff: float32 [1024, 1024], P(('row', 'col'))
- reduced_mass: float32 [1024, 1024], P(('row', 'col'))
- mass_diagonal: float32 [16384], P(('row', 'col'))
The draws below stay inside these ranges and needn't reach their ends.
Inputs may be any that keep to these rules, and one draw needn't show every extreme that they name: Interface block p belongs to tile row p // 16 and tile column p // 32; the pair (block_map[s, a], block_map[s, b]) belongs to the tile of its row's tile row and its column's tile column. Over the 2 substructures of one device (aligned blocks of rows), no two triples (s, a, b) fall into the same tile, and in every draw some tile receives a pair from every device.
All inputs are finite; a program needn't handle non-finite values.
Results may differ from the reference program's by a relative error of at most 0.0058.
Values may be sent and summed in bfloat16 or wider, within the bound.
No kernel may reach another device: no remote copies, remote signals or barrier semaphores. Data moves between devices by JAX's collectives and lax.ppermute only.
A program may use at most 192 MiB of HBM per device.

```python
import math
import jax
import jax.numpy as jnp
from jax import lax

NI = 1024
NBD = 512
BLK = 128
NIF = 16384
NM = 1024
NB = 4
NBLK = 128
SUBS = 64
TILE_ROWS = 2048
TILE_COLS = 4096


def draw_inv_interior(key, part):
    diag_key, noise_key = jax.random.split(jax.random.fold_in(key, 11))
    diagonal = jax.random.uniform(diag_key, (SUBS, NI), jnp.float32, 0.5, 2.0)
    noise = jax.random.normal(noise_key, (SUBS, NI, NI), jnp.float32) * (0.5 / math.sqrt(NI))
    symmetric = (noise + jnp.swapaxes(noise, 1, 2)) * (1.0 / math.sqrt(2.0))
    whole = symmetric + diagonal[:, :, None] * jnp.eye(NI, dtype=jnp.float32)[None, :, :]
    return whole.astype(jnp.bfloat16)


def fix_first(order, common_col):
    position = jnp.argmax(order == common_col).astype(jnp.int32)
    return order.at[position].set(order[0]).at[0].set(common_col)


def draw_block_map(key, part):
    row_groups = NIF // TILE_ROWS
    col_groups = NIF // TILE_COLS
    device_count = row_groups * col_groups
    per_col = row_groups // col_groups
    group_blocks = TILE_ROWS // BLK
    base = jax.random.fold_in(key, 23)
    common_key, order_key, offset_key = jax.random.split(base, 3)
    common_col = jax.random.randint(common_key, (), 0, col_groups).astype(jnp.int32)
    order_keys = jax.random.split(order_key, device_count * per_col)
    orders = jax.vmap(lambda single: jax.random.permutation(single, col_groups))(order_keys).astype(jnp.int32)
    orders = orders.reshape(device_count, per_col, col_groups)
    leading = jax.vmap(fix_first, in_axes=(0, None))(orders[:, 0, :], common_col)
    orders = orders.at[:, 0, :].set(leading)
    parity = jnp.arange(per_col, dtype=jnp.int32)[None, :, None]
    groups = (orders * per_col + parity).reshape(device_count, per_col * col_groups)
    offsets = jax.random.randint(offset_key, (device_count, per_col * col_groups), 0, group_blocks).astype(jnp.int32)
    blocks = groups * group_blocks + offsets
    return blocks.reshape(SUBS, NB).astype(jnp.int32)


def steps_of(rng, dims, cuts, least, high):
    def one(dim, shards_of):
        heights = jax.random.uniform(jax.random.fold_in(jax.random.fold_in(rng, 6), dim), (shards_of,), jnp.float32, least / len(cuts), high / len(cuts))
        return jnp.repeat(jnp.exp(heights), dims[dim] // shards_of).reshape((-1,) + (1,) * (len(dims) - dim - 1))

    level = one(*cuts[0])
    for cut in cuts[1:]:
        level = level * one(*cut)
    return level


def normal_values(rng, dims, spread, bound, shards=(), kind=jnp.bfloat16):
    values = spread * jax.random.normal(rng, dims, jnp.float32)
    if shards:
        values = values * steps_of(rng, dims, shards, -0.22, 0.18)
    return jnp.clip(values, -bound, bound).astype(kind)


def setup_inputs(seed: int = 0) -> dict:
    key_of = jax.random.split(jax.random.key(seed), 8)
    return {
        "inv_interior": draw_inv_interior(jax.random.fold_in(key_of[7], 71), 0),
        "coupling": normal_values(key_of[1], (SUBS, NI, NBD), (NI // 4) ** -0.5, 0.375, ((0, 32),)),
        "boundary_stiff": normal_values(key_of[2], (SUBS, NBD, NBD), 1.0, 6.0, ((0, 32),)),
        "mass_interior": jnp.clip(jnp.exp(math.log(2.0) - 1.3862944 * jax.random.uniform(key_of[3], (SUBS, NI), jnp.float32) ** steps_of(key_of[3], (SUBS, NI), ((0, 32),), -0.2, 0.2)), 0.5, 2.0),
        "mass_boundary": jnp.clip(jnp.exp(math.log(2.0) - 1.3862944 * jax.random.uniform(key_of[4], (SUBS, NBD), jnp.float32) ** steps_of(key_of[4], (SUBS, NBD), ((0, 32),), -0.2, 0.2)), 0.5, 2.0),
        "block_map": draw_block_map(jax.random.fold_in(key_of[7], 71), 0),
        "modes": normal_values(key_of[6], (NIF, NM), NIF ** -0.5, 0.046875, ((0, 4), (1, 8))),
    }


def condense(pieces):
    inverse, couple, stiffness, interior_mass, boundary_mass = pieces
    static_modes = (-jnp.dot(inverse, couple, preferred_element_type=jnp.float32)).astype(jnp.bfloat16)
    stiff_cond = stiffness.astype(jnp.float32) + jnp.dot(couple.T, static_modes, preferred_element_type=jnp.float32)
    weighted = (static_modes.astype(jnp.float32) * interior_mass[:, None]).astype(jnp.bfloat16)
    mass_cond = jnp.dot(static_modes.T, weighted, preferred_element_type=jnp.float32) + jnp.diag(boundary_mass)
    return jnp.stack([stiff_cond, mass_cond])


def reference(inv_interior, coupling, boundary_stiff, mass_interior, mass_boundary, block_map, modes):
    condensed = lax.map(condense, (inv_interior, coupling, boundary_stiff, mass_interior, mass_boundary))
    blocks = condensed.reshape(SUBS, 2, NB, BLK, NB, BLK).transpose(0, 2, 4, 1, 3, 5)
    block_rows = jnp.broadcast_to(block_map[:, :, None], (SUBS, NB, NB))
    block_cols = jnp.broadcast_to(block_map[:, None, :], (SUBS, NB, NB))
    assembled = jnp.zeros((NBLK, NBLK, 2, BLK, BLK), jnp.float32).at[block_rows, block_cols].add(blocks)
    full_pair = assembled.transpose(2, 0, 3, 1, 4).reshape(2, NIF, NIF)
    iface_stiff = full_pair[0].astype(jnp.bfloat16)
    mass_full = full_pair[1]
    mass_diagonal = jnp.diagonal(mass_full)
    positions = jnp.arange(NIF, dtype=jnp.int32)
    iface_mass = mass_full.at[positions, positions].set(jnp.float32(0.0)).astype(jnp.bfloat16)
    modes_exact = modes.astype(jnp.float32)
    stiff_image = jnp.dot(iface_stiff, modes, preferred_element_type=jnp.float32)
    mass_image = jnp.dot(iface_mass, modes, preferred_element_type=jnp.float32) + mass_diagonal[:, None] * modes_exact
    image = jnp.concatenate([stiff_image, mass_image], 1)
    reduced = jnp.dot(modes_exact.T, image, precision=lax.Precision.HIGHEST, preferred_element_type=jnp.float32)
    return iface_stiff, iface_mass, reduced[:, :NM], reduced[:, NM:], mass_diagonal
```

```python
import jax
import jax.numpy as jnp
from jax import lax
from jax.experimental import pallas as pl
from jax.experimental.pallas import tpu as pltpu
from jax.sharding import PartitionSpec as P

BLK = 128
AXES = ("row", "col")
F32 = jnp.float32
BF16 = jnp.bfloat16
VMEM = pl.BlockSpec(memory_space=pltpu.VMEM)
SMEM = pl.BlockSpec(memory_space=pltpu.SMEM)
ANY = pl.BlockSpec(memory_space=pl.ANY)


def exchange(value):
    return lax.all_to_all(value, AXES, split_axis=0, concat_axis=0, tiled=True)


def pick_modes(table, modes, ratio, row_blocks):
    device_count, held = table.shape
    col_blocks, _, width = modes.shape

    def kernel(table_ref, modes_ref, out_ref):
        first = lax.axis_index("col") * ratio

        def one(device, carry):
            for k in range(held):
                block = table_ref[device, k]
                place = lax.div(block, row_blocks) - first

                @pl.when(jnp.logical_and(place >= 0, place < ratio))
                def _():
                    out_ref[device, place] = modes_ref[lax.rem(block, col_blocks)]

            return carry

        lax.fori_loop(0, device_count, one, 0)

    return pl.pallas_call(
        kernel,
        out_shape=jax.ShapeDtypeStruct((device_count, ratio, BLK, width), BF16),
        in_specs=[SMEM, VMEM],
        out_specs=VMEM,
        name="pick_modes",
    )(table, modes)


def condense(
    block_map,
    inv_interior,
    coupling,
    boundary_stiff,
    mass_interior,
    mass_boundary,
    device_count,
    col_count,
    row_blocks,
    col_blocks,
    share_blocks,
):
    local_subs, interior, boundary = coupling.shape
    per_sub = boundary // BLK

    def kernel(
        map_ref, inv_ref, cpl_ref, stiff_ref, mi_ref, mb_ref, out_ref, k_ref, m_ref, d_ref, share_ref
    ):
        sub = pl.program_id(0)
        couple = cpl_ref[0]
        static_modes = (-jnp.dot(inv_ref[0], couple, preferred_element_type=F32)).astype(BF16)
        contract = (((0,), (0,)), ((), ()))
        stiff = stiff_ref[0].astype(F32) + lax.dot_general(
            couple, static_modes, contract, preferred_element_type=F32
        )
        weighted = (static_modes.astype(F32) * mi_ref[0]).astype(BF16)
        mass = lax.dot_general(static_modes, weighted, contract, preferred_element_type=F32)
        eye = lax.broadcasted_iota(jnp.int32, (BLK, BLK), 0) == lax.broadcasted_iota(
            jnp.int32, (BLK, BLK), 1
        )
        for a in range(per_sub):
            block_a = map_ref[sub, a]
            rows = slice(a * BLK, (a + 1) * BLK)
            for b in range(per_sub):
                cols = slice(b * BLK, (b + 1) * BLK)
                owner = lax.div(block_a, row_blocks) * col_count + lax.div(
                    map_ref[sub, b], col_blocks
                )
                stiff_block = stiff[rows, cols].astype(BF16)
                mass_block = mass[rows, cols]
                if a == b:
                    diagonal = (
                        jnp.sum(jnp.where(eye, mass_block, 0.0), axis=0, keepdims=True)
                        + mb_ref[0, :, cols]
                    )
                    d_ref[0, :, cols] = diagonal
                    share_ref[lax.div(block_a, share_blocks)] = diagonal
                    mass_block = jnp.where(eye, 0.0, mass_block)
                mass_block = mass_block.astype(BF16)
                out_ref[owner, 0] = stiff_block
                out_ref[owner, 1] = mass_block
                k_ref[0, rows, cols] = stiff_block
                m_ref[0, rows, cols] = mass_block

    def whole(shape):
        return pl.BlockSpec(shape, lambda s: (0,) * len(shape))

    def piece(*shape):
        return pl.BlockSpec((1,) + shape, lambda s: (s, 0, 0))

    out_blocks = (device_count, 2, BLK, BLK)
    shares = (device_count, 1, BLK)
    return pl.pallas_call(
        kernel,
        grid=(local_subs,),
        in_specs=[
            SMEM,
            piece(interior, interior),
            piece(interior, boundary),
            piece(boundary, boundary),
            piece(interior, 1),
            piece(1, boundary),
        ],
        out_specs=[
            whole(out_blocks),
            piece(boundary, boundary),
            piece(boundary, boundary),
            piece(1, boundary),
            whole(shares),
        ],
        out_shape=[
            jax.ShapeDtypeStruct(out_blocks, BF16),
            jax.ShapeDtypeStruct((local_subs, boundary, boundary), BF16),
            jax.ShapeDtypeStruct((local_subs, boundary, boundary), BF16),
            jax.ShapeDtypeStruct((local_subs, 1, boundary), F32),
            jax.ShapeDtypeStruct(shares, F32),
        ],
        name="condense",
    )(
        block_map,
        inv_interior,
        coupling,
        boundary_stiff,
        mass_interior[:, :, None],
        mass_boundary[:, None, :],
    )


def gather_modes(block_map, fetched, row_blocks):
    row_count, col_count, ratio, _, width = fetched.shape
    local_subs, per_sub = block_map.shape
    depth = local_subs * per_sub * BLK
    modes = row_count * width

    def kernel(map_ref, in_ref, q_ref, t_ref):
        for s in range(local_subs):
            for a in range(per_sub):
                tile_row = lax.div(map_ref[s, a], row_blocks)
                c = lax.div(tile_row, ratio)
                h = lax.rem(tile_row, ratio)
                k = (s * per_sub + a) * BLK
                for r in range(row_count):
                    block = in_ref[r, c, h]
                    q_ref[k : k + BLK, r * width : (r + 1) * width] = block
                    t_ref[r * width : (r + 1) * width, k : k + BLK] = block.T

    return pl.pallas_call(
        kernel,
        out_shape=[
            jax.ShapeDtypeStruct((depth, modes), BF16),
            jax.ShapeDtypeStruct((modes, depth), BF16),
        ],
        in_specs=[SMEM, VMEM],
        out_specs=[VMEM, VMEM],
        name="gather_modes",
    )(block_map, fetched)


def project(q, qt, matrix, diagonal, dims):
    z_size, y_size, x_size = dims
    depth, modes = q.shape
    local_subs, boundary, _ = matrix.shape
    groups = z_size * y_size * x_size
    share = modes // (2 * groups)
    chunk = modes // 2
    pairs = chunk // (2 * share)
    operands = [q, qt, matrix] + ([] if diagonal is None else [diagonal])

    def kernel(*refs):
        q_ref, t_ref, m_ref = refs[:3]
        send_ref, keep_ref, y_ref = refs[-3:]
        row, col = lax.axis_index("row"), lax.axis_index("col")
        my_z, my_y = lax.div(row, y_size), lax.rem(row, y_size)
        my_x, my_core = lax.div(col, 2), lax.rem(col, 2)
        step = pl.program_id(0)
        for s in range(local_subs):
            span = slice(s * boundary, (s + 1) * boundary)
            left = t_ref[:, span]
            y = jnp.dot(left, m_ref[s], preferred_element_type=F32)
            if diagonal is not None:
                y = y + left.astype(F32) * refs[3][s]
            y_ref[:, span] = y.astype(BF16)
        out = jnp.dot(y_ref[...], q_ref[...], preferred_element_type=F32)
        for i in range(pairs):
            group = step * pairs + i
            x = lax.rem(group, x_size)
            y = lax.rem(lax.div(group, x_size), y_size)
            z = lax.div(group, x_size * y_size)
            slot = ((y ^ my_y) * x_size + (x ^ my_x)) * z_size + (z ^ my_z)
            even = out[2 * i * share : (2 * i + 1) * share]
            odd = out[(2 * i + 1) * share : (2 * i + 2) * share]
            mine = my_core == 0
            keep_ref[slot] = jnp.where(mine, even, odd)
            send_ref[slot] = jnp.where(mine, odd, even).astype(BF16)

    def whole(*shape):
        return pl.BlockSpec(shape, lambda i: (0,) * len(shape))

    return pl.pallas_call(
        kernel,
        grid=(modes // chunk,),
        in_specs=[
            whole(depth, modes),
            pl.BlockSpec((chunk, depth), lambda i: (i, 0)),
            whole(local_subs, boundary, boundary),
        ]
        + ([] if diagonal is None else [whole(local_subs, 1, boundary)]),
        out_specs=[whole(groups, share, modes), whole(groups, share, modes)],
        out_shape=[
            jax.ShapeDtypeStruct((groups, share, modes), BF16),
            jax.ShapeDtypeStruct((groups, share, modes), F32),
        ],
        scratch_shapes=[pltpu.VMEM((chunk, depth), BF16)],
        name="project",
    )(*operands)


def reduce_shares(send, keep, dims):
    z_size, y_size, x_size = dims

    def partners(dz, dy, dx, core):
        pairs = []
        for z in range(z_size):
            for y in range(y_size):
                for x in range(x_size):
                    for k in range(2):
                        pairs.append(
                            (
                                ((z * y_size + y) * x_size + x) * 2 + k,
                                (((z ^ dz) * y_size + (y ^ dy)) * x_size + (x ^ dx)) * 2
                                + (k ^ core),
                            )
                        )
        return pairs

    plane = y_size * x_size
    summed = keep + lax.ppermute(send, AXES, partners(0, 0, 0, 1)).astype(F32)
    summed = summed.reshape((plane, z_size) + summed.shape[1:])
    total = summed[0]
    for d in range(1, plane):
        total = total + lax.ppermute(
            summed[d].astype(BF16), AXES, partners(0, d // x_size, d % x_size, 0)
        ).astype(F32)
    result = total[0]
    for d in range(1, z_size):
        result = result + lax.ppermute(
            total[d].astype(BF16), AXES, partners(d, 0, 0, 0)
        ).astype(F32)
    return result


def place(arrived, order, slots, stiff_tile, mass_tile, col_blocks):
    count = arrived.shape[0]
    limit = stiff_tile.shape[0] // BLK * col_blocks

    def kernel(order_ref, slot_ref, in_ref, _s, _m, stiff_ref, mass_ref, sums_ref, sem):
        def copies(j):
            slot = slot_ref[j]
            row = lax.div(slot, col_blocks) * BLK
            col = lax.rem(slot, col_blocks) * BLK
            return [
                pltpu.make_async_copy(
                    sums_ref.at[j, i], ref.at[pl.ds(row, BLK), pl.ds(col, BLK)], sem.at[j, i]
                )
                for i, ref in enumerate((stiff_ref, mass_ref))
            ]

        def last(j):
            ahead = slot_ref[jnp.minimum(j + 1, count - 1)]
            ends = jnp.logical_or(j == count - 1, ahead != slot_ref[j])
            return jnp.logical_and(slot_ref[j] < limit, ends)

        def one(j, total):
            block = in_ref[order_ref[j]].astype(F32)
            same = jnp.logical_and(j > 0, slot_ref[jnp.maximum(j - 1, 0)] == slot_ref[j])
            total = jnp.where(same, total + block, block)
            sums_ref[j] = total.astype(BF16)

            @pl.when(last(j))
            def _():
                for copy in copies(j):
                    copy.start()

            return total

        lax.fori_loop(0, count, one, jnp.zeros((2, BLK, BLK), F32))

        def wait(j, carry):
            @pl.when(last(j))
            def _():
                for copy in copies(j):
                    copy.wait()

            return carry

        lax.fori_loop(0, count, wait, 0)

    return pl.pallas_call(
        kernel,
        in_specs=[SMEM, SMEM, VMEM, ANY, ANY],
        out_specs=[ANY, ANY],
        out_shape=[
            jax.ShapeDtypeStruct(stiff_tile.shape, BF16),
            jax.ShapeDtypeStruct(mass_tile.shape, BF16),
        ],
        input_output_aliases={3: 0, 4: 1},
        scratch_shapes=[
            pltpu.VMEM((count, 2, BLK, BLK), BF16),
            pltpu.SemaphoreType.DMA((count, 2)),
        ],
        name="place",
    )(order, slots, arrived, stiff_tile, mass_tile)


def body(inv_interior, coupling, boundary_stiff, mass_interior, mass_boundary, block_map, modes):
    row_count = lax.axis_size("row")
    col_count = lax.axis_size("col")
    device_count = row_count * col_count
    local_subs, _, boundary = coupling.shape
    per_sub = boundary // BLK
    tile_cols, width = modes.shape
    tile_rows = tile_cols * col_count // row_count
    row_blocks = tile_rows // BLK
    col_blocks = tile_cols // BLK
    ratio = row_count // col_count
    share_blocks = row_blocks // col_count
    x_size = col_count // 2
    y_size = x_size
    dims = (row_count // y_size, y_size, x_size)
    row_index = lax.axis_index("row")
    col_index = lax.axis_index("col")
    held = local_subs * per_sub

    table = exchange(jnp.broadcast_to(block_map.reshape(1, held), (device_count, held)))
    wanted = pick_modes(table, modes.reshape(col_blocks, BLK, width), ratio, row_blocks)
    fetched = exchange(wanted)

    outgoing, stiff, mass, diagonal, shares = condense(
        block_map,
        inv_interior,
        coupling,
        boundary_stiff,
        mass_interior,
        mass_boundary,
        device_count,
        col_count,
        row_blocks,
        col_blocks,
        share_blocks,
    )
    zeros = jnp.zeros((2, tile_rows, tile_cols), BF16)
    stiff_tile, mass_tile = zeros[0], zeros[1]
    outgoing, shares, fetched, stiff_tile, mass_tile = lax.optimization_barrier(
        (outgoing, shares, fetched, stiff_tile, mass_tile)
    )
    arrived = exchange(outgoing)
    arrived_shares = exchange(shares)

    q, qt = gather_modes(
        block_map, fetched.reshape(row_count, col_count, ratio, BLK, width), row_blocks
    )
    reduced_stiff = reduce_shares(*project(q, qt, stiff, None, dims), dims)
    reduced_mass = reduce_shares(*project(q, qt, mass, diagonal, dims), dims)

    me = row_index * col_count + col_index
    hits = table[:, :, None] == me * share_blocks + jnp.arange(share_blocks, dtype=jnp.int32)
    hits = jnp.any(hits, axis=1)
    mass_share = jnp.sum(jnp.where(hits[:, :, None], arrived_shares, 0.0), axis=0).reshape(-1)

    by_sub = table.reshape(device_count, local_subs, per_sub)
    row_slot = jnp.sum(
        jnp.where(by_sub // row_blocks == row_index, by_sub % row_blocks + 1, 0), axis=2
    )
    col_slot = jnp.sum(
        jnp.where(by_sub // col_blocks == col_index, by_sub % col_blocks + 1, 0), axis=2
    )
    both = jnp.logical_and(row_slot > 0, col_slot > 0)
    limit = row_blocks * col_blocks
    slot = jnp.min(jnp.where(both, (row_slot - 1) * col_blocks + col_slot - 1, limit), axis=1)
    ids = jnp.arange(device_count, dtype=jnp.int32)
    before = jnp.logical_or(
        slot[None, :] < slot[:, None],
        jnp.logical_and(slot[None, :] == slot[:, None], ids[None, :] < ids[:, None]),
    )
    rank = jnp.sum(before.astype(jnp.int32), axis=1)
    chosen = rank[None, :] == ids[:, None]
    order = jnp.sum(jnp.where(chosen, ids[None, :], 0), axis=1)
    slots = jnp.sum(jnp.where(chosen, slot[None, :], 0), axis=1)
    stiff_tile, mass_tile = place(arrived, order, slots, stiff_tile, mass_tile, col_blocks)
    return stiff_tile, mass_tile, reduced_stiff, reduced_mass, mass_share


def solution(mesh):
    return jax.shard_map(
        body,
        mesh=mesh,
        in_specs=(
            P(AXES, None, None),
            P(AXES, None, None),
            P(AXES, None, None),
            P(AXES, None),
            P(AXES, None),
            P(AXES, None),
            P("col", "row"),
        ),
        out_specs=(P("row", "col"), P("row", "col"), P(AXES, None), P(AXES, None), P(AXES)),
        check_vma=False,
    )
```

```python
from typing import NamedTuple

import jax
import jax.numpy as jnp
from jax import lax
from jax.experimental import pallas as pl
from jax.experimental.pallas import tpu as pltpu
from jax.sharding import PartitionSpec as P

BLK = 128
EXTRA = 16
AXES = ("row", "col")
F32 = jnp.float32
BF16 = jnp.bfloat16
VMEM = pl.BlockSpec(memory_space=pltpu.VMEM)
SMEM = pl.BlockSpec(memory_space=pltpu.SMEM)
ANY = pl.BlockSpec(memory_space=pl.ANY)


class Sizes(NamedTuple):
    devices: int
    cols: int
    ratio: int
    row_blocks: int
    col_blocks: int
    share_blocks: int


def exchange(value):
    return lax.all_to_all(value, AXES, split_axis=0, concat_axis=0, tiled=True)


def quotient(value, size):
    return lax.shift_right_logical(value, jnp.int32(size.bit_length() - 1))


def remainder(value, size):
    return value & jnp.int32(size - 1)


def describe(block_map, sizes):
    local_subs, per_sub = block_map.shape

    def kernel(map_ref, out_ref):
        shape = out_ref.shape
        device = lax.broadcasted_iota(jnp.int32, shape, 0)
        field = lax.broadcasted_iota(jnp.int32, shape, 1)
        row = quotient(device, sizes.cols)
        col = remainder(device, sizes.cols)
        zero = jnp.zeros(shape, jnp.int32)
        wanted, share = zero, zero - 1
        slot = zero + sizes.row_blocks * sizes.col_blocks
        for s in range(local_subs):
            row_slot, col_slot = zero - 1, zero - 1
            for a in range(per_sub):
                block = map_ref[s, a]
                tile_row = quotient(block, sizes.row_blocks)
                wanted = jnp.where(
                    col * sizes.ratio + field == tile_row, remainder(block, sizes.col_blocks), wanted
                )
                share = jnp.where(
                    device == quotient(block, sizes.share_blocks),
                    remainder(block, sizes.share_blocks),
                    share,
                )
                row_slot = jnp.where(row == tile_row, remainder(block, sizes.row_blocks), row_slot)
                col_slot = jnp.where(
                    col == quotient(block, sizes.col_blocks),
                    remainder(block, sizes.col_blocks),
                    col_slot,
                )
            both = jnp.logical_and(row_slot >= 0, col_slot >= 0)
            slot = jnp.where(both, row_slot * sizes.col_blocks + col_slot, slot)
        out_ref[...] = jnp.where(
            field < sizes.ratio, wanted, jnp.where(field == sizes.ratio, slot, share)
        )

    return pl.pallas_call(
        kernel,
        out_shape=jax.ShapeDtypeStruct((sizes.devices, BLK), jnp.int32),
        in_specs=[SMEM],
        out_specs=VMEM,
        name="describe",
    )(block_map)


def pick_modes(table, modes, ratio):
    device_count = table.shape[0]
    width = modes.shape[2]

    def kernel(table_ref, modes_ref, out_ref):
        def one(device, carry):
            for h in range(ratio):
                out_ref[device, h] = modes_ref[table_ref[device, h]]
            return carry

        lax.fori_loop(0, device_count, one, 0, unroll=4)

    return pl.pallas_call(
        kernel,
        out_shape=jax.ShapeDtypeStruct((device_count, ratio, BLK, width), BF16),
        in_specs=[SMEM, VMEM],
        out_specs=VMEM,
        name="pick_modes",
    )(table, modes)


def condense(
    block_map, inv_interior, coupling, boundary_stiff, mass_interior, mass_boundary, sizes
):
    local_subs, interior, boundary = coupling.shape
    per_sub = boundary // BLK
    tile_shape = (sizes.row_blocks * BLK, sizes.col_blocks * BLK)

    def kernel(
        map_ref,
        inv_ref,
        cpl_ref,
        stiff_ref,
        mi_ref,
        mb_ref,
        out_ref,
        k_ref,
        m_ref,
        d_ref,
        stiff_tile_ref,
        mass_tile_ref,
        zero_ref,
        sem,
    ):
        sub = pl.program_id(0)
        fills = [
            pltpu.make_async_copy(zero_ref, ref.at[pl.ds(i * BLK, BLK), :], sem.at[i, j])
            for i in range(sizes.row_blocks)
            for j, ref in enumerate((stiff_tile_ref, mass_tile_ref))
        ]

        @pl.when(sub == 0)
        def _():
            zero_ref[...] = jnp.zeros_like(zero_ref)
            for fill in fills:
                fill.start()

        couple = cpl_ref[0]
        static_modes = (-jnp.dot(inv_ref[0], couple, preferred_element_type=F32)).astype(BF16)
        contract = (((0,), (0,)), ((), ()))
        stiff = stiff_ref[0].astype(F32) + lax.dot_general(
            couple, static_modes, contract, preferred_element_type=F32
        )
        weighted = (static_modes.astype(F32) * mi_ref[0]).astype(BF16)
        mass = lax.dot_general(static_modes, weighted, contract, preferred_element_type=F32)
        eye = lax.broadcasted_iota(jnp.int32, (BLK, BLK), 0) == lax.broadcasted_iota(
            jnp.int32, (BLK, BLK), 1
        )
        level = lax.broadcasted_iota(jnp.int32, (EXTRA, BLK), 0)
        for a in range(per_sub):
            block_a = map_ref[sub, a]
            rows = slice(a * BLK, (a + 1) * BLK)
            for b in range(per_sub):
                cols = slice(b * BLK, (b + 1) * BLK)
                owner = quotient(block_a, sizes.row_blocks) * sizes.cols + quotient(
                    map_ref[sub, b], sizes.col_blocks
                )
                stiff_block = stiff[rows, cols].astype(BF16)
                mass_block = mass[rows, cols]
                if a == b:
                    diagonal = (
                        jnp.sum(jnp.where(eye, mass_block, 0.0), axis=0, keepdims=True)
                        + mb_ref[0, :, cols]
                    )
                    d_ref[0, :, cols] = diagonal
                    high = diagonal.astype(BF16).astype(F32)
                    middle = (diagonal - high).astype(BF16).astype(F32)
                    low = diagonal - high - middle
                    parts = jnp.where(level == 0, high, jnp.where(level == 1, middle, low))
                    share = quotient(block_a, sizes.share_blocks)
                    out_ref[share, 2 * BLK : 2 * BLK + EXTRA] = parts.astype(BF16)
                    mass_block = jnp.where(eye, 0.0, mass_block)
                mass_block = mass_block.astype(BF16)
                out_ref[owner, :BLK] = stiff_block
                out_ref[owner, BLK : 2 * BLK] = mass_block
                k_ref[0, rows, cols] = stiff_block
                m_ref[0, rows, cols] = mass_block

        @pl.when(sub == local_subs - 1)
        def _():
            for fill in fills:
                fill.wait()

    def piece(*shape):
        return pl.BlockSpec((1,) + shape, lambda s: (s, 0, 0))

    out_blocks = (sizes.devices, 2 * BLK + EXTRA, BLK)
    return pl.pallas_call(
        kernel,
        grid=(local_subs,),
        in_specs=[
            SMEM,
            piece(interior, interior),
            piece(interior, boundary),
            piece(boundary, boundary),
            piece(interior, 1),
            piece(1, boundary),
        ],
        out_specs=[
            pl.BlockSpec(out_blocks, lambda s: (0, 0, 0)),
            piece(boundary, boundary),
            piece(boundary, boundary),
            piece(1, boundary),
            ANY,
            ANY,
        ],
        out_shape=[
            jax.ShapeDtypeStruct(out_blocks, BF16),
            jax.ShapeDtypeStruct((local_subs, boundary, boundary), BF16),
            jax.ShapeDtypeStruct((local_subs, boundary, boundary), BF16),
            jax.ShapeDtypeStruct((local_subs, 1, boundary), F32),
            jax.ShapeDtypeStruct(tile_shape, BF16),
            jax.ShapeDtypeStruct(tile_shape, BF16),
        ],
        scratch_shapes=[
            pltpu.VMEM((BLK, tile_shape[1]), BF16),
            pltpu.SemaphoreType.DMA((sizes.row_blocks, 2)),
        ],
        name="condense",
    )(
        block_map,
        inv_interior,
        coupling,
        boundary_stiff,
        mass_interior[:, :, None],
        mass_boundary[:, None, :],
    )


def project(block_map, fetched, laid_out, matrix, diagonal, dims, row_blocks):
    z_size, y_size, x_size = dims
    local_subs, boundary, _ = matrix.shape
    depth = local_subs * boundary
    per_sub = boundary // BLK
    groups = z_size * y_size * x_size
    gathers = laid_out is None
    if gathers:
        row_count, _, ratio, _, width = fetched.shape
        modes = row_count * width
    else:
        modes = laid_out[0].shape[1]
    share = modes // (2 * groups)
    chunk = modes // 2
    pairs = chunk // (2 * share)

    def kernel(*refs):
        step = pl.program_id(0)
        if gathers:
            map_ref, in_ref, m_ref, send_ref, keep_ref, q_ref, t_ref, y_ref = refs

            @pl.when(step == 0)
            def _():
                for s in range(local_subs):
                    for a in range(per_sub):
                        tile_row = quotient(map_ref[s, a], row_blocks)
                        c = quotient(tile_row, ratio)
                        h = remainder(tile_row, ratio)
                        k = (s * per_sub + a) * BLK
                        for r in range(row_count):
                            block = in_ref[r, c, h]
                            q_ref[k : k + BLK, r * width : (r + 1) * width] = block
                            t_ref[r * width : (r + 1) * width, k : k + BLK] = block.T

            left_rows = pl.ds(pl.multiple_of(step * chunk, chunk), chunk)
        else:
            q_ref, t_ref, m_ref, d_ref, send_ref, keep_ref, y_ref = refs
            left_rows = slice(None)
        row, col = lax.axis_index("row"), lax.axis_index("col")
        my_z, my_y = quotient(row, y_size), remainder(row, y_size)
        my_x, my_core = quotient(col, 2), remainder(col, 2)
        for s in range(local_subs):
            span = slice(s * boundary, (s + 1) * boundary)
            left = t_ref[left_rows, span]
            y = jnp.dot(left, m_ref[s], preferred_element_type=F32)
            if diagonal is not None:
                y = y + left.astype(F32) * d_ref[s]
            y_ref[:, span] = y.astype(BF16)
        out = jnp.dot(y_ref[...], q_ref[...], preferred_element_type=F32)
        for i in range(pairs):
            group = step * pairs + i
            x = remainder(group, x_size)
            y = remainder(quotient(group, x_size), y_size)
            z = quotient(group, x_size * y_size)
            slot = ((y ^ my_y) * x_size + (x ^ my_x)) * z_size + (z ^ my_z)
            even = out[2 * i * share : (2 * i + 1) * share]
            odd = out[(2 * i + 1) * share : (2 * i + 2) * share]
            mine = my_core == 0
            keep_ref[slot] = jnp.where(mine, even, odd)
            send_ref[slot] = jnp.where(mine, odd, even).astype(BF16)

    def whole(*shape):
        return pl.BlockSpec(shape, lambda i: (0,) * len(shape))

    out_specs = [whole(groups, share, modes), whole(groups, share, modes)]
    out_shape = [
        jax.ShapeDtypeStruct((groups, share, modes), BF16),
        jax.ShapeDtypeStruct((groups, share, modes), F32),
    ]
    matrix_spec = whole(local_subs, boundary, boundary)
    if gathers:
        operands = (block_map, fetched, matrix)
        in_specs = [SMEM, whole(*fetched.shape), matrix_spec]
        out_specs += [whole(depth, modes), whole(modes, depth)]
        out_shape += [
            jax.ShapeDtypeStruct((depth, modes), BF16),
            jax.ShapeDtypeStruct((modes, depth), BF16),
        ]
    else:
        operands = (*laid_out, matrix, diagonal)
        in_specs = [
            whole(depth, modes),
            pl.BlockSpec((chunk, depth), lambda i: (i, 0)),
            matrix_spec,
            whole(local_subs, 1, boundary),
        ]
    return pl.pallas_call(
        kernel,
        grid=(modes // chunk,),
        in_specs=in_specs,
        out_specs=out_specs,
        out_shape=out_shape,
        scratch_shapes=[pltpu.VMEM((chunk, depth), BF16)],
        name="project_stiff" if gathers else "project_mass",
    )(*operands)


def reduce_shares(send, keep, dims):
    z_size, y_size, x_size = dims

    def partners(dz, dy, dx, core):
        pairs = []
        for z in range(z_size):
            for y in range(y_size):
                for x in range(x_size):
                    for k in range(2):
                        pairs.append(
                            (
                                ((z * y_size + y) * x_size + x) * 2 + k,
                                (((z ^ dz) * y_size + (y ^ dy)) * x_size + (x ^ dx)) * 2
                                + (k ^ core),
                            )
                        )
        return pairs

    plane = y_size * x_size
    summed = keep + lax.ppermute(send, AXES, partners(0, 0, 0, 1)).astype(F32)
    summed = summed.reshape((plane, z_size) + summed.shape[1:])
    total = summed[0]
    for d in range(1, plane):
        total = total + lax.ppermute(
            summed[d].astype(BF16), AXES, partners(0, d // x_size, d % x_size, 0)
        ).astype(F32)
    result = total[0]
    for d in range(1, z_size):
        result = result + lax.ppermute(
            total[d].astype(BF16), AXES, partners(d, 0, 0, 0)
        ).astype(F32)
    return result


def place(table, order, slots, arrived, stiff_tile, mass_tile, sizes):
    count = sizes.devices
    limit = sizes.row_blocks * sizes.col_blocks

    def kernel(
        table_ref,
        order_ref,
        slot_ref,
        in_ref,
        _stiff,
        _mass,
        stiff_ref,
        mass_ref,
        share_ref,
        sums_ref,
        sem,
    ):
        def copies(j):
            slot = slot_ref[j]
            row = pl.multiple_of(quotient(slot, sizes.col_blocks) * BLK, BLK)
            col = pl.multiple_of(remainder(slot, sizes.col_blocks) * BLK, BLK)
            return [
                pltpu.make_async_copy(
                    sums_ref.at[j, pl.ds(i * BLK, BLK)],
                    ref.at[pl.ds(row, BLK), pl.ds(col, BLK)],
                    sem.at[j, i],
                )
                for i, ref in enumerate((stiff_ref, mass_ref))
            ]

        def last(j):
            ahead = slot_ref[jnp.minimum(j + 1, count - 1)]
            ends = jnp.logical_or(j == count - 1, ahead != slot_ref[j])
            return jnp.logical_and(slot_ref[j] < limit, ends)

        def one(j, total):
            block = in_ref[order_ref[j], : 2 * BLK].astype(F32)
            same = jnp.logical_and(j > 0, slot_ref[jnp.maximum(j - 1, 0)] == slot_ref[j])
            total = jnp.where(same, total + block, block)
            sums_ref[j] = total.astype(BF16)

            @pl.when(last(j))
            def _():
                for copy in copies(j):
                    copy.start()

            return total

        lax.fori_loop(0, count, one, jnp.zeros((2 * BLK, BLK), F32))
        share_ref[...] = jnp.zeros_like(share_ref)

        def add(device, carry):
            share = table_ref[device, sizes.ratio + 1]

            @pl.when(share >= 0)
            def _():
                parts = in_ref[device, 2 * BLK : 2 * BLK + EXTRA].astype(F32)
                share_ref[share] += parts[0:1] + parts[1:2] + parts[2:3]

            return carry

        lax.fori_loop(0, count, add, 0)

        def wait(j, carry):
            @pl.when(last(j))
            def _():
                for copy in copies(j):
                    copy.wait()

            return carry

        lax.fori_loop(0, count, wait, 0)

    return pl.pallas_call(
        kernel,
        in_specs=[SMEM, SMEM, SMEM, VMEM, ANY, ANY],
        out_specs=[ANY, ANY, VMEM],
        out_shape=[
            jax.ShapeDtypeStruct(stiff_tile.shape, BF16),
            jax.ShapeDtypeStruct(mass_tile.shape, BF16),
            jax.ShapeDtypeStruct((sizes.share_blocks, 1, BLK), F32),
        ],
        input_output_aliases={4: 0, 5: 1},
        scratch_shapes=[
            pltpu.VMEM((count, 2 * BLK, BLK), BF16),
            pltpu.SemaphoreType.DMA((count, 2)),
        ],
        name="place",
    )(table, order, slots, arrived, stiff_tile, mass_tile)


def body(inv_interior, coupling, boundary_stiff, mass_interior, mass_boundary, block_map, modes):
    row_count = lax.axis_size("row")
    col_count = lax.axis_size("col")
    tile_cols, width = modes.shape
    tile_rows = tile_cols * col_count // row_count
    sizes = Sizes(
        devices=row_count * col_count,
        cols=col_count,
        ratio=row_count // col_count,
        row_blocks=tile_rows // BLK,
        col_blocks=tile_cols // BLK,
        share_blocks=tile_rows // BLK // col_count,
    )
    x_size = col_count // 2
    y_size = x_size
    dims = (row_count // y_size, y_size, x_size)

    table = exchange(describe(block_map, sizes))
    wanted = pick_modes(table, modes.reshape(sizes.col_blocks, BLK, width), sizes.ratio)
    fetched = exchange(wanted)

    outgoing, stiff, mass, diagonal, stiff_tile, mass_tile = condense(
        block_map, inv_interior, coupling, boundary_stiff, mass_interior, mass_boundary, sizes
    )
    outgoing, fetched = lax.optimization_barrier((outgoing, fetched))
    arrived = exchange(outgoing)

    fetched = fetched.reshape(row_count, col_count, sizes.ratio, BLK, width)
    send, keep, q, qt = project(block_map, fetched, None, stiff, None, dims, sizes.row_blocks)
    reduced_stiff = reduce_shares(send, keep, dims)
    send, keep = project(None, None, (q, qt), mass, diagonal, dims, sizes.row_blocks)
    reduced_mass = reduce_shares(send, keep, dims)

    slot = table[:, sizes.ratio]
    ids = jnp.arange(sizes.devices, dtype=jnp.int32)
    before = jnp.logical_or(
        slot[None, :] < slot[:, None],
        jnp.logical_and(slot[None, :] == slot[:, None], ids[None, :] < ids[:, None]),
    )
    rank = jnp.sum(before.astype(jnp.int32), axis=1)
    chosen = rank[None, :] == ids[:, None]
    order = jnp.sum(jnp.where(chosen, ids[None, :], 0), axis=1)
    slots = jnp.sum(jnp.where(chosen, slot[None, :], 0), axis=1)
    stiff_tile, mass_tile, mass_share = place(
        table, order, slots, arrived, stiff_tile, mass_tile, sizes
    )
    return stiff_tile, mass_tile, reduced_stiff, reduced_mass, mass_share.reshape(-1)


def solution(mesh):
    return jax.shard_map(
        body,
        mesh=mesh,
        in_specs=(
            P(AXES, None, None),
            P(AXES, None, None),
            P(AXES, None, None),
            P(AXES, None),
            P(AXES, None),
            P(AXES, None),
            P("col", "row"),
        ),
        out_specs=(P("row", "col"), P("row", "col"), P(AXES, None), P(AXES, None), P(AXES)),
        check_vma=False,
    )
```

```python
from typing import NamedTuple

import jax
import jax.numpy as jnp
from jax import lax
from jax.experimental import pallas as pl
from jax.experimental.pallas import tpu as pltpu
from jax.sharding import PartitionSpec as P


BLK = 128
EXTRA = 16
AXES = ("row", "col")
F32 = jnp.float32
BF16 = jnp.bfloat16
VMEM = pl.BlockSpec(memory_space=pltpu.VMEM)
SMEM = pl.BlockSpec(memory_space=pltpu.SMEM)
ANY = pl.BlockSpec(memory_space=pl.ANY)


class Sizes(NamedTuple):
    devices: int
    cols: int
    ratio: int
    row_blocks: int
    col_blocks: int
    share_blocks: int
    plane: int


def exchange(value):
    return lax.all_to_all(value, AXES, split_axis=0, concat_axis=0, tiled=True)


def quotient(value, size):
    return lax.shift_right_logical(value, jnp.int32(size.bit_length() - 1))


def remainder(value, size):
    return value & jnp.int32(size - 1)


def describe(block_map, sizes):
    local_subs, per_sub = block_map.shape

    def kernel(map_ref, out_ref):
        shape = out_ref.shape
        device = lax.broadcasted_iota(jnp.int32, shape, 0)
        field = lax.broadcasted_iota(jnp.int32, shape, 1)
        row = quotient(device, sizes.cols)
        col = remainder(device, sizes.cols)
        zero = jnp.zeros(shape, jnp.int32)
        wanted, share = zero, zero - 1
        slot = zero + sizes.row_blocks * sizes.col_blocks
        for s in range(local_subs):
            row_slot, col_slot = zero - 1, zero - 1
            for a in range(per_sub):
                block = map_ref[s, a]
                tile_row = quotient(block, sizes.row_blocks)
                wanted = jnp.where(
                    col * sizes.ratio + field == tile_row, remainder(block, sizes.col_blocks), wanted
                )
                share = jnp.where(
                    device == quotient(block, sizes.share_blocks),
                    remainder(block, sizes.share_blocks),
                    share,
                )
                row_slot = jnp.where(row == tile_row, remainder(block, sizes.row_blocks), row_slot)
                col_slot = jnp.where(
                    col == quotient(block, sizes.col_blocks),
                    remainder(block, sizes.col_blocks),
                    col_slot,
                )
            both = jnp.logical_and(row_slot >= 0, col_slot >= 0)
            slot = jnp.where(both, row_slot * sizes.col_blocks + col_slot, slot)
        out_ref[...] = jnp.where(
            field < sizes.ratio, wanted, jnp.where(field == sizes.ratio, slot, share)
        )

    return pl.pallas_call(
        kernel,
        out_shape=jax.ShapeDtypeStruct((sizes.devices, BLK), jnp.int32),
        in_specs=[SMEM],
        out_specs=VMEM,
        name="describe",
    )(block_map)


def pick_modes(table, modes, ratio):
    device_count = table.shape[0]
    width = modes.shape[2]

    def kernel(table_ref, modes_ref, out_ref):
        def one(device, carry):
            for h in range(ratio):
                out_ref[device, h] = modes_ref[table_ref[device, h]]
            return carry

        lax.fori_loop(0, device_count, one, 0, unroll=4)

    return pl.pallas_call(
        kernel,
        out_shape=jax.ShapeDtypeStruct((device_count, ratio, BLK, width), BF16),
        in_specs=[SMEM, VMEM],
        out_specs=VMEM,
        name="pick_modes",
    )(table, modes)


def condense(
    block_map, inv_interior, coupling, boundary_stiff, mass_interior, mass_boundary, sizes
):
    local_subs, interior, boundary = coupling.shape
    per_sub = boundary // BLK

    def kernel(
        map_ref,
        inv_ref,
        cpl_ref,
        stiff_ref,
        mi_ref,
        mb_ref,
        out_ref,
        k_ref,
        m_ref,
        d_ref,
    ):
        sub = pl.program_id(0)
        me = lax.axis_index("row") * sizes.cols + lax.axis_index("col")
        couple = cpl_ref[0]
        static_modes = (-jnp.dot(inv_ref[0], couple, preferred_element_type=F32)).astype(BF16)
        contract = (((0,), (0,)), ((), ()))
        stiff = stiff_ref[0].astype(F32) + lax.dot_general(
            couple, static_modes, contract, preferred_element_type=F32
        )
        weighted = (static_modes.astype(F32) * mi_ref[0]).astype(BF16)
        mass = lax.dot_general(static_modes, weighted, contract, preferred_element_type=F32)
        eye = lax.broadcasted_iota(jnp.int32, (BLK, BLK), 0) == lax.broadcasted_iota(
            jnp.int32, (BLK, BLK), 1
        )
        level = lax.broadcasted_iota(jnp.int32, (EXTRA, BLK), 0)
        for a in range(per_sub):
            block_a = map_ref[sub, a]
            rows = slice(a * BLK, (a + 1) * BLK)
            for b in range(per_sub):
                cols = slice(b * BLK, (b + 1) * BLK)
                owner = quotient(block_a, sizes.row_blocks) * sizes.cols + quotient(
                    map_ref[sub, b], sizes.col_blocks
                )
                owner = owner ^ me
                near, far = remainder(owner, sizes.plane), quotient(owner, sizes.plane)
                stiff_block = stiff[rows, cols].astype(BF16)
                mass_block = mass[rows, cols]
                if a == b:
                    diagonal = (
                        jnp.sum(jnp.where(eye, mass_block, 0.0), axis=0, keepdims=True)
                        + mb_ref[0, :, cols]
                    )
                    d_ref[0, :, cols] = diagonal
                    high = diagonal.astype(BF16).astype(F32)
                    middle = (diagonal - high).astype(BF16).astype(F32)
                    low = diagonal - high - middle
                    parts = jnp.where(level == 0, high, jnp.where(level == 1, middle, low))
                    share = quotient(block_a, sizes.share_blocks) ^ me
                    out_ref[
                        remainder(share, sizes.plane),
                        quotient(share, sizes.plane),
                        2 * BLK : 2 * BLK + EXTRA,
                    ] = parts.astype(BF16)
                    mass_block = jnp.where(eye, 0.0, mass_block)
                mass_block = mass_block.astype(BF16)
                out_ref[near, far, :BLK] = stiff_block
                out_ref[near, far, BLK : 2 * BLK] = mass_block
                k_ref[0, rows, cols] = stiff_block
                m_ref[0, rows, cols] = mass_block

    def piece(*shape):
        return pl.BlockSpec((1,) + shape, lambda s: (s, 0, 0))

    out_blocks = (sizes.plane, sizes.devices // sizes.plane, 2 * BLK + EXTRA, BLK)
    return pl.pallas_call(
        kernel,
        grid=(local_subs,),
        in_specs=[
            SMEM,
            piece(interior, interior),
            piece(interior, boundary),
            piece(boundary, boundary),
            piece(interior, 1),
            piece(1, boundary),
        ],
        out_specs=[
            pl.BlockSpec(out_blocks, lambda s: (0, 0, 0, 0)),
            piece(boundary, boundary),
            piece(boundary, boundary),
            piece(1, boundary),
        ],
        out_shape=[
            jax.ShapeDtypeStruct(out_blocks, BF16),
            jax.ShapeDtypeStruct((local_subs, boundary, boundary), BF16),
            jax.ShapeDtypeStruct((local_subs, boundary, boundary), BF16),
            jax.ShapeDtypeStruct((local_subs, 1, boundary), F32),
        ],
        name="condense",
    )(
        block_map,
        inv_interior,
        coupling,
        boundary_stiff,
        mass_interior[:, :, None],
        mass_boundary[:, None, :],
    )


def project(block_map, fetched, laid_out, matrix, diagonal, dims, row_blocks):
    z_size, y_size, x_size = dims
    local_subs, boundary, _ = matrix.shape
    depth = local_subs * boundary
    per_sub = boundary // BLK
    groups = z_size * y_size * x_size
    gathers = laid_out is None
    if gathers:
        row_count, _, ratio, _, width = fetched.shape
        modes = row_count * width
    else:
        modes = laid_out[0].shape[1]
    share = modes // (2 * groups)
    chunk = modes // 2
    pairs = chunk // (2 * share)

    def kernel(*refs):
        step = pl.program_id(0)
        if gathers:
            map_ref, in_ref, m_ref, send_ref, keep_ref, q_ref, t_ref, y_ref = refs

            @pl.when(step == 0)
            def _():
                for s in range(local_subs):
                    for a in range(per_sub):
                        tile_row = quotient(map_ref[s, a], row_blocks)
                        c = quotient(tile_row, ratio)
                        h = remainder(tile_row, ratio)
                        k = (s * per_sub + a) * BLK
                        for r in range(row_count):
                            block = in_ref[r, c, h]
                            q_ref[k : k + BLK, r * width : (r + 1) * width] = block
                            t_ref[r * width : (r + 1) * width, k : k + BLK] = block.T

            left_rows = pl.ds(pl.multiple_of(step * chunk, chunk), chunk)
        else:
            q_ref, t_ref, m_ref, d_ref, send_ref, keep_ref, y_ref = refs
            left_rows = slice(None)
        row, col = lax.axis_index("row"), lax.axis_index("col")
        my_z, my_y = quotient(row, y_size), remainder(row, y_size)
        my_x, my_core = quotient(col, 2), remainder(col, 2)
        for s in range(local_subs):
            span = slice(s * boundary, (s + 1) * boundary)
            left = t_ref[left_rows, span]
            y = jnp.dot(left, m_ref[s], preferred_element_type=F32)
            if diagonal is not None:
                y = y + left.astype(F32) * d_ref[s]
            y_ref[:, span] = y.astype(BF16)
        out = jnp.dot(y_ref[...], q_ref[...], preferred_element_type=F32)
        for i in range(pairs):
            group = step * pairs + i
            x = remainder(group, x_size)
            y = remainder(quotient(group, x_size), y_size)
            z = quotient(group, x_size * y_size)
            slot = ((y ^ my_y) * x_size + (x ^ my_x)) * z_size + (z ^ my_z)
            even = out[2 * i * share : (2 * i + 1) * share]
            odd = out[(2 * i + 1) * share : (2 * i + 2) * share]
            mine = my_core == 0
            keep_ref[slot] = jnp.where(mine, even, odd)
            send_ref[slot] = jnp.where(mine, odd, even).astype(BF16)

    def whole(*shape):
        return pl.BlockSpec(shape, lambda i: (0,) * len(shape))

    out_specs = [whole(groups, share, modes), whole(groups, share, modes)]
    out_shape = [
        jax.ShapeDtypeStruct((groups, share, modes), BF16),
        jax.ShapeDtypeStruct((groups, share, modes), F32),
    ]
    matrix_spec = whole(local_subs, boundary, boundary)
    if gathers:
        operands = (block_map, fetched, matrix)
        in_specs = [SMEM, whole(*fetched.shape), matrix_spec]
        out_specs += [whole(depth, modes), whole(modes, depth)]
        out_shape += [
            jax.ShapeDtypeStruct((depth, modes), BF16),
            jax.ShapeDtypeStruct((modes, depth), BF16),
        ]
    else:
        operands = (*laid_out, matrix, diagonal)
        in_specs = [
            whole(depth, modes),
            pl.BlockSpec((chunk, depth), lambda i: (i, 0)),
            matrix_spec,
            whole(local_subs, 1, boundary),
        ]
    return pl.pallas_call(
        kernel,
        grid=(modes // chunk,),
        in_specs=in_specs,
        out_specs=out_specs,
        out_shape=out_shape,
        scratch_shapes=[pltpu.VMEM((chunk, depth), BF16)],
        name="project_stiff" if gathers else "project_mass",
    )(*operands)


def swap(value, offset, device_count):
    return lax.ppermute(value, AXES, [(i, i ^ offset) for i in range(device_count)])


def reduce_shares(send, keep, sizes):
    got = swap(send, 1, sizes.devices)
    summed = keep + got.astype(F32)
    depth = sizes.devices // sizes.plane
    summed = summed.reshape((sizes.plane // 2, depth) + summed.shape[1:])
    total = summed[0]
    for d in range(1, sizes.plane // 2):
        got = swap(summed[d].astype(BF16), 2 * d, sizes.devices)
        total = total + got.astype(F32)
    result = total[0]
    for d in range(1, depth):
        got = swap(total[d].astype(BF16), d * sizes.plane, sizes.devices)
        result = result + got.astype(F32)
    return result


def spread_in_plane(blocks, sizes):
    near = [blocks[0]] + [
        swap(blocks[d], d, sizes.devices) for d in range(1, sizes.plane)
    ]
    return [jnp.stack([part[z] for part in near]) for z in range(sizes.devices // sizes.plane)]


def clear_tiles(table, sizes):
    shape = (sizes.row_blocks * BLK, sizes.col_blocks * BLK)

    def kernel(_table, stiff_ref, mass_ref, zero_ref, sem):
        zero_ref[...] = jnp.zeros_like(zero_ref)
        fills = [
            pltpu.make_async_copy(zero_ref, ref.at[pl.ds(i * BLK, BLK), :], sem.at[i, j])
            for i in range(sizes.row_blocks)
            for j, ref in enumerate((stiff_ref, mass_ref))
        ]
        for fill in fills:
            fill.start()
        for fill in fills:
            fill.wait()

    return pl.pallas_call(
        kernel,
        in_specs=[ANY],
        out_specs=[ANY, ANY],
        out_shape=[jax.ShapeDtypeStruct(shape, BF16), jax.ShapeDtypeStruct(shape, BF16)],
        scratch_shapes=[
            pltpu.VMEM((BLK, shape[1]), BF16),
            pltpu.SemaphoreType.DMA((sizes.row_blocks, 2)),
        ],
        name="clear_tiles",
    )(table)


def place(table, order, slots, arrived, stiff_tile, mass_tile, sizes):
    count = sizes.devices
    limit = sizes.row_blocks * sizes.col_blocks
    depth = len(arrived)
    height = 2 * BLK + EXTRA

    def kernel(*refs):
        table_ref, order_ref, slot_ref = refs[:3]
        in_refs = refs[3 : 3 + depth]
        stiff_ref, mass_ref, share_ref, held_ref, sums_ref, in_sem, sem = refs[-7:]
        me = lax.axis_index("row") * sizes.cols + lax.axis_index("col")
        loads = [
            pltpu.make_async_copy(
                ref, held_ref.at[pl.ds(z * sizes.plane, sizes.plane)], in_sem.at[z]
            )
            for z, ref in enumerate(in_refs)
        ]
        for load in loads:
            load.start()
        for load in loads:
            load.wait()

        def copies(j):
            slot = slot_ref[j]
            row = pl.multiple_of(quotient(slot, sizes.col_blocks) * BLK, BLK)
            col = pl.multiple_of(remainder(slot, sizes.col_blocks) * BLK, BLK)
            return [
                pltpu.make_async_copy(
                    sums_ref.at[j, pl.ds(i * BLK, BLK)],
                    ref.at[pl.ds(row, BLK), pl.ds(col, BLK)],
                    sem.at[j, i],
                )
                for i, ref in enumerate((stiff_ref, mass_ref))
            ]

        def last(j):
            ahead = slot_ref[jnp.minimum(j + 1, count - 1)]
            ends = jnp.logical_or(j == count - 1, ahead != slot_ref[j])
            return jnp.logical_and(slot_ref[j] < limit, ends)

        def one(j, total):
            block = held_ref[order_ref[j] ^ me, : 2 * BLK].astype(F32)
            same = jnp.logical_and(j > 0, slot_ref[jnp.maximum(j - 1, 0)] == slot_ref[j])
            total = jnp.where(same, total + block, block)
            sums_ref[j] = total.astype(BF16)

            @pl.when(last(j))
            def _():
                for copy in copies(j):
                    copy.start()

            return total

        lax.fori_loop(0, count, one, jnp.zeros((2 * BLK, BLK), F32))
        share_ref[...] = jnp.zeros_like(share_ref)

        def add(device, carry):
            share = table_ref[device, sizes.ratio + 1]

            @pl.when(share >= 0)
            def _():
                parts = held_ref[device ^ me, 2 * BLK : 2 * BLK + EXTRA].astype(F32)
                share_ref[share] += parts[0:1] + parts[1:2] + parts[2:3]

            return carry

        lax.fori_loop(0, count, add, 0)

        def wait(j, carry):
            @pl.when(last(j))
            def _():
                for copy in copies(j):
                    copy.wait()

            return carry

        lax.fori_loop(0, count, wait, 0)

    return pl.pallas_call(
        kernel,
        in_specs=[SMEM, SMEM, SMEM] + [ANY] * (depth + 2),
        out_specs=[ANY, ANY, VMEM],
        out_shape=[
            jax.ShapeDtypeStruct(stiff_tile.shape, BF16),
            jax.ShapeDtypeStruct(mass_tile.shape, BF16),
            jax.ShapeDtypeStruct((sizes.share_blocks, 1, BLK), F32),
        ],
        input_output_aliases={3 + depth: 0, 4 + depth: 1},
        scratch_shapes=[
            pltpu.VMEM((count, height, BLK), BF16),
            pltpu.VMEM((count, 2 * BLK, BLK), BF16),
            pltpu.SemaphoreType.DMA((depth,)),
            pltpu.SemaphoreType.DMA((count, 2)),
        ],
        name="place",
    )(table, order, slots, *arrived, stiff_tile, mass_tile)


def reduction(inv_interior, coupling, boundary_stiff, mass_interior, mass_boundary, block_map, modes):
    row_count = lax.axis_size("row")
    col_count = lax.axis_size("col")
    tile_cols, width = modes.shape
    tile_rows = tile_cols * col_count // row_count
    sizes = Sizes(
        devices=row_count * col_count,
        cols=col_count,
        ratio=row_count // col_count,
        row_blocks=tile_rows // BLK,
        col_blocks=tile_cols // BLK,
        share_blocks=tile_rows // BLK // col_count,
        plane=col_count // 2 * col_count,
    )
    x_size = col_count // 2
    y_size = x_size
    dims = (row_count // y_size, y_size, x_size)

    table = exchange(describe(block_map, sizes))
    blocks, stiff, mass, diagonal = condense(
        block_map, inv_interior, coupling, boundary_stiff, mass_interior, mass_boundary, sizes
    )
    table, blocks = lax.optimization_barrier((table, blocks))
    spread = spread_in_plane(blocks, sizes)
    beside = swap(spread[1], sizes.plane, sizes.devices)
    wanted = pick_modes(table, modes.reshape(sizes.col_blocks, BLK, width), sizes.ratio)
    fetched = exchange(wanted)
    stiff_tile, mass_tile = clear_tiles(table, sizes)
    late, beside, fetched, stiff_tile, mass_tile = lax.optimization_barrier(
        (spread[2:], beside, fetched, stiff_tile, mass_tile)
    )
    late = [swap(part, (2 + d) * sizes.plane, sizes.devices) for d, part in enumerate(late)]
    arrived = [spread[0], beside, *late]

    fetched = fetched.reshape(row_count, col_count, sizes.ratio, BLK, width)
    send, keep, q, qt = project(block_map, fetched, None, stiff, None, dims, sizes.row_blocks)
    reduced_stiff = reduce_shares(send, keep, sizes)
    send, keep = project(None, None, (q, qt), mass, diagonal, dims, sizes.row_blocks)
    reduced_mass = reduce_shares(send, keep, sizes)

    slot = table[:, sizes.ratio]
    ids = jnp.arange(sizes.devices, dtype=jnp.int32)
    before = jnp.logical_or(
        slot[None, :] < slot[:, None],
        jnp.logical_and(slot[None, :] == slot[:, None], ids[None, :] < ids[:, None]),
    )
    rank = jnp.sum(before.astype(jnp.int32), axis=1)
    chosen = rank[None, :] == ids[:, None]
    order = jnp.sum(jnp.where(chosen, ids[None, :], 0), axis=1)
    slots = jnp.sum(jnp.where(chosen, slot[None, :], 0), axis=1)
    stiff_tile, mass_tile, mass_share = place(
        table, order, slots, arrived, stiff_tile, mass_tile, sizes
    )
    return stiff_tile, mass_tile, reduced_stiff, reduced_mass, mass_share.reshape(-1)


def solution(mesh):
    return jax.shard_map(
        reduction,
        mesh=mesh,
        in_specs=(
            P(AXES, None, None),
            P(AXES, None, None),
            P(AXES, None, None),
            P(AXES, None),
            P(AXES, None),
            P(AXES, None),
            P("col", "row"),
        ),
        out_specs=(P("row", "col"), P("row", "col"), P(AXES, None), P(AXES, None), P(AXES)),
        check_vma=False,
    )
```

```python
from typing import NamedTuple

import jax
import jax.numpy as jnp
from jax import lax
from jax.experimental import pallas as pl
from jax.experimental.pallas import tpu as pltpu
from jax.sharding import PartitionSpec as P


BLK = 128
EXTRA = 16
AXES = ("row", "col")
F32 = jnp.float32
BF16 = jnp.bfloat16
VMEM = pl.BlockSpec(memory_space=pltpu.VMEM)
SMEM = pl.BlockSpec(memory_space=pltpu.SMEM)
ANY = pl.BlockSpec(memory_space=pl.ANY)


class Sizes(NamedTuple):
    devices: int
    cols: int
    ratio: int
    row_blocks: int
    col_blocks: int
    share_blocks: int
    plane: int


def exchange(value):
    return lax.all_to_all(value, AXES, split_axis=0, concat_axis=0, tiled=True)


def quotient(value, size):
    return lax.shift_right_logical(value, jnp.int32(size.bit_length() - 1))


def remainder(value, size):
    return value & jnp.int32(size - 1)


def describe(block_map, sizes):
    local_subs, per_sub = block_map.shape

    def kernel(map_ref, out_ref):
        shape = out_ref.shape
        device = lax.broadcasted_iota(jnp.int32, shape, 0)
        field = lax.broadcasted_iota(jnp.int32, shape, 1)
        row = quotient(device, sizes.cols)
        col = remainder(device, sizes.cols)
        zero = jnp.zeros(shape, jnp.int32)
        wanted, share = zero, zero - 1
        slot = zero + sizes.row_blocks * sizes.col_blocks
        for s in range(local_subs):
            row_slot, col_slot = zero - 1, zero - 1
            for a in range(per_sub):
                block = map_ref[s, a]
                tile_row = quotient(block, sizes.row_blocks)
                wanted = jnp.where(
                    col * sizes.ratio + field == tile_row, remainder(block, sizes.col_blocks), wanted
                )
                share = jnp.where(
                    device == quotient(block, sizes.share_blocks),
                    remainder(block, sizes.share_blocks),
                    share,
                )
                row_slot = jnp.where(row == tile_row, remainder(block, sizes.row_blocks), row_slot)
                col_slot = jnp.where(
                    col == quotient(block, sizes.col_blocks),
                    remainder(block, sizes.col_blocks),
                    col_slot,
                )
            both = jnp.logical_and(row_slot >= 0, col_slot >= 0)
            slot = jnp.where(both, row_slot * sizes.col_blocks + col_slot, slot)
        out_ref[...] = jnp.where(
            field < sizes.ratio, wanted, jnp.where(field == sizes.ratio, slot, share)
        )

    return pl.pallas_call(
        kernel,
        out_shape=jax.ShapeDtypeStruct((sizes.devices, BLK), jnp.int32),
        in_specs=[SMEM],
        out_specs=VMEM,
        name="describe",
    )(block_map)


def pick_modes(table, modes, ratio):
    device_count = table.shape[0]
    width = modes.shape[1]

    def kernel(table_ref, modes_ref, out_ref):
        def one(device, carry):
            for h in range(ratio):
                out_ref[device, h] = modes_ref[table_ref[device, h]]
            return carry

        lax.fori_loop(0, device_count, one, 0, unroll=4)

    return pl.pallas_call(
        kernel,
        out_shape=jax.ShapeDtypeStruct((device_count, ratio, width, BLK), BF16),
        in_specs=[SMEM, VMEM],
        out_specs=VMEM,
        name="pick_modes",
    )(table, modes)


def condense(
    block_map, inv_interior, coupling, boundary_stiff, mass_interior, mass_boundary, sizes
):
    local_subs, interior, boundary = coupling.shape
    per_sub = boundary // BLK

    def kernel(
        map_ref,
        inv_ref,
        cpl_ref,
        stiff_ref,
        mi_ref,
        mb_ref,
        out_ref,
        k_ref,
        m_ref,
        d_ref,
    ):
        sub = pl.program_id(0)
        me = lax.axis_index("row") * sizes.cols + lax.axis_index("col")
        couple = cpl_ref[0]
        static_modes = (-jnp.dot(inv_ref[0], couple, preferred_element_type=F32)).astype(BF16)
        contract = (((0,), (0,)), ((), ()))
        stiff = stiff_ref[0].astype(F32) + lax.dot_general(
            couple, static_modes, contract, preferred_element_type=F32
        )
        weighted = (static_modes.astype(F32) * mi_ref[0]).astype(BF16)
        mass = lax.dot_general(static_modes, weighted, contract, preferred_element_type=F32)
        eye = lax.broadcasted_iota(jnp.int32, (BLK, BLK), 0) == lax.broadcasted_iota(
            jnp.int32, (BLK, BLK), 1
        )
        level = lax.broadcasted_iota(jnp.int32, (EXTRA, BLK), 0)
        for a in range(per_sub):
            block_a = map_ref[sub, a]
            rows = slice(a * BLK, (a + 1) * BLK)
            for b in range(per_sub):
                cols = slice(b * BLK, (b + 1) * BLK)
                owner = quotient(block_a, sizes.row_blocks) * sizes.cols + quotient(
                    map_ref[sub, b], sizes.col_blocks
                )
                owner = owner ^ me
                near, far = remainder(owner, sizes.plane), quotient(owner, sizes.plane)
                stiff_block = stiff[rows, cols].astype(BF16)
                mass_block = mass[rows, cols]
                if a == b:
                    diagonal = (
                        jnp.sum(jnp.where(eye, mass_block, 0.0), axis=0, keepdims=True)
                        + mb_ref[0, :, cols]
                    )
                    d_ref[0, :, cols] = diagonal
                    high = diagonal.astype(BF16).astype(F32)
                    middle = (diagonal - high).astype(BF16).astype(F32)
                    low = diagonal - high - middle
                    parts = jnp.where(level == 0, high, jnp.where(level == 1, middle, low))
                    share = quotient(block_a, sizes.share_blocks) ^ me
                    out_ref[
                        remainder(share, sizes.plane),
                        quotient(share, sizes.plane),
                        2 * BLK : 2 * BLK + EXTRA,
                    ] = parts.astype(BF16)
                    mass_block = jnp.where(eye, 0.0, mass_block)
                mass_block = mass_block.astype(BF16)
                out_ref[near, far, :BLK] = stiff_block
                out_ref[near, far, BLK : 2 * BLK] = mass_block
                k_ref[0, rows, cols] = stiff_block
                m_ref[0, rows, cols] = mass_block

    def piece(*shape):
        return pl.BlockSpec((1,) + shape, lambda s: (s, 0, 0))

    out_blocks = (sizes.plane, sizes.devices // sizes.plane, 2 * BLK + EXTRA, BLK)
    return pl.pallas_call(
        kernel,
        grid=(local_subs,),
        in_specs=[
            SMEM,
            piece(interior, interior),
            piece(interior, boundary),
            piece(boundary, boundary),
            piece(interior, 1),
            piece(1, boundary),
        ],
        out_specs=[
            pl.BlockSpec(out_blocks, lambda s: (0, 0, 0, 0)),
            piece(boundary, boundary),
            piece(boundary, boundary),
            piece(1, boundary),
        ],
        out_shape=[
            jax.ShapeDtypeStruct(out_blocks, BF16),
            jax.ShapeDtypeStruct((local_subs, boundary, boundary), BF16),
            jax.ShapeDtypeStruct((local_subs, boundary, boundary), BF16),
            jax.ShapeDtypeStruct((local_subs, 1, boundary), F32),
        ],
        name="condense",
    )(
        block_map,
        inv_interior,
        coupling,
        boundary_stiff,
        mass_interior[:, :, None],
        mass_boundary[:, None, :],
    )


def cut_shares(out, step, send_ref, keep_ref, dims):
    _, y_size, x_size = dims
    z_size = dims[0]
    share = send_ref.shape[1]
    pairs = out.shape[0] // (2 * share)
    row, col = lax.axis_index("row"), lax.axis_index("col")
    my_z, my_y = quotient(row, y_size), remainder(row, y_size)
    my_x, mine = quotient(col, 2), remainder(col, 2) == 0
    for i in range(pairs):
        group = step * pairs + i
        x = remainder(group, x_size)
        y = remainder(quotient(group, x_size), y_size)
        z = quotient(group, x_size * y_size)
        slot = ((y ^ my_y) * x_size + (x ^ my_x)) * z_size + (z ^ my_z)
        even = out[2 * i * share : (2 * i + 1) * share]
        odd = out[(2 * i + 1) * share : (2 * i + 2) * share]
        keep_ref[slot] = jnp.where(mine, even, odd)
        send_ref[slot] = jnp.where(mine, odd, even).astype(BF16)


def whole(*shape):
    return pl.BlockSpec(shape, lambda i: (0,) * len(shape))


def project_stiff(block_map, fetched, matrix, dims, row_blocks):
    local_subs, boundary, _ = matrix.shape
    depth = local_subs * boundary
    per_sub = boundary // BLK
    groups = dims[0] * dims[1] * dims[2]
    row_count, _, ratio, width, _ = fetched.shape
    modes = row_count * width
    share = modes // (2 * groups)
    chunk = modes // 2

    def kernel(map_ref, in_ref, m_ref, send_ref, keep_ref, t_ref, y_ref):
        step = pl.program_id(0)

        @pl.when(step == 0)
        def _():
            for s in range(local_subs):
                for a in range(per_sub):
                    tile_row = quotient(map_ref[s, a], row_blocks)
                    c = quotient(tile_row, ratio)
                    h = remainder(tile_row, ratio)
                    k = (s * per_sub + a) * BLK
                    for r in range(row_count):
                        t_ref[r * width : (r + 1) * width, k : k + BLK] = in_ref[r, c, h]

        rows = pl.ds(pl.multiple_of(step * chunk, chunk), chunk)
        for s in range(local_subs):
            span = slice(s * boundary, (s + 1) * boundary)
            y_ref[:, span] = jnp.dot(
                t_ref[rows, span], m_ref[s], preferred_element_type=F32
            ).astype(BF16)
        out = lax.dot_general(
            y_ref[...], t_ref[...], (((1,), (1,)), ((), ())), preferred_element_type=F32
        )
        cut_shares(out, step, send_ref, keep_ref, dims)

    return pl.pallas_call(
        kernel,
        grid=(modes // chunk,),
        in_specs=[SMEM, whole(*fetched.shape), whole(local_subs, boundary, boundary)],
        out_specs=[
            whole(groups, share, modes),
            whole(groups, share, modes),
            whole(modes, depth),
        ],
        out_shape=[
            jax.ShapeDtypeStruct((groups, share, modes), BF16),
            jax.ShapeDtypeStruct((groups, share, modes), F32),
            jax.ShapeDtypeStruct((modes, depth), BF16),
        ],
        scratch_shapes=[pltpu.VMEM((chunk, depth), BF16)],
        name="project_stiff",
    )(block_map, fetched, matrix)


def mix_mass(qt, matrix, diagonal):
    modes, depth = qt.shape
    local_subs, boundary, _ = matrix.shape
    chunk = modes // 4

    def kernel(t_ref, m_ref, d_ref, y_ref):
        for s in range(local_subs):
            span = slice(s * boundary, (s + 1) * boundary)
            left = t_ref[:, span]
            y = jnp.dot(left, m_ref[s], preferred_element_type=F32)
            y_ref[:, span] = (y + left.astype(F32) * d_ref[s]).astype(BF16)

    rows = pl.BlockSpec((chunk, depth), lambda i: (i, 0))
    return pl.pallas_call(
        kernel,
        grid=(modes // chunk,),
        in_specs=[rows, whole(local_subs, boundary, boundary), whole(local_subs, 1, boundary)],
        out_specs=rows,
        out_shape=jax.ShapeDtypeStruct((modes, depth), BF16),
        name="mix_mass",
    )(qt, matrix, diagonal)


def project_mass(mixed, qt, dims):
    modes, depth = qt.shape
    groups = dims[0] * dims[1] * dims[2]
    share = modes // (2 * groups)
    chunk = modes // 2

    def kernel(y_ref, t_ref, send_ref, keep_ref):
        out = lax.dot_general(
            y_ref[...], t_ref[...], (((1,), (1,)), ((), ())), preferred_element_type=F32
        )
        cut_shares(out, pl.program_id(0), send_ref, keep_ref, dims)

    return pl.pallas_call(
        kernel,
        grid=(modes // chunk,),
        in_specs=[pl.BlockSpec((chunk, depth), lambda i: (i, 0)), whole(modes, depth)],
        out_specs=[whole(groups, share, modes), whole(groups, share, modes)],
        out_shape=[
            jax.ShapeDtypeStruct((groups, share, modes), BF16),
            jax.ShapeDtypeStruct((groups, share, modes), F32),
        ],
        name="project_mass",
    )(mixed, qt)


def swap(value, offset, device_count):
    return lax.ppermute(value, AXES, [(i, i ^ offset) for i in range(device_count)])


def reduce_shares(send, keep, sizes):
    got = swap(send, 1, sizes.devices)
    summed = keep + got.astype(F32)
    depth = sizes.devices // sizes.plane
    summed = summed.reshape((sizes.plane // 2, depth) + summed.shape[1:])
    total = summed[0]
    for d in range(1, sizes.plane // 2):
        got = swap(summed[d].astype(BF16), 2 * d, sizes.devices)
        total = total + got.astype(F32)
    result = total[0]
    for d in range(1, depth):
        got = swap(total[d].astype(BF16), d * sizes.plane, sizes.devices)
        result = result + got.astype(F32)
    return result


def spread_in_plane(blocks, sizes):
    near = [blocks[0]]
    for d in range(1, sizes.plane):
        near.append(swap(blocks[d], d, sizes.devices))
    return [jnp.stack([part[z] for part in near]) for z in range(sizes.devices // sizes.plane)]


def clear_tiles(table, sizes):
    shape = (sizes.row_blocks * BLK, sizes.col_blocks * BLK)

    def kernel(_table, stiff_ref, mass_ref, zero_ref, sem):
        zero_ref[...] = jnp.zeros_like(zero_ref)
        fills = [
            pltpu.make_async_copy(zero_ref, ref.at[pl.ds(i * BLK, BLK), :], sem.at[i, j])
            for i in range(sizes.row_blocks)
            for j, ref in enumerate((stiff_ref, mass_ref))
        ]
        for fill in fills:
            fill.start()
        for fill in fills:
            fill.wait()

    return pl.pallas_call(
        kernel,
        in_specs=[ANY],
        out_specs=[ANY, ANY],
        out_shape=[jax.ShapeDtypeStruct(shape, BF16), jax.ShapeDtypeStruct(shape, BF16)],
        scratch_shapes=[
            pltpu.VMEM((BLK, shape[1]), BF16),
            pltpu.SemaphoreType.DMA((sizes.row_blocks, 2)),
        ],
        name="clear_tiles",
    )(table)


def place(table, order, slots, arrived, stiff_tile, mass_tile, sizes):
    count = sizes.devices
    limit = sizes.row_blocks * sizes.col_blocks
    depth = len(arrived)
    height = 2 * BLK + EXTRA

    def kernel(*refs):
        table_ref, order_ref, slot_ref = refs[:3]
        in_refs = refs[3 : 3 + depth]
        stiff_ref, mass_ref, share_ref, held_ref, sums_ref, in_sem, sem = refs[-7:]
        me = lax.axis_index("row") * sizes.cols + lax.axis_index("col")
        loads = [
            pltpu.make_async_copy(
                ref, held_ref.at[pl.ds(z * sizes.plane, sizes.plane)], in_sem.at[z]
            )
            for z, ref in enumerate(in_refs)
        ]
        for load in loads:
            load.start()
        for load in loads:
            load.wait()

        def copies(j):
            slot = slot_ref[j]
            row = pl.multiple_of(quotient(slot, sizes.col_blocks) * BLK, BLK)
            col = pl.multiple_of(remainder(slot, sizes.col_blocks) * BLK, BLK)
            return [
                pltpu.make_async_copy(
                    sums_ref.at[j, pl.ds(i * BLK, BLK)],
                    ref.at[pl.ds(row, BLK), pl.ds(col, BLK)],
                    sem.at[j, i],
                )
                for i, ref in enumerate((stiff_ref, mass_ref))
            ]

        def last(j):
            ahead = slot_ref[jnp.minimum(j + 1, count - 1)]
            ends = jnp.logical_or(j == count - 1, ahead != slot_ref[j])
            return jnp.logical_and(slot_ref[j] < limit, ends)

        def one(j, total):
            block = held_ref[order_ref[j] ^ me, : 2 * BLK].astype(F32)
            same = jnp.logical_and(j > 0, slot_ref[jnp.maximum(j - 1, 0)] == slot_ref[j])
            total = jnp.where(same, total + block, block)
            sums_ref[j] = total.astype(BF16)

            @pl.when(last(j))
            def _():
                for copy in copies(j):
                    copy.start()

            return total

        lax.fori_loop(0, count, one, jnp.zeros((2 * BLK, BLK), F32))
        share_ref[...] = jnp.zeros_like(share_ref)

        def add(device, carry):
            share = table_ref[device, sizes.ratio + 1]

            @pl.when(share >= 0)
            def _():
                parts = held_ref[device ^ me, 2 * BLK : 2 * BLK + EXTRA].astype(F32)
                share_ref[share] += parts[0:1] + parts[1:2] + parts[2:3]

            return carry

        lax.fori_loop(0, count, add, 0)

        def wait(j, carry):
            @pl.when(last(j))
            def _():
                for copy in copies(j):
                    copy.wait()

            return carry

        lax.fori_loop(0, count, wait, 0)

    return pl.pallas_call(
        kernel,
        in_specs=[SMEM, SMEM, SMEM] + [ANY] * (depth + 2),
        out_specs=[ANY, ANY, VMEM],
        out_shape=[
            jax.ShapeDtypeStruct(stiff_tile.shape, BF16),
            jax.ShapeDtypeStruct(mass_tile.shape, BF16),
            jax.ShapeDtypeStruct((sizes.share_blocks, 1, BLK), F32),
        ],
        input_output_aliases={3 + depth: 0, 4 + depth: 1},
        scratch_shapes=[
            pltpu.VMEM((count, height, BLK), BF16),
            pltpu.VMEM((count, 2 * BLK, BLK), BF16),
            pltpu.SemaphoreType.DMA((depth,)),
            pltpu.SemaphoreType.DMA((count, 2)),
        ],
        name="place",
    )(table, order, slots, *arrived, stiff_tile, mass_tile)


def reduction(inv_interior, coupling, boundary_stiff, mass_interior, mass_boundary, block_map, modes):
    row_count = lax.axis_size("row")
    col_count = lax.axis_size("col")
    tile_cols, width = modes.shape
    tile_rows = tile_cols * col_count // row_count
    sizes = Sizes(
        devices=row_count * col_count,
        cols=col_count,
        ratio=row_count // col_count,
        row_blocks=tile_rows // BLK,
        col_blocks=tile_cols // BLK,
        share_blocks=tile_rows // BLK // col_count,
        plane=col_count // 2 * col_count,
    )
    x_size = col_count // 2
    y_size = x_size
    dims = (row_count // y_size, y_size, x_size)

    table = exchange(describe(block_map, sizes))
    turned = jnp.swapaxes(modes.reshape(sizes.col_blocks, BLK, width), 1, 2)
    wanted = pick_modes(table, turned, sizes.ratio)
    fetched = exchange(wanted)
    blocks, stiff, mass, diagonal = condense(
        block_map, inv_interior, coupling, boundary_stiff, mass_interior, mass_boundary, sizes
    )
    spread = spread_in_plane(blocks, sizes)
    beside = swap(spread[1], sizes.plane, sizes.devices)
    stiff_tile, mass_tile = clear_tiles(table, sizes)
    late, fetched, stiff_tile, mass_tile = lax.optimization_barrier(
        (spread[2:], fetched, stiff_tile, mass_tile)
    )
    late = [swap(part, (2 + d) * sizes.plane, sizes.devices) for d, part in enumerate(late)]
    arrived = [spread[0], beside, *late]

    fetched = fetched.reshape(row_count, col_count, sizes.ratio, width, BLK)
    send, keep, qt = project_stiff(block_map, fetched, stiff, dims, sizes.row_blocks)
    reduced_stiff = reduce_shares(send, keep, sizes)
    mixed = mix_mass(qt, mass, diagonal)
    send, keep = project_mass(mixed, qt, dims)
    reduced_mass = reduce_shares(send, keep, sizes)

    slot = table[:, sizes.ratio]
    ids = jnp.arange(sizes.devices, dtype=jnp.int32)
    before = jnp.logical_or(
        slot[None, :] < slot[:, None],
        jnp.logical_and(slot[None, :] == slot[:, None], ids[None, :] < ids[:, None]),
    )
    rank = jnp.sum(before.astype(jnp.int32), axis=1)
    chosen = rank[None, :] == ids[:, None]
    order = jnp.sum(jnp.where(chosen, ids[None, :], 0), axis=1)
    slots = jnp.sum(jnp.where(chosen, slot[None, :], 0), axis=1)
    stiff_tile, mass_tile, mass_share = place(
        table, order, slots, arrived, stiff_tile, mass_tile, sizes
    )
    return stiff_tile, mass_tile, reduced_stiff, reduced_mass, mass_share.reshape(-1)


def solution(mesh):
    return jax.shard_map(
        reduction,
        mesh=mesh,
        in_specs=(
            P(AXES, None, None),
            P(AXES, None, None),
            P(AXES, None, None),
            P(AXES, None),
            P(AXES, None),
            P(AXES, None),
            P("col", "row"),
        ),
        out_specs=(P("row", "col"), P("row", "col"), P(AXES, None), P(AXES, None), P(AXES)),
        check_vma=False,
    )
```

```python
from typing import NamedTuple

import jax
import jax.numpy as jnp
from jax import lax
from jax.experimental import pallas as pl
from jax.experimental.pallas import tpu as pltpu
from jax.sharding import PartitionSpec as P


BLK = 128
EXTRA = 8
AXES = ("row", "col")
F32 = jnp.float32
BF16 = jnp.bfloat16
VMEM = pl.BlockSpec(memory_space=pltpu.VMEM)
SMEM = pl.BlockSpec(memory_space=pltpu.SMEM)
ANY = pl.BlockSpec(memory_space=pl.ANY)


class Sizes(NamedTuple):
    devices: int
    cols: int
    ratio: int
    row_blocks: int
    col_blocks: int
    share_blocks: int
    plane: int


def exchange(value):
    return lax.all_to_all(value, AXES, split_axis=0, concat_axis=0, tiled=True)


def quotient(value, size):
    return lax.shift_right_logical(value, jnp.int32(size.bit_length() - 1))


def remainder(value, size):
    return value & jnp.int32(size - 1)


def describe(block_map, sizes):
    local_subs, per_sub = block_map.shape

    def kernel(map_ref, out_ref):
        shape = out_ref.shape
        device = lax.broadcasted_iota(jnp.int32, shape, 0)
        field = lax.broadcasted_iota(jnp.int32, shape, 1)
        row = quotient(device, sizes.cols)
        col = remainder(device, sizes.cols)
        zero = jnp.zeros(shape, jnp.int32)
        wanted, share = zero, zero - 1
        slot = zero + sizes.row_blocks * sizes.col_blocks
        for s in range(local_subs):
            row_slot, col_slot = zero - 1, zero - 1
            for a in range(per_sub):
                block = map_ref[s, a]
                tile_row = quotient(block, sizes.row_blocks)
                wanted = jnp.where(
                    col * sizes.ratio + field == tile_row, remainder(block, sizes.col_blocks), wanted
                )
                share = jnp.where(
                    device == quotient(block, sizes.share_blocks),
                    remainder(block, sizes.share_blocks),
                    share,
                )
                row_slot = jnp.where(row == tile_row, remainder(block, sizes.row_blocks), row_slot)
                col_slot = jnp.where(
                    col == quotient(block, sizes.col_blocks),
                    remainder(block, sizes.col_blocks),
                    col_slot,
                )
            both = jnp.logical_and(row_slot >= 0, col_slot >= 0)
            slot = jnp.where(both, row_slot * sizes.col_blocks + col_slot, slot)
        out_ref[...] = jnp.where(
            field < sizes.ratio, wanted, jnp.where(field == sizes.ratio, slot, share)
        )

    return pl.pallas_call(
        kernel,
        out_shape=jax.ShapeDtypeStruct((sizes.devices, BLK), jnp.int32),
        in_specs=[SMEM],
        out_specs=VMEM,
        name="describe",
    )(block_map)


def pick_modes(table, modes, ratio):
    device_count = table.shape[0]
    width = modes.shape[1]

    def kernel(table_ref, modes_ref, out_ref):
        def one(device, carry):
            for h in range(ratio):
                out_ref[device, h] = modes_ref[table_ref[device, h]]
            return carry

        lax.fori_loop(0, device_count, one, 0, unroll=4)

    return pl.pallas_call(
        kernel,
        out_shape=jax.ShapeDtypeStruct((device_count, ratio, width, BLK), BF16),
        in_specs=[SMEM, VMEM],
        out_specs=VMEM,
        name="pick_modes",
    )(table, modes)


def condense(
    block_map, inv_interior, coupling, boundary_stiff, mass_interior, mass_boundary, sizes
):
    local_subs, interior, boundary = coupling.shape
    per_sub = boundary // BLK

    def kernel(
        map_ref,
        inv_ref,
        cpl_ref,
        stiff_ref,
        mi_ref,
        mb_ref,
        out_ref,
        k_ref,
        m_ref,
        d_ref,
    ):
        sub = pl.program_id(0)
        couple = cpl_ref[0]
        static_modes = (-jnp.dot(inv_ref[0], couple, preferred_element_type=F32)).astype(BF16)
        contract = (((0,), (0,)), ((), ()))
        stiff = stiff_ref[0].astype(F32) + lax.dot_general(
            couple, static_modes, contract, preferred_element_type=F32
        )
        weighted = (static_modes.astype(F32) * mi_ref[0]).astype(BF16)
        mass = lax.dot_general(static_modes, weighted, contract, preferred_element_type=F32)
        eye = lax.broadcasted_iota(jnp.int32, (BLK, BLK), 0) == lax.broadcasted_iota(
            jnp.int32, (BLK, BLK), 1
        )
        level = lax.broadcasted_iota(jnp.int32, (EXTRA, BLK), 0)
        for a in range(per_sub):
            block_a = map_ref[sub, a]
            rows = slice(a * BLK, (a + 1) * BLK)
            for b in range(per_sub):
                cols = slice(b * BLK, (b + 1) * BLK)
                owner = quotient(block_a, sizes.row_blocks) * sizes.cols + quotient(
                    map_ref[sub, b], sizes.col_blocks
                )
                stiff_block = stiff[rows, cols].astype(BF16)
                mass_block = mass[rows, cols]
                if a == b:
                    diagonal = (
                        jnp.sum(jnp.where(eye, mass_block, 0.0), axis=0, keepdims=True)
                        + mb_ref[0, :, cols]
                    )
                    d_ref[0, :, cols] = diagonal
                    high = diagonal.astype(BF16).astype(F32)
                    middle = (diagonal - high).astype(BF16).astype(F32)
                    low = diagonal - high - middle
                    parts = jnp.where(level == 0, high, jnp.where(level == 1, middle, low))
                    share = quotient(block_a, sizes.share_blocks)
                    out_ref[share, 2 * BLK : 2 * BLK + EXTRA] = parts.astype(BF16)
                    mass_block = jnp.where(eye, 0.0, mass_block)
                mass_block = mass_block.astype(BF16)
                out_ref[owner, :BLK] = stiff_block
                out_ref[owner, BLK : 2 * BLK] = mass_block
                k_ref[0, rows, cols] = stiff_block
                m_ref[0, rows, cols] = mass_block

    def piece(*shape):
        return pl.BlockSpec((1,) + shape, lambda s: (s, 0, 0))

    out_blocks = (sizes.devices, 2 * BLK + EXTRA, BLK)
    return pl.pallas_call(
        kernel,
        grid=(local_subs,),
        in_specs=[
            SMEM,
            piece(interior, interior),
            piece(interior, boundary),
            piece(boundary, boundary),
            piece(interior, 1),
            piece(1, boundary),
        ],
        out_specs=[
            pl.BlockSpec(out_blocks, lambda s: (0, 0, 0)),
            piece(boundary, boundary),
            piece(boundary, boundary),
            piece(1, boundary),
        ],
        out_shape=[
            jax.ShapeDtypeStruct(out_blocks, BF16),
            jax.ShapeDtypeStruct((local_subs, boundary, boundary), BF16),
            jax.ShapeDtypeStruct((local_subs, boundary, boundary), BF16),
            jax.ShapeDtypeStruct((local_subs, 1, boundary), F32),
        ],
        name="condense",
    )(
        block_map,
        inv_interior,
        coupling,
        boundary_stiff,
        mass_interior[:, :, None],
        mass_boundary[:, None, :],
    )


def cut_shares(out, step, send_ref, keep_ref, dims):
    _, y_size, x_size = dims
    z_size = dims[0]
    share = send_ref.shape[1]
    pairs = out.shape[0] // (2 * share)
    row, col = lax.axis_index("row"), lax.axis_index("col")
    my_z, my_y = quotient(row, y_size), remainder(row, y_size)
    my_x, mine = quotient(col, 2), remainder(col, 2) == 0
    for i in range(pairs):
        group = step * pairs + i
        x = remainder(group, x_size)
        y = remainder(quotient(group, x_size), y_size)
        z = quotient(group, x_size * y_size)
        slot = ((y ^ my_y) * x_size + (x ^ my_x)) * z_size + (z ^ my_z)
        even = out[2 * i * share : (2 * i + 1) * share]
        odd = out[(2 * i + 1) * share : (2 * i + 2) * share]
        keep_ref[slot] = jnp.where(mine, even, odd)
        send_ref[slot] = jnp.where(mine, odd, even).astype(BF16)


def whole(*shape):
    return pl.BlockSpec(shape, lambda i: (0,) * len(shape))


def project_stiff(block_map, fetched, matrix, dims, row_blocks):
    local_subs, boundary, _ = matrix.shape
    depth = local_subs * boundary
    per_sub = boundary // BLK
    groups = dims[0] * dims[1] * dims[2]
    row_count, _, ratio, width, _ = fetched.shape
    modes = row_count * width
    share = modes // (2 * groups)
    chunk = modes // 2

    def kernel(map_ref, in_ref, m_ref, send_ref, keep_ref, t_ref, y_ref):
        step = pl.program_id(0)

        @pl.when(step == 0)
        def _():
            for s in range(local_subs):
                for a in range(per_sub):
                    tile_row = quotient(map_ref[s, a], row_blocks)
                    c = quotient(tile_row, ratio)
                    h = remainder(tile_row, ratio)
                    k = (s * per_sub + a) * BLK
                    for r in range(row_count):
                        t_ref[r * width : (r + 1) * width, k : k + BLK] = in_ref[r, c, h]

        rows = pl.ds(pl.multiple_of(step * chunk, chunk), chunk)
        for s in range(local_subs):
            span = slice(s * boundary, (s + 1) * boundary)
            y_ref[:, span] = jnp.dot(
                t_ref[rows, span], m_ref[s], preferred_element_type=F32
            ).astype(BF16)
        out = lax.dot_general(
            y_ref[...], t_ref[...], (((1,), (1,)), ((), ())), preferred_element_type=F32
        )
        cut_shares(out, step, send_ref, keep_ref, dims)

    return pl.pallas_call(
        kernel,
        grid=(modes // chunk,),
        in_specs=[SMEM, whole(*fetched.shape), whole(local_subs, boundary, boundary)],
        out_specs=[
            whole(groups, share, modes),
            whole(groups, share, modes),
            whole(modes, depth),
        ],
        out_shape=[
            jax.ShapeDtypeStruct((groups, share, modes), BF16),
            jax.ShapeDtypeStruct((groups, share, modes), F32),
            jax.ShapeDtypeStruct((modes, depth), BF16),
        ],
        scratch_shapes=[pltpu.VMEM((chunk, depth), BF16)],
        name="project_stiff",
    )(block_map, fetched, matrix)


def mix_mass(qt, matrix, diagonal):
    modes, depth = qt.shape
    local_subs, boundary, _ = matrix.shape
    chunk = modes // 4

    def kernel(t_ref, m_ref, d_ref, y_ref):
        for s in range(local_subs):
            span = slice(s * boundary, (s + 1) * boundary)
            left = t_ref[:, span]
            y = jnp.dot(left, m_ref[s], preferred_element_type=F32)
            y_ref[:, span] = (y + left.astype(F32) * d_ref[s]).astype(BF16)

    rows = pl.BlockSpec((chunk, depth), lambda i: (i, 0))
    return pl.pallas_call(
        kernel,
        grid=(modes // chunk,),
        in_specs=[rows, whole(local_subs, boundary, boundary), whole(local_subs, 1, boundary)],
        out_specs=rows,
        out_shape=jax.ShapeDtypeStruct((modes, depth), BF16),
        name="mix_mass",
    )(qt, matrix, diagonal)


def project_mass(mixed, qt, dims):
    modes, depth = qt.shape
    groups = dims[0] * dims[1] * dims[2]
    share = modes // (2 * groups)
    chunk = modes // 2

    def kernel(y_ref, t_ref, send_ref, keep_ref):
        out = lax.dot_general(
            y_ref[...], t_ref[...], (((1,), (1,)), ((), ())), preferred_element_type=F32
        )
        cut_shares(out, pl.program_id(0), send_ref, keep_ref, dims)

    return pl.pallas_call(
        kernel,
        grid=(modes // chunk,),
        in_specs=[pl.BlockSpec((chunk, depth), lambda i: (i, 0)), whole(modes, depth)],
        out_specs=[whole(groups, share, modes), whole(groups, share, modes)],
        out_shape=[
            jax.ShapeDtypeStruct((groups, share, modes), BF16),
            jax.ShapeDtypeStruct((groups, share, modes), F32),
        ],
        name="project_mass",
    )(mixed, qt)


def swap(value, offset, device_count):
    return lax.ppermute(value, AXES, [(i, i ^ offset) for i in range(device_count)])


def reduce_shares(send, keep, sizes):
    got = swap(send, 1, sizes.devices)
    summed = keep + got.astype(F32)
    depth = sizes.devices // sizes.plane
    summed = summed.reshape((sizes.plane // 2, depth) + summed.shape[1:])
    total = summed[0]
    for d in range(1, sizes.plane // 2):
        got = swap(summed[d].astype(BF16), 2 * d, sizes.devices)
        total = total + got.astype(F32)
    result = total[0]
    for d in range(1, depth):
        got = swap(total[d].astype(BF16), d * sizes.plane, sizes.devices)
        result = result + got.astype(F32)
    return result


def clear_tiles(table, sizes):
    shape = (sizes.row_blocks * BLK, sizes.col_blocks * BLK)

    def kernel(_table, stiff_ref, mass_ref, zero_ref, sem):
        zero_ref[...] = jnp.zeros_like(zero_ref)
        fills = [
            pltpu.make_async_copy(zero_ref, ref.at[pl.ds(i * BLK, BLK), :], sem.at[i, j])
            for i in range(sizes.row_blocks)
            for j, ref in enumerate((stiff_ref, mass_ref))
        ]
        for fill in fills:
            fill.start()
        for fill in fills:
            fill.wait()

    return pl.pallas_call(
        kernel,
        in_specs=[ANY],
        out_specs=[ANY, ANY],
        out_shape=[jax.ShapeDtypeStruct(shape, BF16), jax.ShapeDtypeStruct(shape, BF16)],
        scratch_shapes=[
            pltpu.VMEM((BLK, shape[1]), BF16),
            pltpu.SemaphoreType.DMA((sizes.row_blocks, 2)),
        ],
        name="clear_tiles",
    )(table)


def place(table, order, slots, arrived, stiff_tile, mass_tile, sizes):
    count = sizes.devices
    limit = sizes.row_blocks * sizes.col_blocks

    def kernel(
        table_ref,
        order_ref,
        slot_ref,
        held_ref,
        _stiff,
        _mass,
        stiff_ref,
        mass_ref,
        share_ref,
        sums_ref,
        sem,
    ):
        def copies(j):
            slot = slot_ref[j]
            row = pl.multiple_of(quotient(slot, sizes.col_blocks) * BLK, BLK)
            col = pl.multiple_of(remainder(slot, sizes.col_blocks) * BLK, BLK)
            return [
                pltpu.make_async_copy(
                    sums_ref.at[j, pl.ds(i * BLK, BLK)],
                    ref.at[pl.ds(row, BLK), pl.ds(col, BLK)],
                    sem.at[j, i],
                )
                for i, ref in enumerate((stiff_ref, mass_ref))
            ]

        def last(j):
            ahead = slot_ref[jnp.minimum(j + 1, count - 1)]
            ends = jnp.logical_or(j == count - 1, ahead != slot_ref[j])
            return jnp.logical_and(slot_ref[j] < limit, ends)

        def one(j, total):
            block = held_ref[order_ref[j], : 2 * BLK].astype(F32)
            same = jnp.logical_and(j > 0, slot_ref[jnp.maximum(j - 1, 0)] == slot_ref[j])
            total = jnp.where(same, total + block, block)
            sums_ref[j] = total.astype(BF16)

            @pl.when(last(j))
            def _():
                for copy in copies(j):
                    copy.start()

            return total

        lax.fori_loop(0, count, one, jnp.zeros((2 * BLK, BLK), F32))
        share_ref[...] = jnp.zeros_like(share_ref)

        def add(device, carry):
            share = table_ref[device, sizes.ratio + 1]

            @pl.when(share >= 0)
            def _():
                parts = held_ref[device, 2 * BLK : 2 * BLK + EXTRA].astype(F32)
                share_ref[share] += parts[0:1] + parts[1:2] + parts[2:3]

            return carry

        lax.fori_loop(0, count, add, 0)

        def wait(j, carry):
            @pl.when(last(j))
            def _():
                for copy in copies(j):
                    copy.wait()

            return carry

        lax.fori_loop(0, count, wait, 0)

    return pl.pallas_call(
        kernel,
        in_specs=[SMEM, SMEM, SMEM, VMEM, ANY, ANY],
        out_specs=[ANY, ANY, VMEM],
        out_shape=[
            jax.ShapeDtypeStruct(stiff_tile.shape, BF16),
            jax.ShapeDtypeStruct(mass_tile.shape, BF16),
            jax.ShapeDtypeStruct((sizes.share_blocks, 1, BLK), F32),
        ],
        input_output_aliases={4: 0, 5: 1},
        scratch_shapes=[
            pltpu.VMEM((count, 2 * BLK, BLK), BF16),
            pltpu.SemaphoreType.DMA((count, 2)),
        ],
        name="place",
    )(table, order, slots, arrived, stiff_tile, mass_tile)


def reduction(inv_interior, coupling, boundary_stiff, mass_interior, mass_boundary, block_map, modes):
    row_count = lax.axis_size("row")
    col_count = lax.axis_size("col")
    tile_cols, width = modes.shape
    tile_rows = tile_cols * col_count // row_count
    sizes = Sizes(
        devices=row_count * col_count,
        cols=col_count,
        ratio=row_count // col_count,
        row_blocks=tile_rows // BLK,
        col_blocks=tile_cols // BLK,
        share_blocks=tile_rows // BLK // col_count,
        plane=col_count // 2 * col_count,
    )
    x_size = col_count // 2
    y_size = x_size
    dims = (row_count // y_size, y_size, x_size)

    table = exchange(describe(block_map, sizes))
    turned = jnp.swapaxes(modes.reshape(sizes.col_blocks, BLK, width), 1, 2)
    wanted = pick_modes(table, turned, sizes.ratio)
    fetched = exchange(wanted)
    blocks, stiff, mass, diagonal = condense(
        block_map, inv_interior, coupling, boundary_stiff, mass_interior, mass_boundary, sizes
    )
    stiff_tile, mass_tile = clear_tiles(table, sizes)
    blocks, fetched = lax.optimization_barrier((blocks, fetched))
    arrived = exchange(blocks)

    fetched = fetched.reshape(row_count, col_count, sizes.ratio, width, BLK)
    send, keep, qt = project_stiff(block_map, fetched, stiff, dims, sizes.row_blocks)
    reduced_stiff = reduce_shares(send, keep, sizes)
    mixed = mix_mass(qt, mass, diagonal)
    send, keep = project_mass(mixed, qt, dims)
    reduced_mass = reduce_shares(send, keep, sizes)

    slot = table[:, sizes.ratio]
    ids = jnp.arange(sizes.devices, dtype=jnp.int32)
    before = jnp.logical_or(
        slot[None, :] < slot[:, None],
        jnp.logical_and(slot[None, :] == slot[:, None], ids[None, :] < ids[:, None]),
    )
    rank = jnp.sum(before.astype(jnp.int32), axis=1)
    chosen = rank[None, :] == ids[:, None]
    order = jnp.sum(jnp.where(chosen, ids[None, :], 0), axis=1)
    slots = jnp.sum(jnp.where(chosen, slot[None, :], 0), axis=1)
    stiff_tile, mass_tile, mass_share = place(
        table, order, slots, arrived, stiff_tile, mass_tile, sizes
    )
    return stiff_tile, mass_tile, reduced_stiff, reduced_mass, mass_share.reshape(-1)


def solution(mesh):
    return jax.shard_map(
        reduction,
        mesh=mesh,
        in_specs=(
            P(AXES, None, None),
            P(AXES, None, None),
            P(AXES, None, None),
            P(AXES, None),
            P(AXES, None),
            P(AXES, None),
            P("col", "row"),
        ),
        out_specs=(P("row", "col"), P("row", "col"), P(AXES, None), P(AXES, None), P(AXES)),
        check_vma=False,
    )
```

```python
from typing import NamedTuple

import jax
import jax.numpy as jnp
from jax import lax
from jax.experimental import pallas as pl
from jax.experimental.pallas import tpu as pltpu
from jax.sharding import PartitionSpec as P


BLK = 128
EXTRA = 8
AXES = ("row", "col")
F32 = jnp.float32
BF16 = jnp.bfloat16
VMEM = pl.BlockSpec(memory_space=pltpu.VMEM)
SMEM = pl.BlockSpec(memory_space=pltpu.SMEM)
ANY = pl.BlockSpec(memory_space=pl.ANY)


class Sizes(NamedTuple):
    devices: int
    cols: int
    ratio: int
    row_blocks: int
    col_blocks: int
    share_blocks: int
    plane: int


def exchange(value):
    return lax.all_to_all(value, AXES, split_axis=0, concat_axis=0, tiled=True)


def quotient(value, size):
    return lax.shift_right_logical(value, jnp.int32(size.bit_length() - 1))


def remainder(value, size):
    return value & jnp.int32(size - 1)


def describe(block_map, sizes):
    local_subs, per_sub = block_map.shape

    def kernel(map_ref, out_ref):
        shape = out_ref.shape
        device = lax.broadcasted_iota(jnp.int32, shape, 0)
        field = lax.broadcasted_iota(jnp.int32, shape, 1)
        row = quotient(device, sizes.cols)
        col = remainder(device, sizes.cols)
        zero = jnp.zeros(shape, jnp.int32)
        wanted, share = zero, zero - 1
        slot = zero + sizes.row_blocks * sizes.col_blocks
        for s in range(local_subs):
            row_slot, col_slot = zero - 1, zero - 1
            for a in range(per_sub):
                block = map_ref[s, a]
                tile_row = quotient(block, sizes.row_blocks)
                wanted = jnp.where(
                    col * sizes.ratio + field == tile_row, remainder(block, sizes.col_blocks), wanted
                )
                share = jnp.where(
                    device == quotient(block, sizes.share_blocks),
                    remainder(block, sizes.share_blocks),
                    share,
                )
                row_slot = jnp.where(row == tile_row, remainder(block, sizes.row_blocks), row_slot)
                col_slot = jnp.where(
                    col == quotient(block, sizes.col_blocks),
                    remainder(block, sizes.col_blocks),
                    col_slot,
                )
            both = jnp.logical_and(row_slot >= 0, col_slot >= 0)
            slot = jnp.where(both, row_slot * sizes.col_blocks + col_slot, slot)
        out_ref[...] = jnp.where(
            field < sizes.ratio, wanted, jnp.where(field == sizes.ratio, slot, share)
        )

    return pl.pallas_call(
        kernel,
        out_shape=jax.ShapeDtypeStruct((sizes.devices, BLK), jnp.int32),
        in_specs=[SMEM],
        out_specs=VMEM,
        name="describe",
    )(block_map)


def pick_modes(table, modes, ratio):
    device_count = table.shape[0]
    width = modes.shape[1]

    def kernel(table_ref, modes_ref, out_ref):
        def one(device, carry):
            for h in range(ratio):
                out_ref[device, h] = modes_ref[table_ref[device, h]]
            return carry

        lax.fori_loop(0, device_count, one, 0, unroll=4)

    return pl.pallas_call(
        kernel,
        out_shape=jax.ShapeDtypeStruct((device_count, ratio, width, BLK), BF16),
        in_specs=[SMEM, VMEM],
        out_specs=VMEM,
        name="pick_modes",
    )(table, modes)


def condense(
    block_map, inv_interior, coupling, boundary_stiff, mass_interior, mass_boundary, sizes
):
    local_subs, interior, boundary = coupling.shape
    per_sub = boundary // BLK

    def kernel(
        map_ref,
        inv_ref,
        cpl_ref,
        stiff_ref,
        mi_ref,
        mb_ref,
        out_ref,
        k_ref,
        m_ref,
        d_ref,
    ):
        sub = pl.program_id(0)
        couple = cpl_ref[0]
        static_modes = (-jnp.dot(inv_ref[0], couple, preferred_element_type=F32)).astype(BF16)
        contract = (((0,), (0,)), ((), ()))
        stiff = stiff_ref[0].astype(F32) + lax.dot_general(
            couple, static_modes, contract, preferred_element_type=F32
        )
        weighted = (static_modes.astype(F32) * mi_ref[0]).astype(BF16)
        mass = lax.dot_general(static_modes, weighted, contract, preferred_element_type=F32)
        eye = lax.broadcasted_iota(jnp.int32, (BLK, BLK), 0) == lax.broadcasted_iota(
            jnp.int32, (BLK, BLK), 1
        )
        level = lax.broadcasted_iota(jnp.int32, (EXTRA, BLK), 0)
        for a in range(per_sub):
            block_a = map_ref[sub, a]
            rows = slice(a * BLK, (a + 1) * BLK)
            for b in range(per_sub):
                cols = slice(b * BLK, (b + 1) * BLK)
                owner = quotient(block_a, sizes.row_blocks) * sizes.cols + quotient(
                    map_ref[sub, b], sizes.col_blocks
                )
                stiff_block = stiff[rows, cols].astype(BF16)
                mass_block = mass[rows, cols]
                if a == b:
                    diagonal = (
                        jnp.sum(jnp.where(eye, mass_block, 0.0), axis=0, keepdims=True)
                        + mb_ref[0, :, cols]
                    )
                    d_ref[0, :, cols] = diagonal
                    high = diagonal.astype(BF16).astype(F32)
                    middle = (diagonal - high).astype(BF16).astype(F32)
                    low = diagonal - high - middle
                    parts = jnp.where(level == 0, high, jnp.where(level == 1, middle, low))
                    share = quotient(block_a, sizes.share_blocks)
                    out_ref[share, 2 * BLK : 2 * BLK + EXTRA] = parts.astype(BF16)
                    mass_block = jnp.where(eye, 0.0, mass_block)
                mass_block = mass_block.astype(BF16)
                out_ref[owner, :BLK] = stiff_block
                out_ref[owner, BLK : 2 * BLK] = mass_block
                k_ref[0, rows, cols] = stiff_block
                m_ref[0, rows, cols] = mass_block

    def piece(*shape):
        return pl.BlockSpec((1,) + shape, lambda s: (s, 0, 0))

    out_blocks = (sizes.devices, 2 * BLK + EXTRA, BLK)
    return pl.pallas_call(
        kernel,
        grid=(local_subs,),
        in_specs=[
            SMEM,
            piece(interior, interior),
            piece(interior, boundary),
            piece(boundary, boundary),
            piece(interior, 1),
            piece(1, boundary),
        ],
        out_specs=[
            pl.BlockSpec(out_blocks, lambda s: (0, 0, 0)),
            piece(boundary, boundary),
            piece(boundary, boundary),
            piece(1, boundary),
        ],
        out_shape=[
            jax.ShapeDtypeStruct(out_blocks, BF16),
            jax.ShapeDtypeStruct((local_subs, boundary, boundary), BF16),
            jax.ShapeDtypeStruct((local_subs, boundary, boundary), BF16),
            jax.ShapeDtypeStruct((local_subs, 1, boundary), F32),
        ],
        name="condense",
    )(
        block_map,
        inv_interior,
        coupling,
        boundary_stiff,
        mass_interior[:, :, None],
        mass_boundary[:, None, :],
    )


def cut_shares(out, step, send_ref, keep_ref, dims):
    _, y_size, x_size = dims
    z_size = dims[0]
    share = send_ref.shape[1]
    pairs = out.shape[0] // (2 * share)
    row, col = lax.axis_index("row"), lax.axis_index("col")
    my_z, my_y = quotient(row, y_size), remainder(row, y_size)
    my_x, mine = quotient(col, 2), remainder(col, 2) == 0
    for i in range(pairs):
        group = step * pairs + i
        x = remainder(group, x_size)
        y = remainder(quotient(group, x_size), y_size)
        z = quotient(group, x_size * y_size)
        slot = ((y ^ my_y) * x_size + (x ^ my_x)) * z_size + (z ^ my_z)
        even = out[2 * i * share : (2 * i + 1) * share]
        odd = out[(2 * i + 1) * share : (2 * i + 2) * share]
        keep_ref[slot] = jnp.where(mine, even, odd)
        send_ref[slot] = jnp.where(mine, odd, even).astype(BF16)


def whole(*shape):
    return pl.BlockSpec(shape, lambda i: (0,) * len(shape))


def project_stiff(block_map, fetched, matrix, dims, row_blocks):
    local_subs, boundary, _ = matrix.shape
    depth = local_subs * boundary
    per_sub = boundary // BLK
    groups = dims[0] * dims[1] * dims[2]
    row_count, _, ratio, width, _ = fetched.shape
    modes = row_count * width
    share = modes // (2 * groups)
    chunk = modes // 2

    def kernel(map_ref, in_ref, m_ref, send_ref, keep_ref, t_ref, y_ref):
        step = pl.program_id(0)

        @pl.when(step == 0)
        def _():
            for s in range(local_subs):
                for a in range(per_sub):
                    tile_row = quotient(map_ref[s, a], row_blocks)
                    c = quotient(tile_row, ratio)
                    h = remainder(tile_row, ratio)
                    k = (s * per_sub + a) * BLK
                    for r in range(row_count):
                        t_ref[r * width : (r + 1) * width, k : k + BLK] = in_ref[r, c, h]

        rows = pl.ds(pl.multiple_of(step * chunk, chunk), chunk)
        for s in range(local_subs):
            span = slice(s * boundary, (s + 1) * boundary)
            y_ref[:, span] = jnp.dot(
                t_ref[rows, span], m_ref[s], preferred_element_type=F32
            ).astype(BF16)
        out = lax.dot_general(
            y_ref[...], t_ref[...], (((1,), (1,)), ((), ())), preferred_element_type=F32
        )
        cut_shares(out, step, send_ref, keep_ref, dims)

    return pl.pallas_call(
        kernel,
        grid=(modes // chunk,),
        in_specs=[SMEM, whole(*fetched.shape), whole(local_subs, boundary, boundary)],
        out_specs=[
            whole(groups, share, modes),
            whole(groups, share, modes),
            whole(modes, depth),
        ],
        out_shape=[
            jax.ShapeDtypeStruct((groups, share, modes), BF16),
            jax.ShapeDtypeStruct((groups, share, modes), F32),
            jax.ShapeDtypeStruct((modes, depth), BF16),
        ],
        scratch_shapes=[pltpu.VMEM((chunk, depth), BF16)],
        name="project_stiff",
    )(block_map, fetched, matrix)


def mix_mass(qt, matrix, diagonal):
    modes, depth = qt.shape
    local_subs, boundary, _ = matrix.shape
    chunk = modes // 4

    def kernel(t_ref, m_ref, d_ref, y_ref):
        for s in range(local_subs):
            span = slice(s * boundary, (s + 1) * boundary)
            left = t_ref[:, span]
            y = jnp.dot(left, m_ref[s], preferred_element_type=F32)
            y_ref[:, span] = (y + left.astype(F32) * d_ref[s]).astype(BF16)

    rows = pl.BlockSpec((chunk, depth), lambda i: (i, 0))
    return pl.pallas_call(
        kernel,
        grid=(modes // chunk,),
        in_specs=[rows, whole(local_subs, boundary, boundary), whole(local_subs, 1, boundary)],
        out_specs=rows,
        out_shape=jax.ShapeDtypeStruct((modes, depth), BF16),
        name="mix_mass",
    )(qt, matrix, diagonal)


def project_mass(mixed, qt, dims):
    modes, depth = qt.shape
    groups = dims[0] * dims[1] * dims[2]
    share = modes // (2 * groups)
    chunk = modes // 2

    def kernel(y_ref, t_ref, send_ref, keep_ref):
        out = lax.dot_general(
            y_ref[...], t_ref[...], (((1,), (1,)), ((), ())), preferred_element_type=F32
        )
        cut_shares(out, pl.program_id(0), send_ref, keep_ref, dims)

    return pl.pallas_call(
        kernel,
        grid=(modes // chunk,),
        in_specs=[pl.BlockSpec((chunk, depth), lambda i: (i, 0)), whole(modes, depth)],
        out_specs=[whole(groups, share, modes), whole(groups, share, modes)],
        out_shape=[
            jax.ShapeDtypeStruct((groups, share, modes), BF16),
            jax.ShapeDtypeStruct((groups, share, modes), F32),
        ],
        name="project_mass",
    )(mixed, qt)


def swap(value, offset, device_count):
    return lax.ppermute(value, AXES, [(i, i ^ offset) for i in range(device_count)])


def reduce_shares(send, keep, sizes):
    got = swap(send, 1, sizes.devices)
    depth = sizes.devices // sizes.plane
    shape = (sizes.plane // 2, depth) + keep.shape[1:]
    keep, got = keep.reshape(shape), got.reshape(shape)
    summed = [keep[d] + got[d].astype(F32) for d in range(sizes.plane // 2)]
    total = summed[0]
    for d in range(1, sizes.plane // 2):
        got = swap(summed[d].astype(BF16), 2 * d, sizes.devices)
        total = total + got.astype(F32)
    result = total[0]
    for d in range(1, depth):
        got = swap(total[d].astype(BF16), d * sizes.plane, sizes.devices)
        result = result + got.astype(F32)
    return result


def clear_tiles(table, sizes):
    shape = (sizes.row_blocks * BLK, sizes.col_blocks * BLK)

    def kernel(_table, stiff_ref, mass_ref, zero_ref, sem):
        zero_ref[...] = jnp.zeros_like(zero_ref)
        fills = [
            pltpu.make_async_copy(zero_ref, ref.at[pl.ds(i * BLK, BLK), :], sem.at[i, j])
            for i in range(sizes.row_blocks)
            for j, ref in enumerate((stiff_ref, mass_ref))
        ]
        for fill in fills:
            fill.start()
        for fill in fills:
            fill.wait()

    return pl.pallas_call(
        kernel,
        in_specs=[ANY],
        out_specs=[ANY, ANY],
        out_shape=[jax.ShapeDtypeStruct(shape, BF16), jax.ShapeDtypeStruct(shape, BF16)],
        scratch_shapes=[
            pltpu.VMEM((BLK, shape[1]), BF16),
            pltpu.SemaphoreType.DMA((sizes.row_blocks, 2)),
        ],
        name="clear_tiles",
    )(table)


def place(table, order, slots, arrived, stiff_tile, mass_tile, sizes):
    count = sizes.devices
    limit = sizes.row_blocks * sizes.col_blocks

    def kernel(
        table_ref,
        order_ref,
        slot_ref,
        held_ref,
        _stiff,
        _mass,
        stiff_ref,
        mass_ref,
        share_ref,
        total_ref,
        sums_ref,
        sem,
    ):
        def copies(j, blocks):
            slot = slot_ref[j]
            row = pl.multiple_of(quotient(slot, sizes.col_blocks) * BLK, BLK)
            col = pl.multiple_of(remainder(slot, sizes.col_blocks) * BLK, BLK)
            return [
                pltpu.make_async_copy(
                    blocks.at[pl.ds(i * BLK, BLK)],
                    ref.at[pl.ds(row, BLK), pl.ds(col, BLK)],
                    sem.at[j, i],
                )
                for i, ref in enumerate((stiff_ref, mass_ref))
            ]

        def ends(j):
            slot = slot_ref[j]
            first = jnp.logical_or(j == 0, slot_ref[jnp.maximum(j - 1, 0)] != slot)
            last = jnp.logical_or(j == count - 1, slot_ref[jnp.minimum(j + 1, count - 1)] != slot)
            return slot < limit, first, last

        def one(j, carry):
            valid, first, last = ends(j)
            single = jnp.logical_and(first, last)
            source = order_ref[j]

            @pl.when(jnp.logical_and(valid, single))
            def _():
                for copy in copies(j, held_ref.at[source]):
                    copy.start()

            @pl.when(jnp.logical_and(valid, jnp.logical_not(single)))
            def _():
                block = held_ref[source, : 2 * BLK].astype(F32)
                total = block + jnp.where(first, 0.0, total_ref[...])
                total_ref[...] = total

                @pl.when(last)
                def _():
                    sums_ref[j] = total.astype(BF16)
                    for copy in copies(j, sums_ref.at[j]):
                        copy.start()

            return carry

        total_ref[...] = jnp.zeros_like(total_ref)
        lax.fori_loop(0, count, one, 0)
        share_ref[...] = jnp.zeros_like(share_ref)

        def add(device, carry):
            share = table_ref[device, sizes.ratio + 1]

            @pl.when(share >= 0)
            def _():
                parts = held_ref[device, 2 * BLK : 2 * BLK + EXTRA].astype(F32)
                share_ref[share] += parts[0:1] + parts[1:2] + parts[2:3]

            return carry

        lax.fori_loop(0, count, add, 0)

        def wait(j, carry):
            valid, _, last = ends(j)

            @pl.when(jnp.logical_and(valid, last))
            def _():
                for copy in copies(j, sums_ref.at[j]):
                    copy.wait()

            return carry

        lax.fori_loop(0, count, wait, 0)

    return pl.pallas_call(
        kernel,
        in_specs=[SMEM, SMEM, SMEM, VMEM, ANY, ANY],
        out_specs=[ANY, ANY, VMEM],
        out_shape=[
            jax.ShapeDtypeStruct(stiff_tile.shape, BF16),
            jax.ShapeDtypeStruct(mass_tile.shape, BF16),
            jax.ShapeDtypeStruct((sizes.share_blocks, 1, BLK), F32),
        ],
        input_output_aliases={4: 0, 5: 1},
        scratch_shapes=[
            pltpu.VMEM((2 * BLK, BLK), F32),
            pltpu.VMEM((count, 2 * BLK, BLK), BF16),
            pltpu.SemaphoreType.DMA((count, 2)),
        ],
        name="place",
    )(table, order, slots, arrived, stiff_tile, mass_tile)


def reduction(inv_interior, coupling, boundary_stiff, mass_interior, mass_boundary, block_map, modes):
    row_count = lax.axis_size("row")
    col_count = lax.axis_size("col")
    tile_cols, width = modes.shape
    tile_rows = tile_cols * col_count // row_count
    sizes = Sizes(
        devices=row_count * col_count,
        cols=col_count,
        ratio=row_count // col_count,
        row_blocks=tile_rows // BLK,
        col_blocks=tile_cols // BLK,
        share_blocks=tile_rows // BLK // col_count,
        plane=col_count // 2 * col_count,
    )
    x_size = col_count // 2
    y_size = x_size
    dims = (row_count // y_size, y_size, x_size)

    table = exchange(describe(block_map, sizes))
    turned = jnp.swapaxes(modes.reshape(sizes.col_blocks, BLK, width), 1, 2)
    wanted = pick_modes(table, turned, sizes.ratio)
    fetched = exchange(wanted)
    blocks, stiff, mass, diagonal = condense(
        block_map, inv_interior, coupling, boundary_stiff, mass_interior, mass_boundary, sizes
    )
    stiff_tile, mass_tile = clear_tiles(table, sizes)
    blocks, fetched = lax.optimization_barrier((blocks, fetched))
    arrived = exchange(blocks)

    fetched = fetched.reshape(row_count, col_count, sizes.ratio, width, BLK)
    send, keep, qt = project_stiff(block_map, fetched, stiff, dims, sizes.row_blocks)
    reduced_stiff = reduce_shares(send, keep, sizes)
    mixed = mix_mass(qt, mass, diagonal)
    send, keep = project_mass(mixed, qt, dims)
    reduced_mass = reduce_shares(send, keep, sizes)

    slot = table[:, sizes.ratio]
    ids = jnp.arange(sizes.devices, dtype=jnp.int32)
    before = jnp.logical_or(
        slot[None, :] < slot[:, None],
        jnp.logical_and(slot[None, :] == slot[:, None], ids[None, :] < ids[:, None]),
    )
    rank = jnp.sum(before.astype(jnp.int32), axis=1)
    chosen = rank[None, :] == ids[:, None]
    order = jnp.sum(jnp.where(chosen, ids[None, :], 0), axis=1)
    slots = jnp.sum(jnp.where(chosen, slot[None, :], 0), axis=1)
    stiff_tile, mass_tile, mass_share = place(
        table, order, slots, arrived, stiff_tile, mass_tile, sizes
    )
    return stiff_tile, mass_tile, reduced_stiff, reduced_mass, mass_share.reshape(-1)


def solution(mesh):
    return jax.shard_map(
        reduction,
        mesh=mesh,
        in_specs=(
            P(AXES, None, None),
            P(AXES, None, None),
            P(AXES, None, None),
            P(AXES, None),
            P(AXES, None),
            P(AXES, None),
            P("col", "row"),
        ),
        out_specs=(P("row", "col"), P("row", "col"), P(AXES, None), P(AXES, None), P(AXES)),
        check_vma=False,
    )
```

```python
from typing import NamedTuple

import jax
import jax.numpy as jnp
from jax import lax
from jax.experimental import pallas as pl
from jax.experimental.pallas import tpu as pltpu
from jax.sharding import PartitionSpec as P


BLK = 128
EXTRA = 8
AXES = ("row", "col")
F32 = jnp.float32
BF16 = jnp.bfloat16
VMEM = pl.BlockSpec(memory_space=pltpu.VMEM)
SMEM = pl.BlockSpec(memory_space=pltpu.SMEM)
ANY = pl.BlockSpec(memory_space=pl.ANY)


class Sizes(NamedTuple):
    devices: int
    cols: int
    ratio: int
    row_blocks: int
    col_blocks: int
    share_blocks: int
    plane: int


def exchange(value):
    return lax.all_to_all(value, AXES, split_axis=0, concat_axis=0, tiled=True)


def quotient(value, size):
    return lax.shift_right_logical(value, jnp.int32(size.bit_length() - 1))


def remainder(value, size):
    return value & jnp.int32(size - 1)


def describe(block_map, sizes):
    local_subs, per_sub = block_map.shape

    def kernel(map_ref, out_ref):
        shape = out_ref.shape
        device = lax.broadcasted_iota(jnp.int32, shape, 0)
        field = lax.broadcasted_iota(jnp.int32, shape, 1)
        row = quotient(device, sizes.cols)
        col = remainder(device, sizes.cols)
        zero = jnp.zeros(shape, jnp.int32)
        wanted, share = zero, zero - 1
        slot = zero + sizes.row_blocks * sizes.col_blocks
        for s in range(local_subs):
            row_slot, col_slot = zero - 1, zero - 1
            for a in range(per_sub):
                block = map_ref[s, a]
                tile_row = quotient(block, sizes.row_blocks)
                wanted = jnp.where(
                    col * sizes.ratio + field == tile_row, remainder(block, sizes.col_blocks), wanted
                )
                share = jnp.where(
                    device == quotient(block, sizes.share_blocks),
                    remainder(block, sizes.share_blocks),
                    share,
                )
                row_slot = jnp.where(row == tile_row, remainder(block, sizes.row_blocks), row_slot)
                col_slot = jnp.where(
                    col == quotient(block, sizes.col_blocks),
                    remainder(block, sizes.col_blocks),
                    col_slot,
                )
            both = jnp.logical_and(row_slot >= 0, col_slot >= 0)
            slot = jnp.where(both, row_slot * sizes.col_blocks + col_slot, slot)
        out_ref[...] = jnp.where(
            field < sizes.ratio, wanted, jnp.where(field == sizes.ratio, slot, share)
        )

    return pl.pallas_call(
        kernel,
        out_shape=jax.ShapeDtypeStruct((sizes.devices, BLK), jnp.int32),
        in_specs=[SMEM],
        out_specs=VMEM,
        name="describe",
    )(block_map)


def pick_modes(table, modes, ratio):
    device_count = table.shape[0]
    width = modes.shape[1]

    def kernel(table_ref, modes_ref, out_ref):
        def one(device, carry):
            for h in range(ratio):
                out_ref[device, h] = modes_ref[table_ref[device, h]]
            return carry

        lax.fori_loop(0, device_count, one, 0, unroll=4)

    return pl.pallas_call(
        kernel,
        out_shape=jax.ShapeDtypeStruct((device_count, ratio, width, BLK), BF16),
        in_specs=[SMEM, VMEM],
        out_specs=VMEM,
        name="pick_modes",
    )(table, modes)


def condense(
    block_map, inv_interior, coupling, boundary_stiff, mass_interior, mass_boundary, sizes
):
    local_subs, interior, boundary = coupling.shape
    per_sub = boundary // BLK

    def kernel(
        map_ref,
        inv_ref,
        cpl_ref,
        stiff_ref,
        mi_ref,
        mb_ref,
        k_ref,
        m_ref,
        d_ref,
        *refs,
    ):
        near_refs, out_ref, sem = refs[: sizes.plane], refs[-2], refs[-1]
        sub = pl.program_id(0)
        me = lax.axis_index("row") * sizes.cols + lax.axis_index("col")
        couple = cpl_ref[0]
        static_modes = (-jnp.dot(inv_ref[0], couple, preferred_element_type=F32)).astype(BF16)
        contract = (((0,), (0,)), ((), ()))
        stiff = stiff_ref[0].astype(F32) + lax.dot_general(
            couple, static_modes, contract, preferred_element_type=F32
        )
        weighted = (static_modes.astype(F32) * mi_ref[0]).astype(BF16)
        mass = lax.dot_general(static_modes, weighted, contract, preferred_element_type=F32)
        eye = lax.broadcasted_iota(jnp.int32, (BLK, BLK), 0) == lax.broadcasted_iota(
            jnp.int32, (BLK, BLK), 1
        )
        level = lax.broadcasted_iota(jnp.int32, (EXTRA, BLK), 0)
        for a in range(per_sub):
            block_a = map_ref[sub, a]
            rows = slice(a * BLK, (a + 1) * BLK)
            for b in range(per_sub):
                cols = slice(b * BLK, (b + 1) * BLK)
                owner = quotient(block_a, sizes.row_blocks) * sizes.cols + quotient(
                    map_ref[sub, b], sizes.col_blocks
                )
                owner = owner ^ me
                near, far = remainder(owner, sizes.plane), quotient(owner, sizes.plane)
                stiff_block = stiff[rows, cols].astype(BF16)
                mass_block = mass[rows, cols]
                if a == b:
                    diagonal = (
                        jnp.sum(jnp.where(eye, mass_block, 0.0), axis=0, keepdims=True)
                        + mb_ref[0, :, cols]
                    )
                    d_ref[0, :, cols] = diagonal
                    high = diagonal.astype(BF16).astype(F32)
                    middle = (diagonal - high).astype(BF16).astype(F32)
                    low = diagonal - high - middle
                    parts = jnp.where(level == 0, high, jnp.where(level == 1, middle, low))
                    share = quotient(block_a, sizes.share_blocks) ^ me
                    out_ref[
                        remainder(share, sizes.plane),
                        quotient(share, sizes.plane),
                        2 * BLK : 2 * BLK + EXTRA,
                    ] = parts.astype(BF16)
                    mass_block = jnp.where(eye, 0.0, mass_block)
                mass_block = mass_block.astype(BF16)
                out_ref[near, far, :BLK] = stiff_block
                out_ref[near, far, BLK : 2 * BLK] = mass_block
                k_ref[0, rows, cols] = stiff_block
                m_ref[0, rows, cols] = mass_block

        @pl.when(sub == local_subs - 1)
        def _():
            copies = [
                pltpu.make_async_copy(out_ref.at[d], ref, sem.at[d])
                for d, ref in enumerate(near_refs)
            ]
            for copy in copies:
                copy.start()
            for copy in copies:
                copy.wait()

    def piece(*shape):
        return pl.BlockSpec((1,) + shape, lambda s: (s, 0, 0))

    out_blocks = (sizes.devices // sizes.plane, 2 * BLK + EXTRA, BLK)
    return pl.pallas_call(
        kernel,
        grid=(local_subs,),
        in_specs=[
            SMEM,
            piece(interior, interior),
            piece(interior, boundary),
            piece(boundary, boundary),
            piece(interior, 1),
            piece(1, boundary),
        ],
        out_specs=[
            piece(boundary, boundary),
            piece(boundary, boundary),
            piece(1, boundary),
        ]
        + [ANY] * sizes.plane,
        out_shape=[
            jax.ShapeDtypeStruct((local_subs, boundary, boundary), BF16),
            jax.ShapeDtypeStruct((local_subs, boundary, boundary), BF16),
            jax.ShapeDtypeStruct((local_subs, 1, boundary), F32),
        ]
        + [jax.ShapeDtypeStruct(out_blocks, BF16)] * sizes.plane,
        scratch_shapes=[
            pltpu.VMEM((sizes.plane,) + out_blocks, BF16),
            pltpu.SemaphoreType.DMA((sizes.plane,)),
        ],
        name="condense",
    )(
        block_map,
        inv_interior,
        coupling,
        boundary_stiff,
        mass_interior[:, :, None],
        mass_boundary[:, None, :],
    )


def cut_shares(out, step, send_ref, keep_ref, dims):
    _, y_size, x_size = dims
    z_size = dims[0]
    share = send_ref.shape[1]
    pairs = out.shape[0] // (2 * share)
    row, col = lax.axis_index("row"), lax.axis_index("col")
    my_z, my_y = quotient(row, y_size), remainder(row, y_size)
    my_x, mine = quotient(col, 2), remainder(col, 2) == 0
    for i in range(pairs):
        group = step * pairs + i
        x = remainder(group, x_size)
        y = remainder(quotient(group, x_size), y_size)
        z = quotient(group, x_size * y_size)
        slot = ((y ^ my_y) * x_size + (x ^ my_x)) * z_size + (z ^ my_z)
        even = out[2 * i * share : (2 * i + 1) * share]
        odd = out[(2 * i + 1) * share : (2 * i + 2) * share]
        keep_ref[slot] = jnp.where(mine, even, odd)
        send_ref[slot] = jnp.where(mine, odd, even).astype(BF16)


def whole(*shape):
    return pl.BlockSpec(shape, lambda i: (0,) * len(shape))


def project_stiff(block_map, fetched, matrix, dims, row_blocks):
    local_subs, boundary, _ = matrix.shape
    depth = local_subs * boundary
    per_sub = boundary // BLK
    groups = dims[0] * dims[1] * dims[2]
    row_count, _, ratio, width, _ = fetched.shape
    modes = row_count * width
    share = modes // (2 * groups)
    chunk = modes // 2

    def kernel(map_ref, in_ref, m_ref, send_ref, keep_ref, t_ref, y_ref):
        step = pl.program_id(0)

        @pl.when(step == 0)
        def _():
            for s in range(local_subs):
                for a in range(per_sub):
                    tile_row = quotient(map_ref[s, a], row_blocks)
                    c = quotient(tile_row, ratio)
                    h = remainder(tile_row, ratio)
                    k = (s * per_sub + a) * BLK
                    for r in range(row_count):
                        t_ref[r * width : (r + 1) * width, k : k + BLK] = in_ref[r, c, h]

        rows = pl.ds(pl.multiple_of(step * chunk, chunk), chunk)
        for s in range(local_subs):
            span = slice(s * boundary, (s + 1) * boundary)
            y_ref[:, span] = jnp.dot(
                t_ref[rows, span], m_ref[s], preferred_element_type=F32
            ).astype(BF16)
        out = lax.dot_general(
            y_ref[...], t_ref[...], (((1,), (1,)), ((), ())), preferred_element_type=F32
        )
        cut_shares(out, step, send_ref, keep_ref, dims)

    return pl.pallas_call(
        kernel,
        grid=(modes // chunk,),
        in_specs=[SMEM, whole(*fetched.shape), whole(local_subs, boundary, boundary)],
        out_specs=[
            whole(groups, share, modes),
            whole(groups, share, modes),
            whole(modes, depth),
        ],
        out_shape=[
            jax.ShapeDtypeStruct((groups, share, modes), BF16),
            jax.ShapeDtypeStruct((groups, share, modes), F32),
            jax.ShapeDtypeStruct((modes, depth), BF16),
        ],
        scratch_shapes=[pltpu.VMEM((chunk, depth), BF16)],
        name="project_stiff",
    )(block_map, fetched, matrix)


def mix_mass(qt, matrix, diagonal):
    modes, depth = qt.shape
    local_subs, boundary, _ = matrix.shape
    chunk = modes // 4

    def kernel(t_ref, m_ref, d_ref, y_ref):
        for s in range(local_subs):
            span = slice(s * boundary, (s + 1) * boundary)
            left = t_ref[:, span]
            y = jnp.dot(left, m_ref[s], preferred_element_type=F32)
            y_ref[:, span] = (y + left.astype(F32) * d_ref[s]).astype(BF16)

    rows = pl.BlockSpec((chunk, depth), lambda i: (i, 0))
    return pl.pallas_call(
        kernel,
        grid=(modes // chunk,),
        in_specs=[rows, whole(local_subs, boundary, boundary), whole(local_subs, 1, boundary)],
        out_specs=rows,
        out_shape=jax.ShapeDtypeStruct((modes, depth), BF16),
        name="mix_mass",
    )(qt, matrix, diagonal)


def project_mass(mixed, qt, dims):
    modes, depth = qt.shape
    groups = dims[0] * dims[1] * dims[2]
    share = modes // (2 * groups)
    chunk = modes // 2

    def kernel(y_ref, t_ref, send_ref, keep_ref):
        out = lax.dot_general(
            y_ref[...], t_ref[...], (((1,), (1,)), ((), ())), preferred_element_type=F32
        )
        cut_shares(out, pl.program_id(0), send_ref, keep_ref, dims)

    return pl.pallas_call(
        kernel,
        grid=(modes // chunk,),
        in_specs=[pl.BlockSpec((chunk, depth), lambda i: (i, 0)), whole(modes, depth)],
        out_specs=[whole(groups, share, modes), whole(groups, share, modes)],
        out_shape=[
            jax.ShapeDtypeStruct((groups, share, modes), BF16),
            jax.ShapeDtypeStruct((groups, share, modes), F32),
        ],
        name="project_mass",
    )(mixed, qt)


def swap(value, offset, device_count):
    return lax.ppermute(value, AXES, [(i, i ^ offset) for i in range(device_count)])


def reduce_shares(send, keep, sizes):
    got = swap(send, 1, sizes.devices)
    depth = sizes.devices // sizes.plane
    shape = (sizes.plane // 2, depth) + keep.shape[1:]
    keep, got = keep.reshape(shape), got.reshape(shape)
    summed = [keep[d] + got[d].astype(F32) for d in range(sizes.plane // 2)]
    total = summed[0]
    for d in range(1, sizes.plane // 2):
        got = swap(summed[d].astype(BF16), 2 * d, sizes.devices)
        total = total + got.astype(F32)
    result = total[0]
    for d in range(1, depth):
        got = swap(total[d].astype(BF16), d * sizes.plane, sizes.devices)
        result = result + got.astype(F32)
    return result


def spread_in_plane(blocks, sizes):
    near = [blocks[0]]
    for d in range(1, sizes.plane):
        near.append(swap(blocks[d], d, sizes.devices))
    return [jnp.stack([part[z] for part in near]) for z in range(sizes.devices // sizes.plane)]


def clear_tiles(table, sizes):
    shape = (sizes.row_blocks * BLK, sizes.col_blocks * BLK)

    def kernel(_table, stiff_ref, mass_ref, zero_ref, sem):
        zero_ref[...] = jnp.zeros_like(zero_ref)
        fills = [
            pltpu.make_async_copy(zero_ref, ref.at[pl.ds(i * BLK, BLK), :], sem.at[i, j])
            for i in range(sizes.row_blocks)
            for j, ref in enumerate((stiff_ref, mass_ref))
        ]
        for fill in fills:
            fill.start()
        for fill in fills:
            fill.wait()

    return pl.pallas_call(
        kernel,
        in_specs=[ANY],
        out_specs=[ANY, ANY],
        out_shape=[jax.ShapeDtypeStruct(shape, BF16), jax.ShapeDtypeStruct(shape, BF16)],
        scratch_shapes=[
            pltpu.VMEM((BLK, shape[1]), BF16),
            pltpu.SemaphoreType.DMA((sizes.row_blocks, 2)),
        ],
        name="clear_tiles",
    )(table)


def place(table, order, slots, arrived, stiff_tile, mass_tile, sizes):
    count = sizes.devices
    limit = sizes.row_blocks * sizes.col_blocks
    depth = len(arrived)
    height = 2 * BLK + EXTRA

    def kernel(*refs):
        table_ref, order_ref, slot_ref = refs[:3]
        in_refs = refs[3 : 3 + depth]
        stiff_ref, mass_ref, share_ref, held_ref, sums_ref, in_sem, sem = refs[-7:]
        me = lax.axis_index("row") * sizes.cols + lax.axis_index("col")
        loads = [
            pltpu.make_async_copy(
                ref, held_ref.at[pl.ds(z * sizes.plane, sizes.plane)], in_sem.at[z]
            )
            for z, ref in enumerate(in_refs)
        ]
        for load in loads:
            load.start()
        for load in loads:
            load.wait()

        def copies(j):
            slot = slot_ref[j]
            row = pl.multiple_of(quotient(slot, sizes.col_blocks) * BLK, BLK)
            col = pl.multiple_of(remainder(slot, sizes.col_blocks) * BLK, BLK)
            return [
                pltpu.make_async_copy(
                    sums_ref.at[j, pl.ds(i * BLK, BLK)],
                    ref.at[pl.ds(row, BLK), pl.ds(col, BLK)],
                    sem.at[j, i],
                )
                for i, ref in enumerate((stiff_ref, mass_ref))
            ]

        def last(j):
            ahead = slot_ref[jnp.minimum(j + 1, count - 1)]
            ends = jnp.logical_or(j == count - 1, ahead != slot_ref[j])
            return jnp.logical_and(slot_ref[j] < limit, ends)

        def one(j, total):
            block = held_ref[order_ref[j] ^ me, : 2 * BLK].astype(F32)
            same = jnp.logical_and(j > 0, slot_ref[jnp.maximum(j - 1, 0)] == slot_ref[j])
            total = jnp.where(same, total + block, block)
            sums_ref[j] = total.astype(BF16)

            @pl.when(last(j))
            def _():
                for copy in copies(j):
                    copy.start()

            return total

        lax.fori_loop(0, count, one, jnp.zeros((2 * BLK, BLK), F32))
        share_ref[...] = jnp.zeros_like(share_ref)

        def add(device, carry):
            share = table_ref[device, sizes.ratio + 1]

            @pl.when(share >= 0)
            def _():
                parts = held_ref[device ^ me, 2 * BLK : 2 * BLK + EXTRA].astype(F32)
                share_ref[share] += parts[0:1] + parts[1:2] + parts[2:3]

            return carry

        lax.fori_loop(0, count, add, 0)

        def wait(j, carry):
            @pl.when(last(j))
            def _():
                for copy in copies(j):
                    copy.wait()

            return carry

        lax.fori_loop(0, count, wait, 0)

    return pl.pallas_call(
        kernel,
        in_specs=[SMEM, SMEM, SMEM] + [ANY] * (depth + 2),
        out_specs=[ANY, ANY, VMEM],
        out_shape=[
            jax.ShapeDtypeStruct(stiff_tile.shape, BF16),
            jax.ShapeDtypeStruct(mass_tile.shape, BF16),
            jax.ShapeDtypeStruct((sizes.share_blocks, 1, BLK), F32),
        ],
        input_output_aliases={3 + depth: 0, 4 + depth: 1},
        scratch_shapes=[
            pltpu.VMEM((count, height, BLK), BF16),
            pltpu.VMEM((count, 2 * BLK, BLK), BF16),
            pltpu.SemaphoreType.DMA((depth,)),
            pltpu.SemaphoreType.DMA((count, 2)),
        ],
        name="place",
    )(table, order, slots, *arrived, stiff_tile, mass_tile)


def reduction(inv_interior, coupling, boundary_stiff, mass_interior, mass_boundary, block_map, modes):
    row_count = lax.axis_size("row")
    col_count = lax.axis_size("col")
    tile_cols, width = modes.shape
    tile_rows = tile_cols * col_count // row_count
    sizes = Sizes(
        devices=row_count * col_count,
        cols=col_count,
        ratio=row_count // col_count,
        row_blocks=tile_rows // BLK,
        col_blocks=tile_cols // BLK,
        share_blocks=tile_rows // BLK // col_count,
        plane=col_count // 2 * col_count,
    )
    x_size = col_count // 2
    y_size = x_size
    dims = (row_count // y_size, y_size, x_size)

    table = exchange(describe(block_map, sizes))
    turned = jnp.swapaxes(modes.reshape(sizes.col_blocks, BLK, width), 1, 2)
    wanted = pick_modes(table, turned, sizes.ratio)
    fetched = exchange(wanted)
    stiff, mass, diagonal, *blocks = condense(
        block_map, inv_interior, coupling, boundary_stiff, mass_interior, mass_boundary, sizes
    )
    spread = spread_in_plane(blocks, sizes)
    beside = swap(spread[1], sizes.plane, sizes.devices)
    stiff_tile, mass_tile = clear_tiles(table, sizes)
    late, fetched, stiff_tile, mass_tile = lax.optimization_barrier(
        (spread[2:], fetched, stiff_tile, mass_tile)
    )
    late = [swap(part, (2 + d) * sizes.plane, sizes.devices) for d, part in enumerate(late)]
    arrived = [spread[0], beside, *late]

    fetched = fetched.reshape(row_count, col_count, sizes.ratio, width, BLK)
    send, keep, qt = project_stiff(block_map, fetched, stiff, dims, sizes.row_blocks)
    reduced_stiff = reduce_shares(send, keep, sizes)
    mixed = mix_mass(qt, mass, diagonal)
    send, keep = project_mass(mixed, qt, dims)
    reduced_mass = reduce_shares(send, keep, sizes)

    slot = table[:, sizes.ratio]
    ids = jnp.arange(sizes.devices, dtype=jnp.int32)
    before = jnp.logical_or(
        slot[None, :] < slot[:, None],
        jnp.logical_and(slot[None, :] == slot[:, None], ids[None, :] < ids[:, None]),
    )
    rank = jnp.sum(before.astype(jnp.int32), axis=1)
    chosen = rank[None, :] == ids[:, None]
    order = jnp.sum(jnp.where(chosen, ids[None, :], 0), axis=1)
    slots = jnp.sum(jnp.where(chosen, slot[None, :], 0), axis=1)
    stiff_tile, mass_tile, mass_share = place(
        table, order, slots, arrived, stiff_tile, mass_tile, sizes
    )
    return stiff_tile, mass_tile, reduced_stiff, reduced_mass, mass_share.reshape(-1)


def solution(mesh):
    return jax.shard_map(
        reduction,
        mesh=mesh,
        in_specs=(
            P(AXES, None, None),
            P(AXES, None, None),
            P(AXES, None, None),
            P(AXES, None),
            P(AXES, None),
            P(AXES, None),
            P("col", "row"),
        ),
        out_specs=(P("row", "col"), P("row", "col"), P(AXES, None), P(AXES, None), P(AXES)),
        check_vma=False,
    )
```

```python
from typing import NamedTuple

import jax
import jax.numpy as jnp
from jax import lax
from jax.experimental import pallas as pl
from jax.experimental.pallas import tpu as pltpu
from jax.sharding import PartitionSpec as P


BLK = 128
EXTRA = 8
AXES = ("row", "col")
F32 = jnp.float32
BF16 = jnp.bfloat16
VMEM = pl.BlockSpec(memory_space=pltpu.VMEM)
SMEM = pl.BlockSpec(memory_space=pltpu.SMEM)
ANY = pl.BlockSpec(memory_space=pl.ANY)


class Sizes(NamedTuple):
    devices: int
    cols: int
    ratio: int
    row_blocks: int
    col_blocks: int
    share_blocks: int
    plane: int


def exchange(value):
    return lax.all_to_all(value, AXES, split_axis=0, concat_axis=0, tiled=True)


def quotient(value, size):
    return lax.shift_right_logical(value, jnp.int32(size.bit_length() - 1))


def remainder(value, size):
    return value & jnp.int32(size - 1)


def describe(block_map, sizes):
    local_subs, per_sub = block_map.shape

    def kernel(map_ref, out_ref):
        shape = out_ref.shape
        device = lax.broadcasted_iota(jnp.int32, shape, 0)
        field = lax.broadcasted_iota(jnp.int32, shape, 1)
        row = quotient(device, sizes.cols)
        col = remainder(device, sizes.cols)
        zero = jnp.zeros(shape, jnp.int32)
        wanted, share = zero, zero - 1
        slot = zero + sizes.row_blocks * sizes.col_blocks
        for s in range(local_subs):
            row_slot, col_slot = zero - 1, zero - 1
            for a in range(per_sub):
                block = map_ref[s, a]
                tile_row = quotient(block, sizes.row_blocks)
                wanted = jnp.where(
                    col * sizes.ratio + field == tile_row, remainder(block, sizes.col_blocks), wanted
                )
                share = jnp.where(
                    device == quotient(block, sizes.share_blocks),
                    remainder(block, sizes.share_blocks),
                    share,
                )
                row_slot = jnp.where(row == tile_row, remainder(block, sizes.row_blocks), row_slot)
                col_slot = jnp.where(
                    col == quotient(block, sizes.col_blocks),
                    remainder(block, sizes.col_blocks),
                    col_slot,
                )
            both = jnp.logical_and(row_slot >= 0, col_slot >= 0)
            slot = jnp.where(both, row_slot * sizes.col_blocks + col_slot, slot)
        out_ref[...] = jnp.where(
            field < sizes.ratio, wanted, jnp.where(field == sizes.ratio, slot, share)
        )

    return pl.pallas_call(
        kernel,
        out_shape=jax.ShapeDtypeStruct((sizes.devices, BLK), jnp.int32),
        in_specs=[SMEM],
        out_specs=VMEM,
        name="describe",
    )(block_map)


def pick_modes(table, modes, ratio):
    device_count = table.shape[0]
    width = modes.shape[1]

    def kernel(table_ref, modes_ref, out_ref):
        def one(device, carry):
            for h in range(ratio):
                out_ref[device, h] = modes_ref[table_ref[device, h]]
            return carry

        lax.fori_loop(0, device_count, one, 0, unroll=4)

    return pl.pallas_call(
        kernel,
        out_shape=jax.ShapeDtypeStruct((device_count, ratio, width, BLK), BF16),
        in_specs=[SMEM, VMEM],
        out_specs=VMEM,
        name="pick_modes",
    )(table, modes)


def condense(
    block_map, inv_interior, coupling, boundary_stiff, mass_interior, mass_boundary, sizes
):
    local_subs, interior, boundary = coupling.shape
    per_sub = boundary // BLK

    def kernel(
        map_ref,
        inv_ref,
        cpl_ref,
        stiff_ref,
        mi_ref,
        mb_ref,
        k_ref,
        m_ref,
        d_ref,
        *refs,
    ):
        near_refs, out_ref, sem = refs[: sizes.plane], refs[-2], refs[-1]
        sub = pl.program_id(0)
        me = lax.axis_index("row") * sizes.cols + lax.axis_index("col")
        couple = cpl_ref[0]
        static_modes = (-jnp.dot(inv_ref[0], couple, preferred_element_type=F32)).astype(BF16)
        contract = (((0,), (0,)), ((), ()))
        stiff = stiff_ref[0].astype(F32) + lax.dot_general(
            couple, static_modes, contract, preferred_element_type=F32
        )
        eye = lax.broadcasted_iota(jnp.int32, (BLK, BLK), 0) == lax.broadcasted_iota(
            jnp.int32, (BLK, BLK), 1
        )

        def own_row(ref):
            mine = lax.broadcasted_iota(jnp.int32, ref.shape, 0) == sub
            return jnp.sum(jnp.where(mine, ref[...], 0.0), axis=0, keepdims=True)

        masses, boundary_masses = own_row(mi_ref), own_row(mb_ref)
        column = jnp.concatenate(
            [
                jnp.sum(jnp.where(eye, masses[:, i : i + BLK], 0.0), axis=1, keepdims=True)
                for i in range(0, interior, BLK)
            ],
            axis=0,
        )
        weighted = (static_modes.astype(F32) * column).astype(BF16)
        mass = lax.dot_general(static_modes, weighted, contract, preferred_element_type=F32)
        level = lax.broadcasted_iota(jnp.int32, (EXTRA, BLK), 0)
        for a in range(per_sub):
            block_a = map_ref[sub, a]
            rows = slice(a * BLK, (a + 1) * BLK)
            for b in range(per_sub):
                cols = slice(b * BLK, (b + 1) * BLK)
                owner = quotient(block_a, sizes.row_blocks) * sizes.cols + quotient(
                    map_ref[sub, b], sizes.col_blocks
                )
                owner = owner ^ me
                near, far = remainder(owner, sizes.plane), quotient(owner, sizes.plane)
                stiff_block = stiff[rows, cols].astype(BF16)
                mass_block = mass[rows, cols]
                if a == b:
                    diagonal = (
                        jnp.sum(jnp.where(eye, mass_block, 0.0), axis=0, keepdims=True)
                        + boundary_masses[:, cols]
                    )
                    d_ref[0, :, cols] = diagonal
                    high = diagonal.astype(BF16).astype(F32)
                    middle = (diagonal - high).astype(BF16).astype(F32)
                    low = diagonal - high - middle
                    parts = jnp.where(level == 0, high, jnp.where(level == 1, middle, low))
                    share = quotient(block_a, sizes.share_blocks) ^ me
                    out_ref[
                        remainder(share, sizes.plane),
                        quotient(share, sizes.plane),
                        2 * BLK : 2 * BLK + EXTRA,
                    ] = parts.astype(BF16)
                    mass_block = jnp.where(eye, 0.0, mass_block)
                mass_block = mass_block.astype(BF16)
                out_ref[near, far, :BLK] = stiff_block
                out_ref[near, far, BLK : 2 * BLK] = mass_block
                k_ref[0, rows, cols] = stiff_block
                m_ref[0, rows, cols] = mass_block

        @pl.when(sub == local_subs - 1)
        def _():
            copies = [
                pltpu.make_async_copy(out_ref.at[d], ref, sem.at[d])
                for d, ref in enumerate(near_refs)
            ]
            for copy in copies:
                copy.start()
            for copy in copies:
                copy.wait()

    def piece(*shape):
        return pl.BlockSpec((1,) + shape, lambda s: (s, 0, 0))

    out_blocks = (sizes.devices // sizes.plane, 2 * BLK + EXTRA, BLK)
    return pl.pallas_call(
        kernel,
        grid=(local_subs,),
        in_specs=[
            SMEM,
            piece(interior, interior),
            piece(interior, boundary),
            piece(boundary, boundary),
            pl.BlockSpec((local_subs, interior), lambda s: (0, 0)),
            pl.BlockSpec((local_subs, boundary), lambda s: (0, 0)),
        ],
        out_specs=[
            piece(boundary, boundary),
            piece(boundary, boundary),
            piece(1, boundary),
        ]
        + [ANY] * sizes.plane,
        out_shape=[
            jax.ShapeDtypeStruct((local_subs, boundary, boundary), BF16),
            jax.ShapeDtypeStruct((local_subs, boundary, boundary), BF16),
            jax.ShapeDtypeStruct((local_subs, 1, boundary), F32),
        ]
        + [jax.ShapeDtypeStruct(out_blocks, BF16)] * sizes.plane,
        scratch_shapes=[
            pltpu.VMEM((sizes.plane,) + out_blocks, BF16),
            pltpu.SemaphoreType.DMA((sizes.plane,)),
        ],
        name="condense",
    )(
        block_map,
        inv_interior,
        coupling,
        boundary_stiff,
        mass_interior,
        mass_boundary,
    )


def cut_shares(out, step, send_ref, keep_ref, dims):
    _, y_size, x_size = dims
    z_size = dims[0]
    share = send_ref.shape[1]
    pairs = out.shape[0] // (2 * share)
    row, col = lax.axis_index("row"), lax.axis_index("col")
    my_z, my_y = quotient(row, y_size), remainder(row, y_size)
    my_x, mine = quotient(col, 2), remainder(col, 2) == 0
    for i in range(pairs):
        group = step * pairs + i
        x = remainder(group, x_size)
        y = remainder(quotient(group, x_size), y_size)
        z = quotient(group, x_size * y_size)
        slot = ((y ^ my_y) * x_size + (x ^ my_x)) * z_size + (z ^ my_z)
        even = out[2 * i * share : (2 * i + 1) * share]
        odd = out[(2 * i + 1) * share : (2 * i + 2) * share]
        keep_ref[slot] = jnp.where(mine, even, odd)
        send_ref[slot] = jnp.where(mine, odd, even).astype(BF16)


def whole(*shape):
    return pl.BlockSpec(shape, lambda i: (0,) * len(shape))


def project_stiff(block_map, fetched, matrix, dims, row_blocks):
    local_subs, boundary, _ = matrix.shape
    depth = local_subs * boundary
    per_sub = boundary // BLK
    groups = dims[0] * dims[1] * dims[2]
    row_count, _, ratio, width, _ = fetched.shape
    modes = row_count * width
    share = modes // (2 * groups)
    chunk = modes // 2

    def kernel(map_ref, in_ref, m_ref, send_ref, keep_ref, t_ref, y_ref):
        step = pl.program_id(0)

        @pl.when(step == 0)
        def _():
            for s in range(local_subs):
                for a in range(per_sub):
                    tile_row = quotient(map_ref[s, a], row_blocks)
                    c = quotient(tile_row, ratio)
                    h = remainder(tile_row, ratio)
                    k = (s * per_sub + a) * BLK
                    for r in range(row_count):
                        t_ref[r * width : (r + 1) * width, k : k + BLK] = in_ref[r, c, h]

        rows = pl.ds(pl.multiple_of(step * chunk, chunk), chunk)
        for s in range(local_subs):
            span = slice(s * boundary, (s + 1) * boundary)
            y_ref[:, span] = jnp.dot(
                t_ref[rows, span], m_ref[s], preferred_element_type=F32
            ).astype(BF16)
        out = lax.dot_general(
            y_ref[...], t_ref[...], (((1,), (1,)), ((), ())), preferred_element_type=F32
        )
        cut_shares(out, step, send_ref, keep_ref, dims)

    return pl.pallas_call(
        kernel,
        grid=(modes // chunk,),
        in_specs=[SMEM, whole(*fetched.shape), whole(local_subs, boundary, boundary)],
        out_specs=[
            whole(groups, share, modes),
            whole(groups, share, modes),
            whole(modes, depth),
        ],
        out_shape=[
            jax.ShapeDtypeStruct((groups, share, modes), BF16),
            jax.ShapeDtypeStruct((groups, share, modes), F32),
            jax.ShapeDtypeStruct((modes, depth), BF16),
        ],
        scratch_shapes=[pltpu.VMEM((chunk, depth), BF16)],
        name="project_stiff",
    )(block_map, fetched, matrix)


def mix_mass(qt, matrix, diagonal):
    modes, depth = qt.shape
    local_subs, boundary, _ = matrix.shape
    chunk = modes // 4

    def kernel(t_ref, m_ref, d_ref, y_ref):
        for s in range(local_subs):
            span = slice(s * boundary, (s + 1) * boundary)
            left = t_ref[:, span]
            y = jnp.dot(left, m_ref[s], preferred_element_type=F32)
            y_ref[:, span] = (y + left.astype(F32) * d_ref[s]).astype(BF16)

    rows = pl.BlockSpec((chunk, depth), lambda i: (i, 0))
    return pl.pallas_call(
        kernel,
        grid=(modes // chunk,),
        in_specs=[rows, whole(local_subs, boundary, boundary), whole(local_subs, 1, boundary)],
        out_specs=rows,
        out_shape=jax.ShapeDtypeStruct((modes, depth), BF16),
        name="mix_mass",
    )(qt, matrix, diagonal)


def project_mass(mixed, qt, dims):
    modes, depth = qt.shape
    groups = dims[0] * dims[1] * dims[2]
    share = modes // (2 * groups)
    chunk = modes // 2

    def kernel(y_ref, t_ref, send_ref, keep_ref):
        out = lax.dot_general(
            y_ref[...], t_ref[...], (((1,), (1,)), ((), ())), preferred_element_type=F32
        )
        cut_shares(out, pl.program_id(0), send_ref, keep_ref, dims)

    return pl.pallas_call(
        kernel,
        grid=(modes // chunk,),
        in_specs=[pl.BlockSpec((chunk, depth), lambda i: (i, 0)), whole(modes, depth)],
        out_specs=[whole(groups, share, modes), whole(groups, share, modes)],
        out_shape=[
            jax.ShapeDtypeStruct((groups, share, modes), BF16),
            jax.ShapeDtypeStruct((groups, share, modes), F32),
        ],
        name="project_mass",
    )(mixed, qt)


def swap(value, offset, device_count):
    return lax.ppermute(value, AXES, [(i, i ^ offset) for i in range(device_count)])


def reduce_shares(send, keep, halving, sizes):
    got = swap(send, 1, sizes.devices)
    depth = sizes.devices // sizes.plane
    shape = (sizes.plane // 2, depth) + keep.shape[1:]
    keep, got = keep.reshape(shape), got.reshape(shape)
    summed = [keep[d] + got[d].astype(F32) for d in range(sizes.plane // 2)]
    total = summed[0]
    for d in range(1, sizes.plane // 2):
        got = swap(summed[d].astype(BF16), 2 * d, sizes.devices)
        total = total + got.astype(F32)
    if halving:
        while depth > 1:
            first = sizes.devices // sizes.plane // depth
            pairs = total.reshape((depth // 2, 2) + total.shape[1:])
            got = swap(pairs[:, 1].astype(BF16), first * sizes.plane, sizes.devices)
            total = pairs[:, 0] + got.astype(F32)
            depth //= 2
        return total[0]
    result = total[0]
    for d in range(1, depth):
        got = swap(total[d].astype(BF16), d * sizes.plane, sizes.devices)
        result = result + got.astype(F32)
    return result


def spread_in_plane(blocks, sizes):
    near = [blocks[0]]
    for d in range(1, sizes.plane):
        near.append(swap(blocks[d], d, sizes.devices))
    return [jnp.stack([part[z] for part in near]) for z in range(sizes.devices // sizes.plane)]


def clear_tiles(table, sizes):
    shape = (sizes.row_blocks * BLK, sizes.col_blocks * BLK)

    def kernel(_table, stiff_ref, mass_ref, zero_ref, sem):
        zero_ref[...] = jnp.zeros_like(zero_ref)
        fills = [
            pltpu.make_async_copy(zero_ref, ref.at[pl.ds(i * BLK, BLK), :], sem.at[i, j])
            for i in range(sizes.row_blocks)
            for j, ref in enumerate((stiff_ref, mass_ref))
        ]
        for fill in fills:
            fill.start()
        for fill in fills:
            fill.wait()

    return pl.pallas_call(
        kernel,
        in_specs=[ANY],
        out_specs=[ANY, ANY],
        out_shape=[jax.ShapeDtypeStruct(shape, BF16), jax.ShapeDtypeStruct(shape, BF16)],
        scratch_shapes=[
            pltpu.VMEM((BLK, shape[1]), BF16),
            pltpu.SemaphoreType.DMA((sizes.row_blocks, 2)),
        ],
        name="clear_tiles",
    )(table)


def place(table, order, slots, arrived, stiff_tile, mass_tile, sizes):
    count = sizes.devices
    limit = sizes.row_blocks * sizes.col_blocks
    depth = len(arrived)
    height = 2 * BLK + EXTRA

    def kernel(*refs):
        table_ref, order_ref, slot_ref = refs[:3]
        in_refs = refs[3 : 3 + depth]
        stiff_ref, mass_ref, share_ref, held_ref, sums_ref, in_sem, sem = refs[-7:]
        me = lax.axis_index("row") * sizes.cols + lax.axis_index("col")
        loads = [
            pltpu.make_async_copy(
                ref, held_ref.at[pl.ds(z * sizes.plane, sizes.plane)], in_sem.at[z]
            )
            for z, ref in enumerate(in_refs)
        ]
        for load in loads:
            load.start()
        for load in loads:
            load.wait()

        def copies(j):
            slot = slot_ref[j]
            row = pl.multiple_of(quotient(slot, sizes.col_blocks) * BLK, BLK)
            col = pl.multiple_of(remainder(slot, sizes.col_blocks) * BLK, BLK)
            return [
                pltpu.make_async_copy(
                    sums_ref.at[j, pl.ds(i * BLK, BLK)],
                    ref.at[pl.ds(row, BLK), pl.ds(col, BLK)],
                    sem.at[j, i],
                )
                for i, ref in enumerate((stiff_ref, mass_ref))
            ]

        def last(j):
            ahead = slot_ref[jnp.minimum(j + 1, count - 1)]
            ends = jnp.logical_or(j == count - 1, ahead != slot_ref[j])
            return jnp.logical_and(slot_ref[j] < limit, ends)

        def one(j, total):
            block = held_ref[order_ref[j] ^ me, : 2 * BLK].astype(F32)
            same = jnp.logical_and(j > 0, slot_ref[jnp.maximum(j - 1, 0)] == slot_ref[j])
            total = jnp.where(same, total + block, block)
            sums_ref[j] = total.astype(BF16)

            @pl.when(last(j))
            def _():
                for copy in copies(j):
                    copy.start()

            return total

        lax.fori_loop(0, count, one, jnp.zeros((2 * BLK, BLK), F32))
        share_ref[...] = jnp.zeros_like(share_ref)

        def add(device, carry):
            share = table_ref[device, sizes.ratio + 1]

            @pl.when(share >= 0)
            def _():
                parts = held_ref[device ^ me, 2 * BLK : 2 * BLK + EXTRA].astype(F32)
                share_ref[share] += parts[0:1] + parts[1:2] + parts[2:3]

            return carry

        lax.fori_loop(0, count, add, 0)

        def wait(j, carry):
            @pl.when(last(j))
            def _():
                for copy in copies(j):
                    copy.wait()

            return carry

        lax.fori_loop(0, count, wait, 0)

    return pl.pallas_call(
        kernel,
        in_specs=[SMEM, SMEM, SMEM] + [ANY] * (depth + 2),
        out_specs=[ANY, ANY, VMEM],
        out_shape=[
            jax.ShapeDtypeStruct(stiff_tile.shape, BF16),
            jax.ShapeDtypeStruct(mass_tile.shape, BF16),
            jax.ShapeDtypeStruct((sizes.share_blocks, 1, BLK), F32),
        ],
        input_output_aliases={3 + depth: 0, 4 + depth: 1},
        scratch_shapes=[
            pltpu.VMEM((count, height, BLK), BF16),
            pltpu.VMEM((count, 2 * BLK, BLK), BF16),
            pltpu.SemaphoreType.DMA((depth,)),
            pltpu.SemaphoreType.DMA((count, 2)),
        ],
        name="place",
    )(table, order, slots, *arrived, stiff_tile, mass_tile)


def reduction(inv_interior, coupling, boundary_stiff, mass_interior, mass_boundary, block_map, modes):
    row_count = lax.axis_size("row")
    col_count = lax.axis_size("col")
    tile_cols, width = modes.shape
    tile_rows = tile_cols * col_count // row_count
    sizes = Sizes(
        devices=row_count * col_count,
        cols=col_count,
        ratio=row_count // col_count,
        row_blocks=tile_rows // BLK,
        col_blocks=tile_cols // BLK,
        share_blocks=tile_rows // BLK // col_count,
        plane=col_count // 2 * col_count,
    )
    x_size = col_count // 2
    y_size = x_size
    dims = (row_count // y_size, y_size, x_size)

    table = exchange(describe(block_map, sizes))
    turned = jnp.swapaxes(modes.reshape(sizes.col_blocks, BLK, width), 1, 2)
    wanted = pick_modes(table, turned, sizes.ratio)
    fetched = exchange(wanted)
    stiff, mass, diagonal, *blocks = condense(
        block_map, inv_interior, coupling, boundary_stiff, mass_interior, mass_boundary, sizes
    )
    spread = spread_in_plane(blocks, sizes)
    beside = swap(spread[1], sizes.plane, sizes.devices)
    stiff_tile, mass_tile = clear_tiles(table, sizes)
    late, fetched, stiff_tile, mass_tile = lax.optimization_barrier(
        (spread[2:], fetched, stiff_tile, mass_tile)
    )
    late = [swap(part, (2 + d) * sizes.plane, sizes.devices) for d, part in enumerate(late)]
    arrived = [spread[0], beside, *late]

    fetched = fetched.reshape(row_count, col_count, sizes.ratio, width, BLK)
    send, keep, qt = project_stiff(block_map, fetched, stiff, dims, sizes.row_blocks)
    reduced_stiff = reduce_shares(send, keep, True, sizes)
    mixed = mix_mass(qt, mass, diagonal)
    send, keep = project_mass(mixed, qt, dims)
    reduced_mass = reduce_shares(send, keep, False, sizes)

    slot = table[:, sizes.ratio]
    ids = jnp.arange(sizes.devices, dtype=jnp.int32)
    before = jnp.logical_or(
        slot[None, :] < slot[:, None],
        jnp.logical_and(slot[None, :] == slot[:, None], ids[None, :] < ids[:, None]),
    )
    rank = jnp.sum(before.astype(jnp.int32), axis=1)
    chosen = rank[None, :] == ids[:, None]
    order = jnp.sum(jnp.where(chosen, ids[None, :], 0), axis=1)
    slots = jnp.sum(jnp.where(chosen, slot[None, :], 0), axis=1)
    stiff_tile, mass_tile, mass_share = place(
        table, order, slots, arrived, stiff_tile, mass_tile, sizes
    )
    return stiff_tile, mass_tile, reduced_stiff, reduced_mass, mass_share.reshape(-1)


def solution(mesh):
    return jax.shard_map(
        reduction,
        mesh=mesh,
        in_specs=(
            P(AXES, None, None),
            P(AXES, None, None),
            P(AXES, None, None),
            P(AXES, None),
            P(AXES, None),
            P(AXES, None),
            P("col", "row"),
        ),
        out_specs=(P("row", "col"), P("row", "col"), P(AXES, None), P(AXES, None), P(AXES)),
        check_vma=False,
    )
```

```python
from typing import NamedTuple

import jax
import jax.numpy as jnp
from jax import lax
from jax.experimental import pallas as pl
from jax.experimental.pallas import tpu as pltpu
from jax.sharding import PartitionSpec as P


BLK = 128
EXTRA = 8
AXES = ("row", "col")
F32 = jnp.float32
BF16 = jnp.bfloat16
VMEM = pl.BlockSpec(memory_space=pltpu.VMEM)
SMEM = pl.BlockSpec(memory_space=pltpu.SMEM)
ANY = pl.BlockSpec(memory_space=pl.ANY)


class Sizes(NamedTuple):
    devices: int
    cols: int
    ratio: int
    row_blocks: int
    col_blocks: int
    share_blocks: int
    plane: int


def exchange(value):
    return lax.all_to_all(value, AXES, split_axis=0, concat_axis=0, tiled=True)


def quotient(value, size):
    return lax.shift_right_logical(value, jnp.int32(size.bit_length() - 1))


def remainder(value, size):
    return value & jnp.int32(size - 1)


def describe(block_map, sizes):
    local_subs, per_sub = block_map.shape

    def kernel(map_ref, out_ref):
        shape = out_ref.shape
        device = lax.broadcasted_iota(jnp.int32, shape, 0)
        field = lax.broadcasted_iota(jnp.int32, shape, 1)
        row = quotient(device, sizes.cols)
        col = remainder(device, sizes.cols)
        zero = jnp.zeros(shape, jnp.int32)
        wanted, share = zero, zero - 1
        slot = zero + sizes.row_blocks * sizes.col_blocks
        for s in range(local_subs):
            row_slot, col_slot = zero - 1, zero - 1
            for a in range(per_sub):
                block = map_ref[s, a]
                tile_row = quotient(block, sizes.row_blocks)
                wanted = jnp.where(
                    col * sizes.ratio + field == tile_row, remainder(block, sizes.col_blocks), wanted
                )
                share = jnp.where(
                    device == quotient(block, sizes.share_blocks),
                    remainder(block, sizes.share_blocks),
                    share,
                )
                row_slot = jnp.where(row == tile_row, remainder(block, sizes.row_blocks), row_slot)
                col_slot = jnp.where(
                    col == quotient(block, sizes.col_blocks),
                    remainder(block, sizes.col_blocks),
                    col_slot,
                )
            both = jnp.logical_and(row_slot >= 0, col_slot >= 0)
            slot = jnp.where(both, row_slot * sizes.col_blocks + col_slot, slot)
        out_ref[...] = jnp.where(
            field < sizes.ratio, wanted, jnp.where(field == sizes.ratio, slot, share)
        )

    return pl.pallas_call(
        kernel,
        out_shape=jax.ShapeDtypeStruct((sizes.devices, BLK), jnp.int32),
        in_specs=[SMEM],
        out_specs=VMEM,
        name="describe",
    )(block_map)


def pick_modes(table, modes, ratio):
    device_count = table.shape[0]
    width = modes.shape[1]

    def kernel(table_ref, modes_ref, out_ref):
        def one(device, carry):
            for h in range(ratio):
                out_ref[device, h] = modes_ref[table_ref[device, h]]
            return carry

        lax.fori_loop(0, device_count, one, 0, unroll=4)

    return pl.pallas_call(
        kernel,
        out_shape=jax.ShapeDtypeStruct((device_count, ratio, width, BLK), BF16),
        in_specs=[SMEM, VMEM],
        out_specs=VMEM,
        name="pick_modes",
    )(table, modes)


def condense(
    block_map, inv_interior, coupling, boundary_stiff, mass_interior, mass_boundary, sizes
):
    local_subs, interior, boundary = coupling.shape
    per_sub = boundary // BLK

    def kernel(
        map_ref,
        inv_ref,
        cpl_ref,
        stiff_ref,
        mi_ref,
        mb_ref,
        k_ref,
        m_ref,
        d_ref,
        *refs,
    ):
        near_refs, out_ref, sem = refs[: sizes.plane], refs[-2], refs[-1]
        sub = pl.program_id(0)
        me = lax.axis_index("row") * sizes.cols + lax.axis_index("col")
        couple = cpl_ref[0]
        static_modes = (-jnp.dot(inv_ref[0], couple, preferred_element_type=F32)).astype(BF16)
        contract = (((0,), (0,)), ((), ()))
        stiff = stiff_ref[0].astype(F32) + lax.dot_general(
            couple, static_modes, contract, preferred_element_type=F32
        )
        eye = lax.broadcasted_iota(jnp.int32, (BLK, BLK), 0) == lax.broadcasted_iota(
            jnp.int32, (BLK, BLK), 1
        )

        def own_row(ref):
            mine = lax.broadcasted_iota(jnp.int32, ref.shape, 0) == sub
            return jnp.sum(jnp.where(mine, ref[...], 0.0), axis=0, keepdims=True)

        masses, boundary_masses = own_row(mi_ref), own_row(mb_ref)
        column = jnp.concatenate(
            [
                jnp.sum(jnp.where(eye, masses[:, i : i + BLK], 0.0), axis=1, keepdims=True)
                for i in range(0, interior, BLK)
            ],
            axis=0,
        )
        weighted = (static_modes.astype(F32) * column).astype(BF16)
        mass = lax.dot_general(static_modes, weighted, contract, preferred_element_type=F32)
        level = lax.broadcasted_iota(jnp.int32, (EXTRA, BLK), 0)
        for a in range(per_sub):
            block_a = map_ref[sub, a]
            rows = slice(a * BLK, (a + 1) * BLK)
            for b in range(per_sub):
                cols = slice(b * BLK, (b + 1) * BLK)
                owner = quotient(block_a, sizes.row_blocks) * sizes.cols + quotient(
                    map_ref[sub, b], sizes.col_blocks
                )
                owner = owner ^ me
                near, far = remainder(owner, sizes.plane), quotient(owner, sizes.plane)
                stiff_block = stiff[rows, cols].astype(BF16)
                mass_block = mass[rows, cols]
                if a == b:
                    diagonal = (
                        jnp.sum(jnp.where(eye, mass_block, 0.0), axis=0, keepdims=True)
                        + boundary_masses[:, cols]
                    )
                    d_ref[0, :, cols] = diagonal
                    high = diagonal.astype(BF16).astype(F32)
                    middle = (diagonal - high).astype(BF16).astype(F32)
                    low = diagonal - high - middle
                    parts = jnp.where(level == 0, high, jnp.where(level == 1, middle, low))
                    share = quotient(block_a, sizes.share_blocks) ^ me
                    out_ref[
                        remainder(share, sizes.plane),
                        quotient(share, sizes.plane),
                        2 * BLK : 2 * BLK + EXTRA,
                    ] = parts.astype(BF16)
                    mass_block = jnp.where(eye, 0.0, mass_block)
                mass_block = mass_block.astype(BF16)
                out_ref[near, far, :BLK] = stiff_block
                out_ref[near, far, BLK : 2 * BLK] = mass_block
                k_ref[0, rows, cols] = stiff_block
                m_ref[0, rows, cols] = mass_block

        @pl.when(sub == local_subs - 1)
        def _():
            copies = [
                pltpu.make_async_copy(out_ref.at[d], ref, sem.at[d])
                for d, ref in enumerate(near_refs)
            ]
            for copy in copies:
                copy.start()
            for copy in copies:
                copy.wait()

    def piece(*shape):
        return pl.BlockSpec((1,) + shape, lambda s: (s, 0, 0))

    out_blocks = (sizes.devices // sizes.plane, 2 * BLK + EXTRA, BLK)
    return pl.pallas_call(
        kernel,
        grid=(local_subs,),
        in_specs=[
            SMEM,
            piece(interior, interior),
            piece(interior, boundary),
            piece(boundary, boundary),
            pl.BlockSpec((local_subs, interior), lambda s: (0, 0)),
            pl.BlockSpec((local_subs, boundary), lambda s: (0, 0)),
        ],
        out_specs=[
            piece(boundary, boundary),
            piece(boundary, boundary),
            piece(1, boundary),
        ]
        + [ANY] * sizes.plane,
        out_shape=[
            jax.ShapeDtypeStruct((local_subs, boundary, boundary), BF16),
            jax.ShapeDtypeStruct((local_subs, boundary, boundary), BF16),
            jax.ShapeDtypeStruct((local_subs, 1, boundary), F32),
        ]
        + [jax.ShapeDtypeStruct(out_blocks, BF16)] * sizes.plane,
        scratch_shapes=[
            pltpu.VMEM((sizes.plane,) + out_blocks, BF16),
            pltpu.SemaphoreType.DMA((sizes.plane,)),
        ],
        name="condense",
    )(
        block_map,
        inv_interior,
        coupling,
        boundary_stiff,
        mass_interior,
        mass_boundary,
    )


def cut_shares(out, step, steps, held, results, sem, dims):
    z_size, y_size, x_size = dims
    groups, share, _ = results[0].shape
    pairs = out.shape[0] // (2 * share)
    row, col = lax.axis_index("row"), lax.axis_index("col")
    my_z, my_y = quotient(row, y_size), remainder(row, y_size)
    my_x, mine = quotient(col, 2), remainder(col, 2) == 0

    def copies(slot):
        return [
            pltpu.make_async_copy(ref.at[slot], result.at[slot], sem.at[i, slot])
            for i, (ref, result) in enumerate(zip(held, results))
        ]

    for i in range(pairs):
        group = step * pairs + i
        x = remainder(group, x_size)
        y = remainder(quotient(group, x_size), y_size)
        z = quotient(group, x_size * y_size)
        slot = ((y ^ my_y) * x_size + (x ^ my_x)) * z_size + (z ^ my_z)
        even = out[2 * i * share : (2 * i + 1) * share]
        odd = out[(2 * i + 1) * share : (2 * i + 2) * share]
        held[0][slot] = jnp.where(mine, odd, even).astype(BF16)
        held[1][slot] = jnp.where(mine, even, odd)
        for copy in copies(slot):
            copy.start()

    @pl.when(step == steps - 1)
    def _():
        for slot in range(groups):
            for copy in copies(slot):
                copy.wait()


def whole(*shape):
    return pl.BlockSpec(shape, lambda i: (0,) * len(shape))


def project_stiff(block_map, fetched, matrix, dims, row_blocks):
    local_subs, boundary, _ = matrix.shape
    depth = local_subs * boundary
    per_sub = boundary // BLK
    groups = dims[0] * dims[1] * dims[2]
    row_count, _, ratio, width, _ = fetched.shape
    modes = row_count * width
    share = modes // (2 * groups)
    chunk = modes // 2

    def kernel(
        map_ref, in_ref, m_ref, send_ref, keep_ref, qt_ref, t_ref, y_ref, s_ref, k_ref, t_sem, sem
    ):
        step = pl.program_id(0)
        copy_out = pltpu.make_async_copy(t_ref, qt_ref, t_sem.at[0])

        @pl.when(step == 0)
        def _():
            for s in range(local_subs):
                for a in range(per_sub):
                    tile_row = quotient(map_ref[s, a], row_blocks)
                    c = quotient(tile_row, ratio)
                    h = remainder(tile_row, ratio)
                    k = (s * per_sub + a) * BLK
                    for r in range(row_count):
                        t_ref[r * width : (r + 1) * width, k : k + BLK] = in_ref[r, c, h]
            copy_out.start()

        rows = pl.ds(pl.multiple_of(step * chunk, chunk), chunk)
        for s in range(local_subs):
            span = slice(s * boundary, (s + 1) * boundary)
            y_ref[:, span] = jnp.dot(
                t_ref[rows, span], m_ref[s], preferred_element_type=F32
            ).astype(BF16)
        out = lax.dot_general(
            y_ref[...], t_ref[...], (((1,), (1,)), ((), ())), preferred_element_type=F32
        )
        cut_shares(out, step, 2, (s_ref, k_ref), (send_ref, keep_ref), sem, dims)

        @pl.when(step == 1)
        def _():
            copy_out.wait()

    return pl.pallas_call(
        kernel,
        grid=(2,),
        in_specs=[SMEM, whole(*fetched.shape), whole(local_subs, boundary, boundary)],
        out_specs=[ANY, ANY, ANY],
        out_shape=[
            jax.ShapeDtypeStruct((groups, share, modes), BF16),
            jax.ShapeDtypeStruct((groups, share, modes), F32),
            jax.ShapeDtypeStruct((modes, depth), BF16),
        ],
        scratch_shapes=[
            pltpu.VMEM((modes, depth), BF16),
            pltpu.VMEM((chunk, depth), BF16),
            pltpu.VMEM((groups, share, modes), BF16),
            pltpu.VMEM((groups, share, modes), F32),
            pltpu.SemaphoreType.DMA((1,)),
            pltpu.SemaphoreType.DMA((2, groups)),
        ],
        name="project_stiff",
    )(block_map, fetched, matrix)


def mix_mass(qt, matrix, diagonal):
    modes, depth = qt.shape
    local_subs, boundary, _ = matrix.shape
    chunk = modes // 4

    def kernel(t_ref, m_ref, d_ref, y_ref):
        for s in range(local_subs):
            span = slice(s * boundary, (s + 1) * boundary)
            left = t_ref[:, span]
            y = jnp.dot(left, m_ref[s], preferred_element_type=F32)
            y_ref[:, span] = (y + left.astype(F32) * d_ref[s]).astype(BF16)

    rows = pl.BlockSpec((chunk, depth), lambda i: (i, 0))
    return pl.pallas_call(
        kernel,
        grid=(modes // chunk,),
        in_specs=[rows, whole(local_subs, boundary, boundary), whole(local_subs, 1, boundary)],
        out_specs=rows,
        out_shape=jax.ShapeDtypeStruct((modes, depth), BF16),
        name="mix_mass",
    )(qt, matrix, diagonal)


def project_mass(mixed, qt, dims):
    modes, depth = qt.shape
    groups = dims[0] * dims[1] * dims[2]
    share = modes // (2 * groups)
    chunk = modes // 2

    def kernel(y_ref, t_ref, send_ref, keep_ref, s_ref, k_ref, sem):
        out = lax.dot_general(
            y_ref[...], t_ref[...], (((1,), (1,)), ((), ())), preferred_element_type=F32
        )
        cut_shares(out, pl.program_id(0), 2, (s_ref, k_ref), (send_ref, keep_ref), sem, dims)

    return pl.pallas_call(
        kernel,
        grid=(2,),
        in_specs=[pl.BlockSpec((chunk, depth), lambda i: (i, 0)), whole(modes, depth)],
        out_specs=[ANY, ANY],
        out_shape=[
            jax.ShapeDtypeStruct((groups, share, modes), BF16),
            jax.ShapeDtypeStruct((groups, share, modes), F32),
        ],
        scratch_shapes=[
            pltpu.VMEM((groups, share, modes), BF16),
            pltpu.VMEM((groups, share, modes), F32),
            pltpu.SemaphoreType.DMA((2, groups)),
        ],
        name="project_mass",
    )(mixed, qt)


def swap(value, offset, device_count):
    return lax.ppermute(value, AXES, [(i, i ^ offset) for i in range(device_count)])


def reduce_shares(send, keep, sizes):
    got = swap(send, 1, sizes.devices)
    depth = sizes.devices // sizes.plane
    shape = (sizes.plane // 2, depth) + keep.shape[1:]
    keep, got = keep.reshape(shape), got.reshape(shape)
    summed = [keep[d] + got[d].astype(F32) for d in range(sizes.plane // 2)]
    total = summed[0]
    for d in range(1, sizes.plane // 2):
        got = swap(summed[d].astype(BF16), 2 * d, sizes.devices)
        total = total + got.astype(F32)
    result = total[0]
    for d in range(1, depth):
        got = swap(total[d].astype(BF16), d * sizes.plane, sizes.devices)
        result = result + got.astype(F32)
    return result


def spread_in_plane(blocks, sizes):
    near = [blocks[0]]
    for d in range(1, sizes.plane):
        near.append(swap(blocks[d], d, sizes.devices))
    return [jnp.stack([part[z] for part in near]) for z in range(sizes.devices // sizes.plane)]


def clear_tiles(table, sizes):
    shape = (sizes.row_blocks * BLK, sizes.col_blocks * BLK)

    def kernel(_table, stiff_ref, mass_ref, zero_ref, sem):
        zero_ref[...] = jnp.zeros_like(zero_ref)
        fills = [
            pltpu.make_async_copy(zero_ref, ref.at[pl.ds(i * BLK, BLK), :], sem.at[i, j])
            for i in range(sizes.row_blocks)
            for j, ref in enumerate((stiff_ref, mass_ref))
        ]
        for fill in fills:
            fill.start()
        for fill in fills:
            fill.wait()

    return pl.pallas_call(
        kernel,
        in_specs=[ANY],
        out_specs=[ANY, ANY],
        out_shape=[jax.ShapeDtypeStruct(shape, BF16), jax.ShapeDtypeStruct(shape, BF16)],
        scratch_shapes=[
            pltpu.VMEM((BLK, shape[1]), BF16),
            pltpu.SemaphoreType.DMA((sizes.row_blocks, 2)),
        ],
        name="clear_tiles",
    )(table)


def place(table, order, slots, arrived, stiff_tile, mass_tile, sizes):
    count = sizes.devices
    limit = sizes.row_blocks * sizes.col_blocks
    depth = len(arrived)
    height = 2 * BLK + EXTRA

    def kernel(*refs):
        table_ref, order_ref, slot_ref = refs[:3]
        in_refs = refs[3 : 3 + depth]
        stiff_ref, mass_ref, share_ref, held_ref, sums_ref, in_sem, sem = refs[-7:]
        me = lax.axis_index("row") * sizes.cols + lax.axis_index("col")
        loads = [
            pltpu.make_async_copy(
                ref, held_ref.at[pl.ds(z * sizes.plane, sizes.plane)], in_sem.at[z]
            )
            for z, ref in enumerate(in_refs)
        ]
        for load in loads:
            load.start()
        for load in loads:
            load.wait()

        def copies(j):
            slot = slot_ref[j]
            row = pl.multiple_of(quotient(slot, sizes.col_blocks) * BLK, BLK)
            col = pl.multiple_of(remainder(slot, sizes.col_blocks) * BLK, BLK)
            return [
                pltpu.make_async_copy(
                    sums_ref.at[j, pl.ds(i * BLK, BLK)],
                    ref.at[pl.ds(row, BLK), pl.ds(col, BLK)],
                    sem.at[j, i],
                )
                for i, ref in enumerate((stiff_ref, mass_ref))
            ]

        def last(j):
            ahead = slot_ref[jnp.minimum(j + 1, count - 1)]
            ends = jnp.logical_or(j == count - 1, ahead != slot_ref[j])
            return jnp.logical_and(slot_ref[j] < limit, ends)

        def one(j, total):
            block = held_ref[order_ref[j] ^ me, : 2 * BLK].astype(F32)
            same = jnp.logical_and(j > 0, slot_ref[jnp.maximum(j - 1, 0)] == slot_ref[j])
            total = jnp.where(same, total + block, block)
            sums_ref[j] = total.astype(BF16)

            @pl.when(last(j))
            def _():
                for copy in copies(j):
                    copy.start()

            return total

        lax.fori_loop(0, count, one, jnp.zeros((2 * BLK, BLK), F32))
        share_ref[...] = jnp.zeros_like(share_ref)

        def add(device, carry):
            share = table_ref[device, sizes.ratio + 1]

            @pl.when(share >= 0)
            def _():
                parts = held_ref[device ^ me, 2 * BLK : 2 * BLK + EXTRA].astype(F32)
                share_ref[share] += parts[0:1] + parts[1:2] + parts[2:3]

            return carry

        lax.fori_loop(0, count, add, 0)

        def wait(j, carry):
            @pl.when(last(j))
            def _():
                for copy in copies(j):
                    copy.wait()

            return carry

        lax.fori_loop(0, count, wait, 0)

    return pl.pallas_call(
        kernel,
        in_specs=[SMEM, SMEM, SMEM] + [ANY] * (depth + 2),
        out_specs=[ANY, ANY, VMEM],
        out_shape=[
            jax.ShapeDtypeStruct(stiff_tile.shape, BF16),
            jax.ShapeDtypeStruct(mass_tile.shape, BF16),
            jax.ShapeDtypeStruct((sizes.share_blocks, 1, BLK), F32),
        ],
        input_output_aliases={3 + depth: 0, 4 + depth: 1},
        scratch_shapes=[
            pltpu.VMEM((count, height, BLK), BF16),
            pltpu.VMEM((count, 2 * BLK, BLK), BF16),
            pltpu.SemaphoreType.DMA((depth,)),
            pltpu.SemaphoreType.DMA((count, 2)),
        ],
        name="place",
    )(table, order, slots, *arrived, stiff_tile, mass_tile)


def reduction(inv_interior, coupling, boundary_stiff, mass_interior, mass_boundary, block_map, modes):
    row_count = lax.axis_size("row")
    col_count = lax.axis_size("col")
    tile_cols, width = modes.shape
    tile_rows = tile_cols * col_count // row_count
    sizes = Sizes(
        devices=row_count * col_count,
        cols=col_count,
        ratio=row_count // col_count,
        row_blocks=tile_rows // BLK,
        col_blocks=tile_cols // BLK,
        share_blocks=tile_rows // BLK // col_count,
        plane=col_count // 2 * col_count,
    )
    x_size = col_count // 2
    y_size = x_size
    dims = (row_count // y_size, y_size, x_size)

    table = exchange(describe(block_map, sizes))
    turned = jnp.swapaxes(modes.reshape(sizes.col_blocks, BLK, width), 1, 2)
    wanted = pick_modes(table, turned, sizes.ratio)
    fetched = exchange(wanted)
    stiff, mass, diagonal, *blocks = condense(
        block_map, inv_interior, coupling, boundary_stiff, mass_interior, mass_boundary, sizes
    )
    spread = spread_in_plane(blocks, sizes)
    beside = swap(spread[1], sizes.plane, sizes.devices)
    stiff_tile, mass_tile = clear_tiles(table, sizes)
    late, fetched, stiff_tile, mass_tile = lax.optimization_barrier(
        (spread[2:], fetched, stiff_tile, mass_tile)
    )
    late = [swap(part, (2 + d) * sizes.plane, sizes.devices) for d, part in enumerate(late)]
    arrived = [spread[0], beside, *late]

    fetched = fetched.reshape(row_count, col_count, sizes.ratio, width, BLK)
    send, keep, qt = project_stiff(block_map, fetched, stiff, dims, sizes.row_blocks)
    reduced_stiff = reduce_shares(send, keep, sizes)
    mixed = mix_mass(qt, mass, diagonal)
    send, keep = project_mass(mixed, qt, dims)
    reduced_mass = reduce_shares(send, keep, sizes)

    slot = table[:, sizes.ratio]
    ids = jnp.arange(sizes.devices, dtype=jnp.int32)
    before = jnp.logical_or(
        slot[None, :] < slot[:, None],
        jnp.logical_and(slot[None, :] == slot[:, None], ids[None, :] < ids[:, None]),
    )
    rank = jnp.sum(before.astype(jnp.int32), axis=1)
    chosen = rank[None, :] == ids[:, None]
    order = jnp.sum(jnp.where(chosen, ids[None, :], 0), axis=1)
    slots = jnp.sum(jnp.where(chosen, slot[None, :], 0), axis=1)
    stiff_tile, mass_tile, mass_share = place(
        table, order, slots, arrived, stiff_tile, mass_tile, sizes
    )
    return stiff_tile, mass_tile, reduced_stiff, reduced_mass, mass_share.reshape(-1)


def solution(mesh):
    return jax.shard_map(
        reduction,
        mesh=mesh,
        in_specs=(
            P(AXES, None, None),
            P(AXES, None, None),
            P(AXES, None, None),
            P(AXES, None),
            P(AXES, None),
            P(AXES, None),
            P("col", "row"),
        ),
        out_specs=(P("row", "col"), P("row", "col"), P(AXES, None), P(AXES, None), P(AXES)),
        check_vma=False,
    )
```

```python
from typing import NamedTuple

import jax
import jax.numpy as jnp
from jax import lax
from jax.experimental import pallas as pl
from jax.experimental.pallas import tpu as pltpu
from jax.sharding import PartitionSpec as P


BLK = 128
EXTRA = 8
CHIP = 2
AXES = ("row", "col")
F32 = jnp.float32
BF16 = jnp.bfloat16
VMEM = pl.BlockSpec(memory_space=pltpu.VMEM)
SMEM = pl.BlockSpec(memory_space=pltpu.SMEM)
ANY = pl.BlockSpec(memory_space=pl.ANY)


class Sizes(NamedTuple):
    devices: int
    cols: int
    ratio: int
    row_blocks: int
    col_blocks: int
    share_blocks: int
    plane: int


def exchange(value):
    return lax.all_to_all(value, AXES, split_axis=0, concat_axis=0, tiled=True)


def quotient(value, size):
    return lax.shift_right_logical(value, jnp.int32(size.bit_length() - 1))


def remainder(value, size):
    return value & jnp.int32(size - 1)


def describe(block_map, sizes):
    local_subs, per_sub = block_map.shape

    def kernel(map_ref, out_ref):
        shape = out_ref.shape
        device = lax.broadcasted_iota(jnp.int32, shape, 0)
        field = lax.broadcasted_iota(jnp.int32, shape, 1)
        row = quotient(device, sizes.cols)
        col = remainder(device, sizes.cols)
        zero = jnp.zeros(shape, jnp.int32)
        wanted, share = zero, zero - 1
        slot = zero + sizes.row_blocks * sizes.col_blocks
        for s in range(local_subs):
            row_slot, col_slot = zero - 1, zero - 1
            for a in range(per_sub):
                block = map_ref[s, a]
                tile_row = quotient(block, sizes.row_blocks)
                wanted = jnp.where(
                    col * sizes.ratio + field == tile_row, remainder(block, sizes.col_blocks), wanted
                )
                share = jnp.where(
                    device == quotient(block, sizes.share_blocks),
                    remainder(block, sizes.share_blocks),
                    share,
                )
                row_slot = jnp.where(row == tile_row, remainder(block, sizes.row_blocks), row_slot)
                col_slot = jnp.where(
                    col == quotient(block, sizes.col_blocks),
                    remainder(block, sizes.col_blocks),
                    col_slot,
                )
            both = jnp.logical_and(row_slot >= 0, col_slot >= 0)
            slot = jnp.where(both, row_slot * sizes.col_blocks + col_slot, slot)
        out_ref[...] = jnp.where(
            field < sizes.ratio, wanted, jnp.where(field == sizes.ratio, slot, share)
        )

    return pl.pallas_call(
        kernel,
        out_shape=jax.ShapeDtypeStruct((sizes.devices, BLK), jnp.int32),
        in_specs=[SMEM],
        out_specs=VMEM,
        name="describe",
    )(block_map)


def pick_modes(table, modes, ratio):
    device_count = table.shape[0]
    width = modes.shape[1]

    def kernel(table_ref, modes_ref, out_ref, sem):
        def copy(device, h):
            return pltpu.make_async_copy(
                modes_ref.at[table_ref[device, h]], out_ref.at[device, h], sem.at[device, h]
            )

        def start(device, carry):
            for h in range(ratio):
                copy(device, h).start()
            return carry

        def wait(device, carry):
            for h in range(ratio):
                copy(device, h).wait()
            return carry

        lax.fori_loop(0, device_count, start, 0, unroll=4)
        lax.fori_loop(0, device_count, wait, 0, unroll=4)

    return pl.pallas_call(
        kernel,
        out_shape=jax.ShapeDtypeStruct((device_count, ratio, width, BLK), BF16),
        in_specs=[SMEM, ANY],
        out_specs=ANY,
        scratch_shapes=[pltpu.SemaphoreType.DMA((device_count, ratio))],
        name="pick_modes",
    )(table, modes)


def condense(
    block_map, inv_interior, coupling, boundary_stiff, mass_interior, mass_boundary, sizes
):
    local_subs, interior, boundary = coupling.shape
    per_sub = boundary // BLK

    def kernel(
        map_ref,
        inv_ref,
        cpl_ref,
        stiff_ref,
        mi_ref,
        mb_ref,
        k_ref,
        m_ref,
        d_ref,
        *refs,
    ):
        near_refs, out_ref, sem = refs[: sizes.plane], refs[-2], refs[-1]
        sub = pl.program_id(0)
        me = lax.axis_index("row") * sizes.cols + lax.axis_index("col")
        couple = cpl_ref[0]
        static_modes = (-jnp.dot(inv_ref[0], couple, preferred_element_type=F32)).astype(BF16)
        contract = (((0,), (0,)), ((), ()))
        stiff = stiff_ref[0].astype(F32) + lax.dot_general(
            couple, static_modes, contract, preferred_element_type=F32
        )
        eye = lax.broadcasted_iota(jnp.int32, (BLK, BLK), 0) == lax.broadcasted_iota(
            jnp.int32, (BLK, BLK), 1
        )

        def own_row(ref):
            mine = lax.broadcasted_iota(jnp.int32, ref.shape, 0) == sub
            return jnp.sum(jnp.where(mine, ref[...], 0.0), axis=0, keepdims=True)

        masses, boundary_masses = own_row(mi_ref), own_row(mb_ref)
        column = jnp.concatenate(
            [
                jnp.sum(jnp.where(eye, masses[:, i : i + BLK], 0.0), axis=1, keepdims=True)
                for i in range(0, interior, BLK)
            ],
            axis=0,
        )
        weighted = (static_modes.astype(F32) * column).astype(BF16)
        mass = lax.dot_general(static_modes, weighted, contract, preferred_element_type=F32)
        level = lax.broadcasted_iota(jnp.int32, (EXTRA, BLK), 0)
        for a in range(per_sub):
            block_a = map_ref[sub, a]
            rows = slice(a * BLK, (a + 1) * BLK)
            for b in range(per_sub):
                cols = slice(b * BLK, (b + 1) * BLK)
                owner = quotient(block_a, sizes.row_blocks) * sizes.cols + quotient(
                    map_ref[sub, b], sizes.col_blocks
                )
                owner = owner ^ me
                near, far = remainder(owner, sizes.plane), quotient(owner, sizes.plane)
                stiff_block = stiff[rows, cols].astype(BF16)
                mass_block = mass[rows, cols]
                if a == b:
                    diagonal = (
                        jnp.sum(jnp.where(eye, mass_block, 0.0), axis=0, keepdims=True)
                        + boundary_masses[:, cols]
                    )
                    d_ref[0, :, cols] = diagonal
                    high = diagonal.astype(BF16).astype(F32)
                    middle = (diagonal - high).astype(BF16).astype(F32)
                    low = diagonal - high - middle
                    parts = jnp.where(level == 0, high, jnp.where(level == 1, middle, low))
                    share = quotient(block_a, sizes.share_blocks) ^ me
                    out_ref[
                        remainder(share, sizes.plane),
                        quotient(share, sizes.plane),
                        2 * BLK : 2 * BLK + EXTRA,
                    ] = parts.astype(BF16)
                    mass_block = jnp.where(eye, 0.0, mass_block)
                mass_block = mass_block.astype(BF16)
                out_ref[near, far, :BLK] = stiff_block
                out_ref[near, far, BLK : 2 * BLK] = mass_block
                k_ref[0, rows, cols] = stiff_block
                m_ref[0, rows, cols] = mass_block

        @pl.when(sub == local_subs - 1)
        def _():
            copies = [
                pltpu.make_async_copy(out_ref.at[d], ref, sem.at[d])
                for d, ref in enumerate(near_refs)
            ]
            for copy in copies:
                copy.start()
            for copy in copies:
                copy.wait()

    def piece(*shape):
        return pl.BlockSpec((1,) + shape, lambda s: (s, 0, 0))

    out_blocks = (sizes.devices // sizes.plane, 2 * BLK + EXTRA, BLK)
    return pl.pallas_call(
        kernel,
        grid=(local_subs,),
        in_specs=[
            SMEM,
            piece(interior, interior),
            piece(interior, boundary),
            piece(boundary, boundary),
            pl.BlockSpec((local_subs, interior), lambda s: (0, 0)),
            pl.BlockSpec((local_subs, boundary), lambda s: (0, 0)),
        ],
        out_specs=[
            piece(boundary, boundary),
            piece(boundary, boundary),
            piece(1, boundary),
        ]
        + [ANY] * sizes.plane,
        out_shape=[
            jax.ShapeDtypeStruct((local_subs, boundary, boundary), BF16),
            jax.ShapeDtypeStruct((local_subs, boundary, boundary), BF16),
            jax.ShapeDtypeStruct((local_subs, 1, boundary), F32),
        ]
        + [jax.ShapeDtypeStruct(out_blocks, BF16)] * sizes.plane,
        scratch_shapes=[
            pltpu.VMEM((sizes.plane,) + out_blocks, BF16),
            pltpu.SemaphoreType.DMA((sizes.plane,)),
        ],
        name="condense",
    )(
        block_map,
        inv_interior,
        coupling,
        boundary_stiff,
        mass_interior,
        mass_boundary,
    )


def cut_shares(out, step, steps, held, results, sem, dims):
    z_size, y_size, x_size = dims
    groups, share, _ = results[0].shape
    pairs = out.shape[0] // (2 * share)
    row, col = lax.axis_index("row"), lax.axis_index("col")
    my_z, my_y = quotient(row, y_size), remainder(row, y_size)
    my_x, mine = quotient(col, 2), remainder(col, 2) == 0

    def copies(slot):
        return [
            pltpu.make_async_copy(ref.at[slot], result.at[slot], sem.at[i, slot])
            for i, (ref, result) in enumerate(zip(held, results))
        ]

    for i in range(pairs):
        group = step * pairs + i
        x = remainder(group, x_size)
        y = remainder(quotient(group, x_size), y_size)
        z = quotient(group, x_size * y_size)
        slot = ((y ^ my_y) * x_size + (x ^ my_x)) * z_size + (z ^ my_z)
        even = out[2 * i * share : (2 * i + 1) * share]
        odd = out[(2 * i + 1) * share : (2 * i + 2) * share]
        held[0][slot] = jnp.where(mine, odd, even).astype(BF16)
        held[1][slot] = jnp.where(mine, even, odd)
        for copy in copies(slot):
            copy.start()

    @pl.when(step == steps - 1)
    def _():
        for slot in range(groups):
            for copy in copies(slot):
                copy.wait()


def whole(*shape):
    return pl.BlockSpec(shape, lambda i: (0,) * len(shape))


def project_stiff(block_map, fetched, matrix, dims, row_blocks):
    local_subs, boundary, _ = matrix.shape
    depth = local_subs * boundary
    per_sub = boundary // BLK
    groups = dims[0] * dims[1] * dims[2]
    row_count, _, ratio, width, _ = fetched.shape
    modes = row_count * width
    share = modes // (2 * groups)
    chunk = modes // 2

    def kernel(
        map_ref, in_ref, m_ref, send_ref, keep_ref, qt_ref, t_ref, y_ref, s_ref, k_ref, t_sem, sem
    ):
        step = pl.program_id(0)
        copy_out = pltpu.make_async_copy(t_ref, qt_ref, t_sem.at[0])

        @pl.when(step == 0)
        def _():
            for s in range(local_subs):
                for a in range(per_sub):
                    tile_row = quotient(map_ref[s, a], row_blocks)
                    c = quotient(tile_row, ratio)
                    h = remainder(tile_row, ratio)
                    k = (s * per_sub + a) * BLK
                    for r in range(row_count):
                        t_ref[r * width : (r + 1) * width, k : k + BLK] = in_ref[r, c, h]
            copy_out.start()

        rows = pl.ds(pl.multiple_of(step * chunk, chunk), chunk)
        for s in range(local_subs):
            span = slice(s * boundary, (s + 1) * boundary)
            y_ref[:, span] = jnp.dot(
                t_ref[rows, span], m_ref[s], preferred_element_type=F32
            ).astype(BF16)
        out = lax.dot_general(
            y_ref[...], t_ref[...], (((1,), (1,)), ((), ())), preferred_element_type=F32
        )
        cut_shares(out, step, 2, (s_ref, k_ref), (send_ref, keep_ref), sem, dims)

        @pl.when(step == 1)
        def _():
            copy_out.wait()

    return pl.pallas_call(
        kernel,
        grid=(2,),
        in_specs=[SMEM, whole(*fetched.shape), whole(local_subs, boundary, boundary)],
        out_specs=[ANY, ANY, ANY],
        out_shape=[
            jax.ShapeDtypeStruct((groups, share, modes), BF16),
            jax.ShapeDtypeStruct((groups, share, modes), F32),
            jax.ShapeDtypeStruct((modes, depth), BF16),
        ],
        scratch_shapes=[
            pltpu.VMEM((modes, depth), BF16),
            pltpu.VMEM((chunk, depth), BF16),
            pltpu.VMEM((groups, share, modes), BF16),
            pltpu.VMEM((groups, share, modes), F32),
            pltpu.SemaphoreType.DMA((1,)),
            pltpu.SemaphoreType.DMA((2, groups)),
        ],
        name="project_stiff",
    )(block_map, fetched, matrix)


def mix_mass(qt, matrix, diagonal):
    modes, depth = qt.shape
    local_subs, boundary, _ = matrix.shape
    chunk = modes // 4

    def kernel(t_ref, m_ref, d_ref, y_ref):
        for s in range(local_subs):
            span = slice(s * boundary, (s + 1) * boundary)
            left = t_ref[:, span]
            y = jnp.dot(left, m_ref[s], preferred_element_type=F32)
            y_ref[:, span] = (y + left.astype(F32) * d_ref[s]).astype(BF16)

    rows = pl.BlockSpec((chunk, depth), lambda i: (i, 0))
    return pl.pallas_call(
        kernel,
        grid=(modes // chunk,),
        in_specs=[rows, whole(local_subs, boundary, boundary), whole(local_subs, 1, boundary)],
        out_specs=rows,
        out_shape=jax.ShapeDtypeStruct((modes, depth), BF16),
        name="mix_mass",
    )(qt, matrix, diagonal)


def project_mass(mixed, qt, dims):
    modes, depth = qt.shape
    groups = dims[0] * dims[1] * dims[2]
    share = modes // (2 * groups)
    chunk = modes // 2

    def kernel(y_ref, t_ref, send_ref, keep_ref, s_ref, k_ref, sem):
        out = lax.dot_general(
            y_ref[...], t_ref[...], (((1,), (1,)), ((), ())), preferred_element_type=F32
        )
        cut_shares(out, pl.program_id(0), 2, (s_ref, k_ref), (send_ref, keep_ref), sem, dims)

    return pl.pallas_call(
        kernel,
        grid=(2,),
        in_specs=[pl.BlockSpec((chunk, depth), lambda i: (i, 0)), whole(modes, depth)],
        out_specs=[ANY, ANY],
        out_shape=[
            jax.ShapeDtypeStruct((groups, share, modes), BF16),
            jax.ShapeDtypeStruct((groups, share, modes), F32),
        ],
        scratch_shapes=[
            pltpu.VMEM((groups, share, modes), BF16),
            pltpu.VMEM((groups, share, modes), F32),
            pltpu.SemaphoreType.DMA((2, groups)),
        ],
        name="project_mass",
    )(mixed, qt)


def swap(value, offset, device_count):
    return lax.ppermute(value, AXES, [(i, i ^ offset) for i in range(device_count)])


def reduce_shares(send, keep, sizes):
    got = swap(send, 1, sizes.devices)
    depth = sizes.devices // sizes.plane
    shape = (sizes.plane // 2, depth) + keep.shape[1:]
    keep, got = keep.reshape(shape), got.reshape(shape)
    summed = [keep[d] + got[d].astype(F32) for d in range(sizes.plane // 2)]
    total = summed[0]
    for d in range(1, sizes.plane // 2):
        got = swap(summed[d].astype(BF16), 2 * d, sizes.devices)
        total = total + got.astype(F32)
    result = total[0]
    for d in range(1, depth):
        got = swap(total[d].astype(BF16), d * sizes.plane, sizes.devices)
        result = result + got.astype(F32)
    return result


def spread_in_plane(blocks, sizes):
    near = [blocks[0]]
    for d in range(1, sizes.plane):
        near.append(swap(blocks[d], d, sizes.devices))
    return near


def regroup(near, z):
    return jnp.stack([part[z] for part in near])


def clear_tiles(table, sizes):
    shape = (sizes.row_blocks * BLK, sizes.col_blocks * BLK)

    def kernel(_table, stiff_ref, mass_ref, zero_ref, sem):
        zero_ref[...] = jnp.zeros_like(zero_ref)
        fills = [
            pltpu.make_async_copy(zero_ref, ref.at[pl.ds(i * BLK, BLK), :], sem.at[i, j])
            for i in range(sizes.row_blocks)
            for j, ref in enumerate((stiff_ref, mass_ref))
        ]
        for fill in fills:
            fill.start()
        for fill in fills:
            fill.wait()

    return pl.pallas_call(
        kernel,
        in_specs=[ANY],
        out_specs=[ANY, ANY],
        out_shape=[jax.ShapeDtypeStruct(shape, BF16), jax.ShapeDtypeStruct(shape, BF16)],
        scratch_shapes=[
            pltpu.VMEM((BLK, shape[1]), BF16),
            pltpu.SemaphoreType.DMA((sizes.row_blocks, 2)),
        ],
        name="clear_tiles",
    )(table)


def place(table, order, slots, arrived, stiff_tile, mass_tile, sizes):
    count = sizes.devices
    limit = sizes.row_blocks * sizes.col_blocks
    parts = len(arrived)
    height = 2 * BLK + EXTRA

    def kernel(*refs):
        table_ref, order_ref, slot_ref = refs[:3]
        in_refs = refs[3 : 3 + parts]
        stiff_ref, mass_ref, share_ref, held_ref, sums_ref, in_sem, sem = refs[-7:]
        me = lax.axis_index("row") * sizes.cols + lax.axis_index("col")
        loads, first = [], 0
        for i, ref in enumerate(in_refs):
            span = pl.ds(first, ref.shape[0])
            loads.append(pltpu.make_async_copy(ref, held_ref.at[span], in_sem.at[i]))
            first += ref.shape[0]
        for load in loads:
            load.start()
        for load in loads:
            load.wait()

        def copies(j):
            slot = slot_ref[j]
            row = pl.multiple_of(quotient(slot, sizes.col_blocks) * BLK, BLK)
            col = pl.multiple_of(remainder(slot, sizes.col_blocks) * BLK, BLK)
            return [
                pltpu.make_async_copy(
                    sums_ref.at[j, pl.ds(i * BLK, BLK)],
                    ref.at[pl.ds(row, BLK), pl.ds(col, BLK)],
                    sem.at[j, i],
                )
                for i, ref in enumerate((stiff_ref, mass_ref))
            ]

        def last(j):
            ahead = slot_ref[jnp.minimum(j + 1, count - 1)]
            ends = jnp.logical_or(j == count - 1, ahead != slot_ref[j])
            return jnp.logical_and(slot_ref[j] < limit, ends)

        def one(j, total):
            block = held_ref[order_ref[j] ^ me, : 2 * BLK].astype(F32)
            same = jnp.logical_and(j > 0, slot_ref[jnp.maximum(j - 1, 0)] == slot_ref[j])
            total = jnp.where(same, total + block, block)
            sums_ref[j] = total.astype(BF16)

            @pl.when(last(j))
            def _():
                for copy in copies(j):
                    copy.start()

            return total

        lax.fori_loop(0, count, one, jnp.zeros((2 * BLK, BLK), F32))
        share_ref[...] = jnp.zeros_like(share_ref)

        def add(device, carry):
            share = table_ref[device, sizes.ratio + 1]

            @pl.when(share >= 0)
            def _():
                parts = held_ref[device ^ me, 2 * BLK : 2 * BLK + EXTRA].astype(F32)
                share_ref[share] += parts[0:1] + parts[1:2] + parts[2:3]

            return carry

        lax.fori_loop(0, count, add, 0)

        def wait(j, carry):
            @pl.when(last(j))
            def _():
                for copy in copies(j):
                    copy.wait()

            return carry

        lax.fori_loop(0, count, wait, 0)

    return pl.pallas_call(
        kernel,
        in_specs=[SMEM, SMEM, SMEM] + [ANY] * (parts + 2),
        out_specs=[ANY, ANY, VMEM],
        out_shape=[
            jax.ShapeDtypeStruct(stiff_tile.shape, BF16),
            jax.ShapeDtypeStruct(mass_tile.shape, BF16),
            jax.ShapeDtypeStruct((sizes.share_blocks, 1, BLK), F32),
        ],
        input_output_aliases={3 + parts: 0, 4 + parts: 1},
        scratch_shapes=[
            pltpu.VMEM((count, height, BLK), BF16),
            pltpu.VMEM((count, 2 * BLK, BLK), BF16),
            pltpu.SemaphoreType.DMA((parts,)),
            pltpu.SemaphoreType.DMA((count, 2)),
        ],
        name="place",
    )(table, order, slots, *arrived, stiff_tile, mass_tile)


def reduction(inv_interior, coupling, boundary_stiff, mass_interior, mass_boundary, block_map, modes):
    row_count = lax.axis_size("row")
    col_count = lax.axis_size("col")
    tile_cols, width = modes.shape
    tile_rows = tile_cols * col_count // row_count
    sizes = Sizes(
        devices=row_count * col_count,
        cols=col_count,
        ratio=row_count // col_count,
        row_blocks=tile_rows // BLK,
        col_blocks=tile_cols // BLK,
        share_blocks=tile_rows // BLK // col_count,
        plane=col_count // 2 * col_count,
    )
    x_size = col_count // 2
    y_size = x_size
    dims = (row_count // y_size, y_size, x_size)
    depth = dims[0]

    table = exchange(describe(block_map, sizes))
    turned = jnp.swapaxes(modes.reshape(sizes.col_blocks, BLK, width), 1, 2)
    wanted = pick_modes(table, turned, sizes.ratio)
    fetched = exchange(wanted)
    stiff, mass, diagonal, *blocks = condense(
        block_map, inv_interior, coupling, boundary_stiff, mass_interior, mass_boundary, sizes
    )
    near = spread_in_plane(blocks, sizes)
    depth = dims[0]
    early = [swap(regroup(near[:CHIP], z), z * sizes.plane, sizes.devices) for z in range(2, depth)]
    stiff_tile, mass_tile = clear_tiles(table, sizes)
    late = [swap(regroup(near[CHIP:], z), z * sizes.plane, sizes.devices) for z in range(2, depth)]
    beside = swap(regroup(near, 1), sizes.plane, sizes.devices)
    arrived = [regroup(near, 0), beside]
    for pieces in zip(early, late):
        arrived.extend(pieces)

    fetched = fetched.reshape(row_count, col_count, sizes.ratio, width, BLK)
    send, keep, qt = project_stiff(block_map, fetched, stiff, dims, sizes.row_blocks)
    reduced_stiff = reduce_shares(send, keep, sizes)
    mixed = mix_mass(qt, mass, diagonal)
    send, keep = project_mass(mixed, qt, dims)
    reduced_mass = reduce_shares(send, keep, sizes)

    slot = table[:, sizes.ratio]
    ids = jnp.arange(sizes.devices, dtype=jnp.int32)
    before = jnp.logical_or(
        slot[None, :] < slot[:, None],
        jnp.logical_and(slot[None, :] == slot[:, None], ids[None, :] < ids[:, None]),
    )
    rank = jnp.sum(before.astype(jnp.int32), axis=1)
    chosen = rank[None, :] == ids[:, None]
    order = jnp.sum(jnp.where(chosen, ids[None, :], 0), axis=1)
    slots = jnp.sum(jnp.where(chosen, slot[None, :], 0), axis=1)
    stiff_tile, mass_tile, mass_share = place(
        table, order, slots, arrived, stiff_tile, mass_tile, sizes
    )
    return stiff_tile, mass_tile, reduced_stiff, reduced_mass, mass_share.reshape(-1)


def solution(mesh):
    return jax.shard_map(
        reduction,
        mesh=mesh,
        in_specs=(
            P(AXES, None, None),
            P(AXES, None, None),
            P(AXES, None, None),
            P(AXES, None),
            P(AXES, None),
            P(AXES, None),
            P("col", "row"),
        ),
        out_specs=(P("row", "col"), P("row", "col"), P(AXES, None), P(AXES, None), P(AXES)),
        check_vma=False,
    )
```

```python
from typing import NamedTuple

import jax
import jax.numpy as jnp
from jax import lax
from jax.experimental import pallas as pl
from jax.experimental.pallas import tpu as pltpu
from jax.sharding import PartitionSpec as P


BLK = 128
EXTRA = 8
AXES = ("row", "col")
F32 = jnp.float32
BF16 = jnp.bfloat16
VMEM = pl.BlockSpec(memory_space=pltpu.VMEM)
SMEM = pl.BlockSpec(memory_space=pltpu.SMEM)
ANY = pl.BlockSpec(memory_space=pl.ANY)


class Sizes(NamedTuple):
    devices: int
    cols: int
    ratio: int
    row_blocks: int
    col_blocks: int
    share_blocks: int
    plane: int


def exchange(value):
    return lax.all_to_all(value, AXES, split_axis=0, concat_axis=0, tiled=True)


def quotient(value, size):
    return lax.shift_right_logical(value, jnp.int32(size.bit_length() - 1))


def remainder(value, size):
    return value & jnp.int32(size - 1)


def describe(block_map, sizes):
    local_subs, per_sub = block_map.shape

    def kernel(map_ref, out_ref):
        shape = out_ref.shape
        device = lax.broadcasted_iota(jnp.int32, shape, 0)
        field = lax.broadcasted_iota(jnp.int32, shape, 1)
        row = quotient(device, sizes.cols)
        col = remainder(device, sizes.cols)
        zero = jnp.zeros(shape, jnp.int32)
        wanted, share = zero, zero - 1
        slot = zero + sizes.row_blocks * sizes.col_blocks
        for s in range(local_subs):
            row_slot, col_slot = zero - 1, zero - 1
            for a in range(per_sub):
                block = map_ref[s, a]
                tile_row = quotient(block, sizes.row_blocks)
                wanted = jnp.where(
                    col * sizes.ratio + field == tile_row, remainder(block, sizes.col_blocks), wanted
                )
                share = jnp.where(
                    device == quotient(block, sizes.share_blocks),
                    remainder(block, sizes.share_blocks),
                    share,
                )
                row_slot = jnp.where(row == tile_row, remainder(block, sizes.row_blocks), row_slot)
                col_slot = jnp.where(
                    col == quotient(block, sizes.col_blocks),
                    remainder(block, sizes.col_blocks),
                    col_slot,
                )
            both = jnp.logical_and(row_slot >= 0, col_slot >= 0)
            slot = jnp.where(both, row_slot * sizes.col_blocks + col_slot, slot)
        out_ref[...] = jnp.where(
            field < sizes.ratio, wanted, jnp.where(field == sizes.ratio, slot, share)
        )

    return pl.pallas_call(
        kernel,
        out_shape=jax.ShapeDtypeStruct((sizes.devices, BLK), jnp.int32),
        in_specs=[SMEM],
        out_specs=VMEM,
        name="describe",
    )(block_map)


def pick_modes(table, modes, ratio):
    device_count = table.shape[0]
    width = modes.shape[1]

    def kernel(table_ref, modes_ref, out_ref, sem):
        def copy(device, h):
            return pltpu.make_async_copy(
                modes_ref.at[table_ref[device, h]], out_ref.at[device, h], sem.at[device, h]
            )

        def start(device, carry):
            for h in range(ratio):
                copy(device, h).start()
            return carry

        def wait(device, carry):
            for h in range(ratio):
                copy(device, h).wait()
            return carry

        lax.fori_loop(0, device_count, start, 0, unroll=4)
        lax.fori_loop(0, device_count, wait, 0, unroll=4)

    return pl.pallas_call(
        kernel,
        out_shape=jax.ShapeDtypeStruct((device_count, ratio, width, BLK), BF16),
        in_specs=[SMEM, VMEM],
        out_specs=ANY,
        scratch_shapes=[pltpu.SemaphoreType.DMA((device_count, ratio))],
        name="pick_modes",
    )(table, modes)


def condense(
    block_map, inv_interior, coupling, boundary_stiff, mass_interior, mass_boundary, sizes
):
    local_subs, interior, boundary = coupling.shape
    per_sub = boundary // BLK

    def kernel(
        map_ref,
        inv_ref,
        cpl_ref,
        stiff_ref,
        mi_ref,
        mb_ref,
        k_ref,
        m_ref,
        d_ref,
        *refs,
    ):
        stiff_refs, mass_refs = refs[: sizes.plane], refs[sizes.plane : 2 * sizes.plane]
        out_k_ref, out_m_ref, sem = refs[-3:]
        sub = pl.program_id(0)
        me = lax.axis_index("row") * sizes.cols + lax.axis_index("col")
        couple = cpl_ref[0]
        static_modes = (-jnp.dot(inv_ref[0], couple, preferred_element_type=F32)).astype(BF16)
        contract = (((0,), (0,)), ((), ()))
        stiff = stiff_ref[0].astype(F32) + lax.dot_general(
            couple, static_modes, contract, preferred_element_type=F32
        )
        eye = lax.broadcasted_iota(jnp.int32, (BLK, BLK), 0) == lax.broadcasted_iota(
            jnp.int32, (BLK, BLK), 1
        )

        def own_row(ref):
            mine = lax.broadcasted_iota(jnp.int32, ref.shape, 0) == sub
            return jnp.sum(jnp.where(mine, ref[...], 0.0), axis=0, keepdims=True)

        masses, boundary_masses = own_row(mi_ref), own_row(mb_ref)
        column = jnp.concatenate(
            [
                jnp.sum(jnp.where(eye, masses[:, i : i + BLK], 0.0), axis=1, keepdims=True)
                for i in range(0, interior, BLK)
            ],
            axis=0,
        )
        weighted = (static_modes.astype(F32) * column).astype(BF16)
        mass = lax.dot_general(static_modes, weighted, contract, preferred_element_type=F32)
        level = lax.broadcasted_iota(jnp.int32, (EXTRA, BLK), 0)
        for a in range(per_sub):
            block_a = map_ref[sub, a]
            rows = slice(a * BLK, (a + 1) * BLK)
            for b in range(per_sub):
                cols = slice(b * BLK, (b + 1) * BLK)
                owner = quotient(block_a, sizes.row_blocks) * sizes.cols + quotient(
                    map_ref[sub, b], sizes.col_blocks
                )
                owner = owner ^ me
                near, far = remainder(owner, sizes.plane), quotient(owner, sizes.plane)
                stiff_block = stiff[rows, cols].astype(BF16)
                mass_block = mass[rows, cols]
                if a == b:
                    diagonal = (
                        jnp.sum(jnp.where(eye, mass_block, 0.0), axis=0, keepdims=True)
                        + boundary_masses[:, cols]
                    )
                    d_ref[0, :, cols] = diagonal
                    high = diagonal.astype(BF16).astype(F32)
                    middle = (diagonal - high).astype(BF16).astype(F32)
                    low = diagonal - high - middle
                    parts = jnp.where(level == 0, high, jnp.where(level == 1, middle, low))
                    share = quotient(block_a, sizes.share_blocks) ^ me
                    out_m_ref[
                        remainder(share, sizes.plane),
                        quotient(share, sizes.plane),
                        BLK : BLK + EXTRA,
                    ] = parts.astype(BF16)
                    mass_block = jnp.where(eye, 0.0, mass_block)
                mass_block = mass_block.astype(BF16)
                out_k_ref[near, far] = stiff_block
                out_m_ref[near, far, :BLK] = mass_block
                k_ref[0, rows, cols] = stiff_block
                m_ref[0, rows, cols] = mass_block

        @pl.when(sub == local_subs - 1)
        def _():
            copies = [
                pltpu.make_async_copy(held.at[d], ref, sem.at[i, d])
                for i, (held, near_refs) in enumerate(
                    ((out_k_ref, stiff_refs), (out_m_ref, mass_refs))
                )
                for d, ref in enumerate(near_refs)
            ]
            for copy in copies:
                copy.start()
            for copy in copies:
                copy.wait()

    def piece(*shape):
        return pl.BlockSpec((1,) + shape, lambda s: (s, 0, 0))

    out_k = (sizes.devices // sizes.plane, BLK, BLK)
    out_m = (sizes.devices // sizes.plane, BLK + EXTRA, BLK)
    return pl.pallas_call(
        kernel,
        grid=(local_subs,),
        in_specs=[
            SMEM,
            piece(interior, interior),
            piece(interior, boundary),
            piece(boundary, boundary),
            pl.BlockSpec((local_subs, interior), lambda s: (0, 0)),
            pl.BlockSpec((local_subs, boundary), lambda s: (0, 0)),
        ],
        out_specs=[
            piece(boundary, boundary),
            piece(boundary, boundary),
            piece(1, boundary),
        ]
        + [ANY] * (2 * sizes.plane),
        out_shape=[
            jax.ShapeDtypeStruct((local_subs, boundary, boundary), BF16),
            jax.ShapeDtypeStruct((local_subs, boundary, boundary), BF16),
            jax.ShapeDtypeStruct((local_subs, 1, boundary), F32),
        ]
        + [jax.ShapeDtypeStruct(out_k, BF16)] * sizes.plane
        + [jax.ShapeDtypeStruct(out_m, BF16)] * sizes.plane,
        scratch_shapes=[
            pltpu.VMEM((sizes.plane,) + out_k, BF16),
            pltpu.VMEM((sizes.plane,) + out_m, BF16),
            pltpu.SemaphoreType.DMA((2, sizes.plane)),
        ],
        name="condense",
    )(
        block_map,
        inv_interior,
        coupling,
        boundary_stiff,
        mass_interior,
        mass_boundary,
    )


def cut_shares(out, step, steps, held, results, sem, dims):
    z_size, y_size, x_size = dims
    groups, share, _ = results[0].shape
    pairs = out.shape[0] // (2 * share)
    row, col = lax.axis_index("row"), lax.axis_index("col")
    my_z, my_y = quotient(row, y_size), remainder(row, y_size)
    my_x, mine = quotient(col, 2), remainder(col, 2) == 0

    def copies(slot):
        return [
            pltpu.make_async_copy(ref.at[slot], result.at[slot], sem.at[i, slot])
            for i, (ref, result) in enumerate(zip(held, results))
        ]

    for i in range(pairs):
        group = step * pairs + i
        x = remainder(group, x_size)
        y = remainder(quotient(group, x_size), y_size)
        z = quotient(group, x_size * y_size)
        slot = ((y ^ my_y) * x_size + (x ^ my_x)) * z_size + (z ^ my_z)
        even = out[2 * i * share : (2 * i + 1) * share]
        odd = out[(2 * i + 1) * share : (2 * i + 2) * share]
        held[0][slot] = jnp.where(mine, odd, even).astype(BF16)
        held[1][slot] = jnp.where(mine, even, odd)
        for copy in copies(slot):
            copy.start()

    @pl.when(step == steps - 1)
    def _():
        for slot in range(groups):
            for copy in copies(slot):
                copy.wait()


def whole(*shape):
    return pl.BlockSpec(shape, lambda i: (0,) * len(shape))


def project_stiff(block_map, fetched, matrix, dims, row_blocks):
    local_subs, boundary, _ = matrix.shape
    depth = local_subs * boundary
    per_sub = boundary // BLK
    groups = dims[0] * dims[1] * dims[2]
    row_count, _, ratio, width, _ = fetched.shape
    modes = row_count * width
    share = modes // (2 * groups)
    chunk = modes // 2

    def kernel(
        map_ref, in_ref, m_ref, send_ref, keep_ref, qt_ref, t_ref, y_ref, s_ref, k_ref, t_sem, sem
    ):
        step = pl.program_id(0)
        copy_out = pltpu.make_async_copy(t_ref, qt_ref, t_sem.at[0])

        @pl.when(step == 0)
        def _():
            for s in range(local_subs):
                for a in range(per_sub):
                    tile_row = quotient(map_ref[s, a], row_blocks)
                    c = quotient(tile_row, ratio)
                    h = remainder(tile_row, ratio)
                    k = (s * per_sub + a) * BLK
                    for r in range(row_count):
                        t_ref[r * width : (r + 1) * width, k : k + BLK] = in_ref[r, c, h]
            copy_out.start()

        rows = pl.ds(pl.multiple_of(step * chunk, chunk), chunk)
        for s in range(local_subs):
            span = slice(s * boundary, (s + 1) * boundary)
            y_ref[:, span] = jnp.dot(
                t_ref[rows, span], m_ref[s], preferred_element_type=F32
            ).astype(BF16)
        out = lax.dot_general(
            y_ref[...], t_ref[...], (((1,), (1,)), ((), ())), preferred_element_type=F32
        )
        cut_shares(out, step, 2, (s_ref, k_ref), (send_ref, keep_ref), sem, dims)

        @pl.when(step == 1)
        def _():
            copy_out.wait()

    return pl.pallas_call(
        kernel,
        grid=(2,),
        in_specs=[SMEM, whole(*fetched.shape), whole(local_subs, boundary, boundary)],
        out_specs=[ANY, ANY, ANY],
        out_shape=[
            jax.ShapeDtypeStruct((groups, share, modes), BF16),
            jax.ShapeDtypeStruct((groups, share, modes), F32),
            jax.ShapeDtypeStruct((modes, depth), BF16),
        ],
        scratch_shapes=[
            pltpu.VMEM((modes, depth), BF16),
            pltpu.VMEM((chunk, depth), BF16),
            pltpu.VMEM((groups, share, modes), BF16),
            pltpu.VMEM((groups, share, modes), F32),
            pltpu.SemaphoreType.DMA((1,)),
            pltpu.SemaphoreType.DMA((2, groups)),
        ],
        name="project_stiff",
    )(block_map, fetched, matrix)


def mix_mass(qt, matrix, diagonal):
    modes, depth = qt.shape
    local_subs, boundary, _ = matrix.shape
    chunk = modes // 4

    def kernel(t_ref, m_ref, d_ref, y_ref):
        for s in range(local_subs):
            span = slice(s * boundary, (s + 1) * boundary)
            left = t_ref[:, span]
            y = jnp.dot(left, m_ref[s], preferred_element_type=F32)
            y_ref[:, span] = (y + left.astype(F32) * d_ref[s]).astype(BF16)

    rows = pl.BlockSpec((chunk, depth), lambda i: (i, 0))
    return pl.pallas_call(
        kernel,
        grid=(modes // chunk,),
        in_specs=[rows, whole(local_subs, boundary, boundary), whole(local_subs, 1, boundary)],
        out_specs=rows,
        out_shape=jax.ShapeDtypeStruct((modes, depth), BF16),
        name="mix_mass",
    )(qt, matrix, diagonal)


def project_mass(mixed, qt, dims):
    modes, depth = qt.shape
    groups = dims[0] * dims[1] * dims[2]
    share = modes // (2 * groups)
    chunk = modes // 2

    def kernel(y_ref, t_ref, send_ref, keep_ref, s_ref, k_ref, sem):
        out = lax.dot_general(
            y_ref[...], t_ref[...], (((1,), (1,)), ((), ())), preferred_element_type=F32
        )
        cut_shares(out, pl.program_id(0), 2, (s_ref, k_ref), (send_ref, keep_ref), sem, dims)

    return pl.pallas_call(
        kernel,
        grid=(2,),
        in_specs=[pl.BlockSpec((chunk, depth), lambda i: (i, 0)), whole(modes, depth)],
        out_specs=[ANY, ANY],
        out_shape=[
            jax.ShapeDtypeStruct((groups, share, modes), BF16),
            jax.ShapeDtypeStruct((groups, share, modes), F32),
        ],
        scratch_shapes=[
            pltpu.VMEM((groups, share, modes), BF16),
            pltpu.VMEM((groups, share, modes), F32),
            pltpu.SemaphoreType.DMA((2, groups)),
        ],
        name="project_mass",
    )(mixed, qt)


def swap(value, offset, device_count):
    return lax.ppermute(value, AXES, [(i, i ^ offset) for i in range(device_count)])


def reduce_shares(send, keep, sizes):
    got = swap(send, 1, sizes.devices)
    depth = sizes.devices // sizes.plane
    shape = (sizes.plane // 2, depth) + keep.shape[1:]
    keep, got = keep.reshape(shape), got.reshape(shape)
    summed = [keep[d] + got[d].astype(F32) for d in range(sizes.plane // 2)]
    total = summed[0]
    for d in range(1, sizes.plane // 2):
        got = swap(summed[d].astype(BF16), 2 * d, sizes.devices)
        total = total + got.astype(F32)
    result = total[0]
    for d in range(1, depth):
        got = swap(total[d].astype(BF16), d * sizes.plane, sizes.devices)
        result = result + got.astype(F32)
    return result


def spread_in_plane(blocks, sizes):
    near = [blocks[0]]
    for d in range(1, sizes.plane):
        near.append(swap(blocks[d], d, sizes.devices))
    return near


def regroup(near):
    plane, (depth, height, _) = len(near), near[0].shape

    def kernel(*refs):
        in_refs, out_refs, sem = refs[:plane], refs[plane : plane + depth], refs[-1]
        copies = [
            pltpu.make_async_copy(in_ref.at[z], out_ref.at[d], sem.at[d, z])
            for d, in_ref in enumerate(in_refs)
            for z, out_ref in enumerate(out_refs)
        ]
        for copy in copies:
            copy.start()
        for copy in copies:
            copy.wait()

    return pl.pallas_call(
        kernel,
        in_specs=[VMEM] * plane,
        out_specs=[ANY] * depth,
        out_shape=[jax.ShapeDtypeStruct((plane, height, BLK), BF16)] * depth,
        scratch_shapes=[pltpu.SemaphoreType.DMA((plane, depth))],
        name="regroup",
    )(*near)


def clear_tiles(table, sizes):
    shape = (sizes.row_blocks * BLK, sizes.col_blocks * BLK)

    def kernel(_table, stiff_ref, mass_ref, zero_ref, sem):
        zero_ref[...] = jnp.zeros_like(zero_ref)
        fills = [
            pltpu.make_async_copy(zero_ref, ref.at[pl.ds(i * BLK, BLK), :], sem.at[i, j])
            for i in range(sizes.row_blocks)
            for j, ref in enumerate((stiff_ref, mass_ref))
        ]
        for fill in fills:
            fill.start()
        for fill in fills:
            fill.wait()

    return pl.pallas_call(
        kernel,
        in_specs=[ANY],
        out_specs=[ANY, ANY],
        out_shape=[jax.ShapeDtypeStruct(shape, BF16), jax.ShapeDtypeStruct(shape, BF16)],
        scratch_shapes=[
            pltpu.VMEM((BLK, shape[1]), BF16),
            pltpu.SemaphoreType.DMA((sizes.row_blocks, 2)),
        ],
        name="clear_tiles",
    )(table)


def place(table, order, slots, arrived, tile, sizes):
    count = sizes.devices
    limit = sizes.row_blocks * sizes.col_blocks
    depth = len(arrived)
    height = arrived[0].shape[1]
    shared = height > BLK

    def kernel(*refs):
        table_ref, order_ref, slot_ref = refs[:3]
        in_refs = refs[3 : 3 + depth]
        tile_ref = refs[4 + depth]
        held_ref, sums_ref, in_sem, sem = refs[-4:]
        me = lax.axis_index("row") * sizes.cols + lax.axis_index("col")
        loads = [
            pltpu.make_async_copy(
                ref, held_ref.at[pl.ds(z * sizes.plane, sizes.plane)], in_sem.at[z]
            )
            for z, ref in enumerate(in_refs)
        ]
        for load in loads:
            load.start()
        for load in loads:
            load.wait()

        def copy(j):
            slot = slot_ref[j]
            row = pl.multiple_of(quotient(slot, sizes.col_blocks) * BLK, BLK)
            col = pl.multiple_of(remainder(slot, sizes.col_blocks) * BLK, BLK)
            return pltpu.make_async_copy(
                sums_ref.at[j], tile_ref.at[pl.ds(row, BLK), pl.ds(col, BLK)], sem.at[j]
            )

        def last(j):
            ahead = slot_ref[jnp.minimum(j + 1, count - 1)]
            ends = jnp.logical_or(j == count - 1, ahead != slot_ref[j])
            return jnp.logical_and(slot_ref[j] < limit, ends)

        def one(j, total):
            block = held_ref[order_ref[j] ^ me, :BLK].astype(F32)
            same = jnp.logical_and(j > 0, slot_ref[jnp.maximum(j - 1, 0)] == slot_ref[j])
            total = jnp.where(same, total + block, block)
            sums_ref[j] = total.astype(BF16)

            @pl.when(last(j))
            def _():
                copy(j).start()

            return total

        lax.fori_loop(0, count, one, jnp.zeros((BLK, BLK), F32))
        if shared:
            share_ref = refs[5 + depth]
            share_ref[...] = jnp.zeros_like(share_ref)

            def add(device, carry):
                share = table_ref[device, sizes.ratio + 1]

                @pl.when(share >= 0)
                def _():
                    parts = held_ref[device ^ me, BLK : BLK + EXTRA].astype(F32)
                    share_ref[share] += parts[0:1] + parts[1:2] + parts[2:3]

                return carry

            lax.fori_loop(0, count, add, 0)

        def wait(j, carry):
            @pl.when(last(j))
            def _():
                copy(j).wait()

            return carry

        lax.fori_loop(0, count, wait, 0)

    out_shape = [jax.ShapeDtypeStruct(tile.shape, BF16)]
    if shared:
        out_shape.append(jax.ShapeDtypeStruct((sizes.share_blocks, 1, BLK), F32))
    return pl.pallas_call(
        kernel,
        in_specs=[SMEM, SMEM, SMEM] + [ANY] * (depth + 1),
        out_specs=[ANY, VMEM][: len(out_shape)],
        out_shape=out_shape,
        input_output_aliases={3 + depth: 0},
        scratch_shapes=[
            pltpu.VMEM((count, height, BLK), BF16),
            pltpu.VMEM((count, BLK, BLK), BF16),
            pltpu.SemaphoreType.DMA((depth,)),
            pltpu.SemaphoreType.DMA((count,)),
        ],
        name="place_mass" if shared else "place_stiff",
    )(table, order, slots, *arrived, tile)


def reduction(inv_interior, coupling, boundary_stiff, mass_interior, mass_boundary, block_map, modes):
    row_count = lax.axis_size("row")
    col_count = lax.axis_size("col")
    tile_cols, width = modes.shape
    tile_rows = tile_cols * col_count // row_count
    sizes = Sizes(
        devices=row_count * col_count,
        cols=col_count,
        ratio=row_count // col_count,
        row_blocks=tile_rows // BLK,
        col_blocks=tile_cols // BLK,
        share_blocks=tile_rows // BLK // col_count,
        plane=col_count // 2 * col_count,
    )
    x_size = col_count // 2
    y_size = x_size
    dims = (row_count // y_size, y_size, x_size)

    table = exchange(describe(block_map, sizes))
    turned = jnp.swapaxes(modes.reshape(sizes.col_blocks, BLK, width), 1, 2)
    wanted = pick_modes(table, turned, sizes.ratio)
    fetched = exchange(wanted)
    stiff, mass, diagonal, *blocks = condense(
        block_map, inv_interior, coupling, boundary_stiff, mass_interior, mass_boundary, sizes
    )
    stiff_tile, mass_tile = clear_tiles(table, sizes)
    near_stiff = spread_in_plane(blocks[: sizes.plane], sizes)
    near_mass = spread_in_plane(blocks[sizes.plane :], sizes)

    def along_line(near):
        parts = regroup(near)
        arrived = [parts[0]]
        for d in range(1, dims[0]):
            arrived.append(swap(parts[d], d * sizes.plane, sizes.devices))
        return arrived

    stiff_arrived = along_line(near_stiff)
    mass_arrived = along_line(near_mass)

    fetched = fetched.reshape(row_count, col_count, sizes.ratio, width, BLK)
    send, keep, qt = project_stiff(block_map, fetched, stiff, dims, sizes.row_blocks)
    reduced_stiff = reduce_shares(send, keep, sizes)
    mixed = mix_mass(qt, mass, diagonal)
    send, keep = project_mass(mixed, qt, dims)
    reduced_mass = reduce_shares(send, keep, sizes)

    slot = table[:, sizes.ratio]
    ids = jnp.arange(sizes.devices, dtype=jnp.int32)
    before = jnp.logical_or(
        slot[None, :] < slot[:, None],
        jnp.logical_and(slot[None, :] == slot[:, None], ids[None, :] < ids[:, None]),
    )
    rank = jnp.sum(before.astype(jnp.int32), axis=1)
    chosen = rank[None, :] == ids[:, None]
    order = jnp.sum(jnp.where(chosen, ids[None, :], 0), axis=1)
    slots = jnp.sum(jnp.where(chosen, slot[None, :], 0), axis=1)
    (stiff_tile,) = place(table, order, slots, stiff_arrived, stiff_tile, sizes)
    mass_tile, mass_share = place(table, order, slots, mass_arrived, mass_tile, sizes)
    return stiff_tile, mass_tile, reduced_stiff, reduced_mass, mass_share.reshape(-1)


def solution(mesh):
    return jax.shard_map(
        reduction,
        mesh=mesh,
        in_specs=(
            P(AXES, None, None),
            P(AXES, None, None),
            P(AXES, None, None),
            P(AXES, None),
            P(AXES, None),
            P(AXES, None),
            P("col", "row"),
        ),
        out_specs=(P("row", "col"), P("row", "col"), P(AXES, None), P(AXES, None), P(AXES)),
        check_vma=False,
    )
```

```python
from typing import NamedTuple

import jax
import jax.numpy as jnp
from jax import lax
from jax.experimental import pallas as pl
from jax.experimental.pallas import tpu as pltpu
from jax.sharding import PartitionSpec as P


BLK = 128
EXTRA = 8
AXES = ("row", "col")
F32 = jnp.float32
BF16 = jnp.bfloat16
VMEM = pl.BlockSpec(memory_space=pltpu.VMEM)
SMEM = pl.BlockSpec(memory_space=pltpu.SMEM)
ANY = pl.BlockSpec(memory_space=pl.ANY)


class Sizes(NamedTuple):
    devices: int
    cols: int
    ratio: int
    row_blocks: int
    col_blocks: int
    share_blocks: int
    plane: int


def exchange(value):
    return lax.all_to_all(value, AXES, split_axis=0, concat_axis=0, tiled=True)


def quotient(value, size):
    return lax.shift_right_logical(value, jnp.int32(size.bit_length() - 1))


def remainder(value, size):
    return value & jnp.int32(size - 1)


def describe(block_map, sizes):
    local_subs, per_sub = block_map.shape

    def kernel(map_ref, out_ref):
        shape = out_ref.shape
        device = lax.broadcasted_iota(jnp.int32, shape, 0)
        field = lax.broadcasted_iota(jnp.int32, shape, 1)
        row = quotient(device, sizes.cols)
        col = remainder(device, sizes.cols)
        zero = jnp.zeros(shape, jnp.int32)
        wanted, share = zero, zero - 1
        slot = zero + sizes.row_blocks * sizes.col_blocks
        for s in range(local_subs):
            row_slot, col_slot = zero - 1, zero - 1
            for a in range(per_sub):
                block = map_ref[s, a]
                tile_row = quotient(block, sizes.row_blocks)
                wanted = jnp.where(
                    col * sizes.ratio + field == tile_row, remainder(block, sizes.col_blocks), wanted
                )
                share = jnp.where(
                    device == quotient(block, sizes.share_blocks),
                    remainder(block, sizes.share_blocks),
                    share,
                )
                row_slot = jnp.where(row == tile_row, remainder(block, sizes.row_blocks), row_slot)
                col_slot = jnp.where(
                    col == quotient(block, sizes.col_blocks),
                    remainder(block, sizes.col_blocks),
                    col_slot,
                )
            both = jnp.logical_and(row_slot >= 0, col_slot >= 0)
            slot = jnp.where(both, row_slot * sizes.col_blocks + col_slot, slot)
        out_ref[...] = jnp.where(
            field < sizes.ratio, wanted, jnp.where(field == sizes.ratio, slot, share)
        )

    return pl.pallas_call(
        kernel,
        out_shape=jax.ShapeDtypeStruct((sizes.devices, BLK), jnp.int32),
        in_specs=[SMEM],
        out_specs=VMEM,
        name="describe",
    )(block_map)


def pick_modes(table, modes, ratio):
    device_count = table.shape[0]
    width = modes.shape[1]

    steps = 4
    rows = device_count // steps

    def kernel(table_ref, modes_ref, out_ref):
        first = pl.program_id(0) * rows

        def one(i, carry):
            for h in range(ratio):
                out_ref[i, h] = modes_ref[table_ref[first + i, h]]
            return carry

        lax.fori_loop(0, rows, one, 0, unroll=4)

    return pl.pallas_call(
        kernel,
        grid=(steps,),
        out_shape=jax.ShapeDtypeStruct((device_count, ratio, width, BLK), BF16),
        in_specs=[SMEM, pl.BlockSpec(modes.shape, lambda i: (0, 0, 0))],
        out_specs=pl.BlockSpec((rows, ratio, width, BLK), lambda i: (i, 0, 0, 0)),
        name="pick_modes",
    )(table, modes)


def condense(
    block_map, inv_interior, coupling, boundary_stiff, mass_interior, mass_boundary, sizes
):
    local_subs, interior, boundary = coupling.shape
    per_sub = boundary // BLK

    def kernel(
        map_ref,
        inv_ref,
        cpl_ref,
        stiff_ref,
        mi_ref,
        mb_ref,
        k_ref,
        m_ref,
        d_ref,
        *refs,
    ):
        stiff_refs, mass_refs = refs[: sizes.plane], refs[sizes.plane : 2 * sizes.plane]
        out_k_ref, out_m_ref, sem = refs[-3:]
        sub = pl.program_id(0)
        me = lax.axis_index("row") * sizes.cols + lax.axis_index("col")
        couple = cpl_ref[0]
        static_modes = (-jnp.dot(inv_ref[0], couple, preferred_element_type=F32)).astype(BF16)
        contract = (((0,), (0,)), ((), ()))
        stiff = stiff_ref[0].astype(F32) + lax.dot_general(
            couple, static_modes, contract, preferred_element_type=F32
        )
        eye = lax.broadcasted_iota(jnp.int32, (BLK, BLK), 0) == lax.broadcasted_iota(
            jnp.int32, (BLK, BLK), 1
        )

        def own_row(ref):
            mine = lax.broadcasted_iota(jnp.int32, ref.shape, 0) == sub
            return jnp.sum(jnp.where(mine, ref[...], 0.0), axis=0, keepdims=True)

        masses, boundary_masses = own_row(mi_ref), own_row(mb_ref)
        column = jnp.concatenate(
            [
                jnp.sum(jnp.where(eye, masses[:, i : i + BLK], 0.0), axis=1, keepdims=True)
                for i in range(0, interior, BLK)
            ],
            axis=0,
        )
        weighted = (static_modes.astype(F32) * column).astype(BF16)
        mass = lax.dot_general(static_modes, weighted, contract, preferred_element_type=F32)
        level = lax.broadcasted_iota(jnp.int32, (EXTRA, BLK), 0)
        for a in range(per_sub):
            block_a = map_ref[sub, a]
            rows = slice(a * BLK, (a + 1) * BLK)
            for b in range(per_sub):
                cols = slice(b * BLK, (b + 1) * BLK)
                owner = quotient(block_a, sizes.row_blocks) * sizes.cols + quotient(
                    map_ref[sub, b], sizes.col_blocks
                )
                owner = owner ^ me
                near, far = remainder(owner, sizes.plane), quotient(owner, sizes.plane)
                stiff_block = stiff[rows, cols].astype(BF16)
                mass_block = mass[rows, cols]
                if a == b:
                    diagonal = (
                        jnp.sum(jnp.where(eye, mass_block, 0.0), axis=0, keepdims=True)
                        + boundary_masses[:, cols]
                    )
                    d_ref[0, :, cols] = diagonal
                    high = diagonal.astype(BF16).astype(F32)
                    middle = (diagonal - high).astype(BF16).astype(F32)
                    low = diagonal - high - middle
                    parts = jnp.where(level == 0, high, jnp.where(level == 1, middle, low))
                    share = quotient(block_a, sizes.share_blocks) ^ me
                    out_m_ref[
                        remainder(share, sizes.plane),
                        quotient(share, sizes.plane),
                        BLK : BLK + EXTRA,
                    ] = parts.astype(BF16)
                    mass_block = jnp.where(eye, 0.0, mass_block)
                mass_block = mass_block.astype(BF16)
                out_k_ref[near, far] = stiff_block
                out_m_ref[near, far, :BLK] = mass_block
                k_ref[0, rows, cols] = stiff_block
                m_ref[0, rows, cols] = mass_block

        @pl.when(sub == local_subs - 1)
        def _():
            copies = [
                pltpu.make_async_copy(held.at[d], ref, sem.at[i, d])
                for i, (held, near_refs) in enumerate(
                    ((out_k_ref, stiff_refs), (out_m_ref, mass_refs))
                )
                for d, ref in enumerate(near_refs)
            ]
            for copy in copies:
                copy.start()
            for copy in copies:
                copy.wait()

    def piece(*shape):
        return pl.BlockSpec((1,) + shape, lambda s: (s, 0, 0))

    out_k = (sizes.devices // sizes.plane, BLK, BLK)
    out_m = (sizes.devices // sizes.plane, BLK + EXTRA, BLK)
    return pl.pallas_call(
        kernel,
        grid=(local_subs,),
        in_specs=[
            SMEM,
            piece(interior, interior),
            piece(interior, boundary),
            piece(boundary, boundary),
            pl.BlockSpec((local_subs, interior), lambda s: (0, 0)),
            pl.BlockSpec((local_subs, boundary), lambda s: (0, 0)),
        ],
        out_specs=[
            piece(boundary, boundary),
            piece(boundary, boundary),
            piece(1, boundary),
        ]
        + [ANY] * (2 * sizes.plane),
        out_shape=[
            jax.ShapeDtypeStruct((local_subs, boundary, boundary), BF16),
            jax.ShapeDtypeStruct((local_subs, boundary, boundary), BF16),
            jax.ShapeDtypeStruct((local_subs, 1, boundary), F32),
        ]
        + [jax.ShapeDtypeStruct(out_k, BF16)] * sizes.plane
        + [jax.ShapeDtypeStruct(out_m, BF16)] * sizes.plane,
        scratch_shapes=[
            pltpu.VMEM((sizes.plane,) + out_k, BF16),
            pltpu.VMEM((sizes.plane,) + out_m, BF16),
            pltpu.SemaphoreType.DMA((2, sizes.plane)),
        ],
        name="condense",
    )(
        block_map,
        inv_interior,
        coupling,
        boundary_stiff,
        mass_interior,
        mass_boundary,
    )


def cut_shares(out, step, steps, held, results, sem, dims):
    z_size, y_size, x_size = dims
    groups, share, _ = results[0].shape
    pairs = out.shape[0] // (2 * share)
    row, col = lax.axis_index("row"), lax.axis_index("col")
    my_z, my_y = quotient(row, y_size), remainder(row, y_size)
    my_x, mine = quotient(col, 2), remainder(col, 2) == 0

    def copies(slot):
        return [
            pltpu.make_async_copy(ref.at[slot], result.at[slot], sem.at[i, slot])
            for i, (ref, result) in enumerate(zip(held, results))
        ]

    for i in range(pairs):
        group = step * pairs + i
        x = remainder(group, x_size)
        y = remainder(quotient(group, x_size), y_size)
        z = quotient(group, x_size * y_size)
        slot = ((y ^ my_y) * x_size + (x ^ my_x)) * z_size + (z ^ my_z)
        even = out[2 * i * share : (2 * i + 1) * share]
        odd = out[(2 * i + 1) * share : (2 * i + 2) * share]
        held[0][slot] = jnp.where(mine, odd, even).astype(BF16)
        held[1][slot] = jnp.where(mine, even, odd)
        for copy in copies(slot):
            copy.start()

    @pl.when(step == steps - 1)
    def _():
        for slot in range(groups):
            for copy in copies(slot):
                copy.wait()


def whole(*shape):
    return pl.BlockSpec(shape, lambda i: (0,) * len(shape))


def project_stiff(block_map, fetched, matrix, dims, row_blocks):
    local_subs, boundary, _ = matrix.shape
    depth = local_subs * boundary
    per_sub = boundary // BLK
    groups = dims[0] * dims[1] * dims[2]
    row_count, _, ratio, width, _ = fetched.shape
    modes = row_count * width
    share = modes // (2 * groups)
    chunk = modes // 2

    def kernel(
        map_ref, in_ref, m_ref, send_ref, keep_ref, qt_ref, t_ref, y_ref, s_ref, k_ref, t_sem, sem
    ):
        step = pl.program_id(0)
        copy_out = pltpu.make_async_copy(t_ref, qt_ref, t_sem.at[0])

        @pl.when(step == 0)
        def _():
            for s in range(local_subs):
                for a in range(per_sub):
                    tile_row = quotient(map_ref[s, a], row_blocks)
                    c = quotient(tile_row, ratio)
                    h = remainder(tile_row, ratio)
                    k = (s * per_sub + a) * BLK
                    for r in range(row_count):
                        t_ref[r * width : (r + 1) * width, k : k + BLK] = in_ref[r, c, h]
            copy_out.start()

        rows = pl.ds(pl.multiple_of(step * chunk, chunk), chunk)
        for s in range(local_subs):
            span = slice(s * boundary, (s + 1) * boundary)
            y_ref[:, span] = jnp.dot(
                t_ref[rows, span], m_ref[s], preferred_element_type=F32
            ).astype(BF16)
        out = lax.dot_general(
            y_ref[...], t_ref[...], (((1,), (1,)), ((), ())), preferred_element_type=F32
        )
        cut_shares(out, step, 2, (s_ref, k_ref), (send_ref, keep_ref), sem, dims)

        @pl.when(step == 1)
        def _():
            copy_out.wait()

    return pl.pallas_call(
        kernel,
        grid=(2,),
        in_specs=[SMEM, whole(*fetched.shape), whole(local_subs, boundary, boundary)],
        out_specs=[ANY, ANY, ANY],
        out_shape=[
            jax.ShapeDtypeStruct((groups, share, modes), BF16),
            jax.ShapeDtypeStruct((groups, share, modes), F32),
            jax.ShapeDtypeStruct((modes, depth), BF16),
        ],
        scratch_shapes=[
            pltpu.VMEM((modes, depth), BF16),
            pltpu.VMEM((chunk, depth), BF16),
            pltpu.VMEM((groups, share, modes), BF16),
            pltpu.VMEM((groups, share, modes), F32),
            pltpu.SemaphoreType.DMA((1,)),
            pltpu.SemaphoreType.DMA((2, groups)),
        ],
        name="project_stiff",
    )(block_map, fetched, matrix)


def mix_mass(qt, matrix, diagonal):
    modes, depth = qt.shape
    local_subs, boundary, _ = matrix.shape
    chunk = modes // 4

    def kernel(t_ref, m_ref, d_ref, y_ref):
        for s in range(local_subs):
            span = slice(s * boundary, (s + 1) * boundary)
            left = t_ref[:, span]
            y = jnp.dot(left, m_ref[s], preferred_element_type=F32)
            y_ref[:, span] = (y + left.astype(F32) * d_ref[s]).astype(BF16)

    rows = pl.BlockSpec((chunk, depth), lambda i: (i, 0))
    return pl.pallas_call(
        kernel,
        grid=(modes // chunk,),
        in_specs=[rows, whole(local_subs, boundary, boundary), whole(local_subs, 1, boundary)],
        out_specs=rows,
        out_shape=jax.ShapeDtypeStruct((modes, depth), BF16),
        name="mix_mass",
    )(qt, matrix, diagonal)


def project_mass(mixed, qt, dims):
    modes, depth = qt.shape
    groups = dims[0] * dims[1] * dims[2]
    share = modes // (2 * groups)
    chunk = modes // 2

    def kernel(y_ref, t_ref, send_ref, keep_ref, s_ref, k_ref, sem):
        out = lax.dot_general(
            y_ref[...], t_ref[...], (((1,), (1,)), ((), ())), preferred_element_type=F32
        )
        cut_shares(out, pl.program_id(0), 2, (s_ref, k_ref), (send_ref, keep_ref), sem, dims)

    return pl.pallas_call(
        kernel,
        grid=(2,),
        in_specs=[pl.BlockSpec((chunk, depth), lambda i: (i, 0)), whole(modes, depth)],
        out_specs=[ANY, ANY],
        out_shape=[
            jax.ShapeDtypeStruct((groups, share, modes), BF16),
            jax.ShapeDtypeStruct((groups, share, modes), F32),
        ],
        scratch_shapes=[
            pltpu.VMEM((groups, share, modes), BF16),
            pltpu.VMEM((groups, share, modes), F32),
            pltpu.SemaphoreType.DMA((2, groups)),
        ],
        name="project_mass",
    )(mixed, qt)


def swap(value, offset, device_count):
    return lax.ppermute(value, AXES, [(i, i ^ offset) for i in range(device_count)])


def reduce_shares(send, keep, sizes):
    got = swap(send, 1, sizes.devices)
    depth = sizes.devices // sizes.plane
    shape = (sizes.plane // 2, depth) + keep.shape[1:]
    keep, got = keep.reshape(shape), got.reshape(shape)
    summed = [keep[d] + got[d].astype(F32) for d in range(sizes.plane // 2)]
    total = summed[0]
    for d in range(1, sizes.plane // 2):
        got = swap(summed[d].astype(BF16), 2 * d, sizes.devices)
        total = total + got.astype(F32)
    result = total[0]
    for d in range(1, depth):
        got = swap(total[d].astype(BF16), d * sizes.plane, sizes.devices)
        result = result + got.astype(F32)
    return result


def spread_in_plane(blocks, sizes):
    near = [blocks[0]]
    for d in range(1, sizes.plane):
        near.append(swap(blocks[d], d, sizes.devices))
    return near


def regroup(near):
    plane, (depth, height, _) = len(near), near[0].shape
    parts = [jnp.zeros((plane, height, BLK), BF16)] * depth
    for d, piece in enumerate(near):
        parts = [
            lax.dynamic_update_slice(part, piece[z : z + 1], (d, 0, 0))
            for z, part in enumerate(parts)
        ]
    return parts


def clear_tiles(table, sizes):
    shape = (sizes.row_blocks * BLK, sizes.col_blocks * BLK)

    def kernel(_table, stiff_ref, mass_ref, zero_ref, sem):
        zero_ref[...] = jnp.zeros_like(zero_ref)
        fills = [
            pltpu.make_async_copy(zero_ref, ref.at[pl.ds(i * BLK, BLK), :], sem.at[i, j])
            for i in range(sizes.row_blocks)
            for j, ref in enumerate((stiff_ref, mass_ref))
        ]
        for fill in fills:
            fill.start()
        for fill in fills:
            fill.wait()

    return pl.pallas_call(
        kernel,
        in_specs=[ANY],
        out_specs=[ANY, ANY],
        out_shape=[jax.ShapeDtypeStruct(shape, BF16), jax.ShapeDtypeStruct(shape, BF16)],
        scratch_shapes=[
            pltpu.VMEM((BLK, shape[1]), BF16),
            pltpu.SemaphoreType.DMA((sizes.row_blocks, 2)),
        ],
        name="clear_tiles",
    )(table)


def place(table, order, slots, arrived, tile, sizes):
    count = sizes.devices
    limit = sizes.row_blocks * sizes.col_blocks
    depth = len(arrived)
    height = arrived[0].shape[1]
    shared = height > BLK

    def kernel(*refs):
        table_ref, order_ref, slot_ref = refs[:3]
        in_refs = refs[3 : 3 + depth]
        tile_ref = refs[4 + depth]
        held_ref, sums_ref, in_sem, sem = refs[-4:]
        me = lax.axis_index("row") * sizes.cols + lax.axis_index("col")
        loads = [
            pltpu.make_async_copy(
                ref, held_ref.at[pl.ds(z * sizes.plane, sizes.plane)], in_sem.at[z]
            )
            for z, ref in enumerate(in_refs)
        ]
        for load in loads:
            load.start()
        for load in loads:
            load.wait()

        def copy(j):
            slot = slot_ref[j]
            row = pl.multiple_of(quotient(slot, sizes.col_blocks) * BLK, BLK)
            col = pl.multiple_of(remainder(slot, sizes.col_blocks) * BLK, BLK)
            return pltpu.make_async_copy(
                sums_ref.at[j], tile_ref.at[pl.ds(row, BLK), pl.ds(col, BLK)], sem.at[j]
            )

        def last(j):
            ahead = slot_ref[jnp.minimum(j + 1, count - 1)]
            ends = jnp.logical_or(j == count - 1, ahead != slot_ref[j])
            return jnp.logical_and(slot_ref[j] < limit, ends)

        def one(j, total):
            block = held_ref[order_ref[j] ^ me, :BLK].astype(F32)
            same = jnp.logical_and(j > 0, slot_ref[jnp.maximum(j - 1, 0)] == slot_ref[j])
            total = jnp.where(same, total + block, block)
            sums_ref[j] = total.astype(BF16)

            @pl.when(last(j))
            def _():
                copy(j).start()

            return total

        lax.fori_loop(0, count, one, jnp.zeros((BLK, BLK), F32))
        if shared:
            share_ref = refs[5 + depth]
            share_ref[...] = jnp.zeros_like(share_ref)

            def add(device, carry):
                share = table_ref[device, sizes.ratio + 1]

                @pl.when(share >= 0)
                def _():
                    parts = held_ref[device ^ me, BLK : BLK + EXTRA].astype(F32)
                    share_ref[share] += parts[0:1] + parts[1:2] + parts[2:3]

                return carry

            lax.fori_loop(0, count, add, 0)

        def wait(j, carry):
            @pl.when(last(j))
            def _():
                copy(j).wait()

            return carry

        lax.fori_loop(0, count, wait, 0)

    out_shape = [jax.ShapeDtypeStruct(tile.shape, BF16)]
    if shared:
        out_shape.append(jax.ShapeDtypeStruct((sizes.share_blocks, 1, BLK), F32))
    return pl.pallas_call(
        kernel,
        in_specs=[SMEM, SMEM, SMEM] + [ANY] * (depth + 1),
        out_specs=[ANY, VMEM][: len(out_shape)],
        out_shape=out_shape,
        input_output_aliases={3 + depth: 0},
        scratch_shapes=[
            pltpu.VMEM((count, height, BLK), BF16),
            pltpu.VMEM((count, BLK, BLK), BF16),
            pltpu.SemaphoreType.DMA((depth,)),
            pltpu.SemaphoreType.DMA((count,)),
        ],
        name="place_mass" if shared else "place_stiff",
    )(table, order, slots, *arrived, tile)


def reduction(inv_interior, coupling, boundary_stiff, mass_interior, mass_boundary, block_map, modes):
    row_count = lax.axis_size("row")
    col_count = lax.axis_size("col")
    tile_cols, width = modes.shape
    tile_rows = tile_cols * col_count // row_count
    sizes = Sizes(
        devices=row_count * col_count,
        cols=col_count,
        ratio=row_count // col_count,
        row_blocks=tile_rows // BLK,
        col_blocks=tile_cols // BLK,
        share_blocks=tile_rows // BLK // col_count,
        plane=col_count // 2 * col_count,
    )
    x_size = col_count // 2
    y_size = x_size
    dims = (row_count // y_size, y_size, x_size)

    table = exchange(describe(block_map, sizes))
    turned = jnp.swapaxes(modes.reshape(sizes.col_blocks, BLK, width), 1, 2)
    wanted = pick_modes(table, turned, sizes.ratio)
    fetched = exchange(wanted)
    stiff, mass, diagonal, *blocks = condense(
        block_map, inv_interior, coupling, boundary_stiff, mass_interior, mass_boundary, sizes
    )
    stiff_tile, mass_tile = clear_tiles(table, sizes)
    near_stiff = spread_in_plane(blocks[: sizes.plane], sizes)
    near_mass = spread_in_plane(blocks[sizes.plane :], sizes)

    def along_line(near):
        parts = regroup(near)
        arrived = [parts[0]]
        for d in range(1, dims[0]):
            arrived.append(swap(parts[d], d * sizes.plane, sizes.devices))
        return arrived

    stiff_arrived = along_line(near_stiff)
    mass_arrived = along_line(near_mass)

    fetched = fetched.reshape(row_count, col_count, sizes.ratio, width, BLK)
    send, keep, qt = project_stiff(block_map, fetched, stiff, dims, sizes.row_blocks)
    reduced_stiff = reduce_shares(send, keep, sizes)
    mixed = mix_mass(qt, mass, diagonal)
    send, keep = project_mass(mixed, qt, dims)
    reduced_mass = reduce_shares(send, keep, sizes)

    slot = table[:, sizes.ratio]
    ids = jnp.arange(sizes.devices, dtype=jnp.int32)
    before = jnp.logical_or(
        slot[None, :] < slot[:, None],
        jnp.logical_and(slot[None, :] == slot[:, None], ids[None, :] < ids[:, None]),
    )
    rank = jnp.sum(before.astype(jnp.int32), axis=1)
    chosen = rank[None, :] == ids[:, None]
    order = jnp.sum(jnp.where(chosen, ids[None, :], 0), axis=1)
    slots = jnp.sum(jnp.where(chosen, slot[None, :], 0), axis=1)
    (stiff_tile,) = place(table, order, slots, stiff_arrived, stiff_tile, sizes)
    mass_tile, mass_share = place(table, order, slots, mass_arrived, mass_tile, sizes)
    return stiff_tile, mass_tile, reduced_stiff, reduced_mass, mass_share.reshape(-1)


def solution(mesh):
    return jax.shard_map(
        reduction,
        mesh=mesh,
        in_specs=(
            P(AXES, None, None),
            P(AXES, None, None),
            P(AXES, None, None),
            P(AXES, None),
            P(AXES, None),
            P(AXES, None),
            P("col", "row"),
        ),
        out_specs=(P("row", "col"), P("row", "col"), P(AXES, None), P(AXES, None), P(AXES)),
        check_vma=False,
    )
```

```python
from typing import NamedTuple

import jax
import jax.numpy as jnp
from jax import lax
from jax.experimental import pallas as pl
from jax.experimental.pallas import tpu as pltpu
from jax.sharding import PartitionSpec as P


BLK = 128
EXTRA = 8
AXES = ("row", "col")
F32 = jnp.float32
BF16 = jnp.bfloat16
VMEM = pl.BlockSpec(memory_space=pltpu.VMEM)
SMEM = pl.BlockSpec(memory_space=pltpu.SMEM)
ANY = pl.BlockSpec(memory_space=pl.ANY)


class Sizes(NamedTuple):
    devices: int
    cols: int
    ratio: int
    row_blocks: int
    col_blocks: int
    share_blocks: int
    plane: int


def exchange(value):
    return lax.all_to_all(value, AXES, split_axis=0, concat_axis=0, tiled=True)


def quotient(value, size):
    return lax.shift_right_logical(value, jnp.int32(size.bit_length() - 1))


def remainder(value, size):
    return value & jnp.int32(size - 1)


def describe(block_map, sizes):
    local_subs, per_sub = block_map.shape

    def kernel(map_ref, out_ref):
        shape = out_ref.shape
        device = lax.broadcasted_iota(jnp.int32, shape, 0)
        field = lax.broadcasted_iota(jnp.int32, shape, 1)
        row = quotient(device, sizes.cols)
        col = remainder(device, sizes.cols)
        zero = jnp.zeros(shape, jnp.int32)
        wanted, share = zero, zero - 1
        slot = zero + sizes.row_blocks * sizes.col_blocks
        for s in range(local_subs):
            row_slot, col_slot = zero - 1, zero - 1
            for a in range(per_sub):
                block = map_ref[s, a]
                tile_row = quotient(block, sizes.row_blocks)
                wanted = jnp.where(
                    col * sizes.ratio + field == tile_row, remainder(block, sizes.col_blocks), wanted
                )
                share = jnp.where(
                    device == quotient(block, sizes.share_blocks),
                    remainder(block, sizes.share_blocks),
                    share,
                )
                row_slot = jnp.where(row == tile_row, remainder(block, sizes.row_blocks), row_slot)
                col_slot = jnp.where(
                    col == quotient(block, sizes.col_blocks),
                    remainder(block, sizes.col_blocks),
                    col_slot,
                )
            both = jnp.logical_and(row_slot >= 0, col_slot >= 0)
            slot = jnp.where(both, row_slot * sizes.col_blocks + col_slot, slot)
        out_ref[...] = jnp.where(
            field < sizes.ratio, wanted, jnp.where(field == sizes.ratio, slot, share)
        )

    return pl.pallas_call(
        kernel,
        out_shape=jax.ShapeDtypeStruct((sizes.devices, BLK), jnp.int32),
        in_specs=[SMEM],
        out_specs=VMEM,
        name="describe",
    )(block_map)


def pick_modes(table, modes, ratio):
    device_count = table.shape[0]
    width = modes.shape[1]

    def kernel(table_ref, modes_ref, out_ref):
        def one(device, carry):
            for h in range(ratio):
                out_ref[device, h] = modes_ref[table_ref[device, h]]
            return carry

        lax.fori_loop(0, device_count, one, 0, unroll=4)

    return pl.pallas_call(
        kernel,
        out_shape=jax.ShapeDtypeStruct((device_count, ratio, width, BLK), BF16),
        in_specs=[SMEM, VMEM],
        out_specs=VMEM,
        name="pick_modes",
    )(table, modes)


def condense(
    block_map, inv_interior, coupling, boundary_stiff, mass_interior, mass_boundary, sizes
):
    local_subs, interior, boundary = coupling.shape
    per_sub = boundary // BLK

    def kernel(
        map_ref,
        inv_ref,
        cpl_ref,
        stiff_ref,
        mi_ref,
        mb_ref,
        k_ref,
        m_ref,
        d_ref,
        *refs,
    ):
        near_refs, out_ref, sem = refs[: sizes.plane], refs[-2], refs[-1]
        sub = pl.program_id(0)
        me = lax.axis_index("row") * sizes.cols + lax.axis_index("col")

        def own_row(ref):
            mine = lax.broadcasted_iota(jnp.int32, ref.shape, 0) == sub
            return jnp.sum(jnp.where(mine, ref[...], 0.0), axis=0, keepdims=True)

        masses, boundary_masses = own_row(mi_ref), own_row(mb_ref)
        contract = (((1,), (1,)), ((), ()))
        couple = cpl_ref[0].T
        static_modes = (
            -lax.dot_general(couple, inv_ref[0], contract, preferred_element_type=F32)
        ).astype(BF16)
        stiff = stiff_ref[0].astype(F32) + lax.dot_general(
            couple, static_modes, contract, preferred_element_type=F32
        )
        weighted = (static_modes.astype(F32) * masses).astype(BF16)
        mass = lax.dot_general(static_modes, weighted, contract, preferred_element_type=F32)
        eye = lax.broadcasted_iota(jnp.int32, (BLK, BLK), 0) == lax.broadcasted_iota(
            jnp.int32, (BLK, BLK), 1
        )
        level = lax.broadcasted_iota(jnp.int32, (EXTRA, BLK), 0)
        for a in range(per_sub):
            block_a = map_ref[sub, a]
            rows = slice(a * BLK, (a + 1) * BLK)
            for b in range(per_sub):
                cols = slice(b * BLK, (b + 1) * BLK)
                owner = quotient(block_a, sizes.row_blocks) * sizes.cols + quotient(
                    map_ref[sub, b], sizes.col_blocks
                )
                owner = owner ^ me
                near, far = remainder(owner, sizes.plane), quotient(owner, sizes.plane)
                stiff_block = stiff[rows, cols].astype(BF16)
                mass_block = mass[rows, cols]
                if a == b:
                    diagonal = (
                        jnp.sum(jnp.where(eye, mass_block, 0.0), axis=0, keepdims=True)
                        + boundary_masses[:, cols]
                    )
                    d_ref[0, :, cols] = diagonal
                    high = diagonal.astype(BF16).astype(F32)
                    middle = (diagonal - high).astype(BF16).astype(F32)
                    low = diagonal - high - middle
                    parts = jnp.where(level == 0, high, jnp.where(level == 1, middle, low))
                    share = quotient(block_a, sizes.share_blocks) ^ me
                    out_ref[
                        remainder(share, sizes.plane),
                        quotient(share, sizes.plane),
                        2 * BLK : 2 * BLK + EXTRA,
                    ] = parts.astype(BF16)
                    mass_block = jnp.where(eye, 0.0, mass_block)
                mass_block = mass_block.astype(BF16)
                out_ref[near, far, :BLK] = stiff_block
                out_ref[near, far, BLK : 2 * BLK] = mass_block
                k_ref[0, rows, cols] = stiff_block
                m_ref[0, rows, cols] = mass_block

        @pl.when(sub == local_subs - 1)
        def _():
            copies = [
                pltpu.make_async_copy(out_ref.at[d], ref, sem.at[d])
                for d, ref in enumerate(near_refs)
            ]
            for copy in copies:
                copy.start()
            for copy in copies:
                copy.wait()

    def piece(*shape):
        return pl.BlockSpec((1,) + shape, lambda s: (s, 0, 0))

    out_blocks = (sizes.devices // sizes.plane, 2 * BLK + EXTRA, BLK)
    return pl.pallas_call(
        kernel,
        grid=(local_subs,),
        in_specs=[
            SMEM,
            piece(interior, interior),
            piece(interior, boundary),
            piece(boundary, boundary),
            pl.BlockSpec((local_subs, interior), lambda s: (0, 0)),
            pl.BlockSpec((local_subs, boundary), lambda s: (0, 0)),
        ],
        out_specs=[
            piece(boundary, boundary),
            piece(boundary, boundary),
            piece(1, boundary),
        ]
        + [ANY] * sizes.plane,
        out_shape=[
            jax.ShapeDtypeStruct((local_subs, boundary, boundary), BF16),
            jax.ShapeDtypeStruct((local_subs, boundary, boundary), BF16),
            jax.ShapeDtypeStruct((local_subs, 1, boundary), F32),
        ]
        + [jax.ShapeDtypeStruct(out_blocks, BF16)] * sizes.plane,
        scratch_shapes=[
            pltpu.VMEM((sizes.plane,) + out_blocks, BF16),
            pltpu.SemaphoreType.DMA((sizes.plane,)),
        ],
        name="condense",
    )(
        block_map,
        inv_interior,
        coupling,
        boundary_stiff,
        mass_interior,
        mass_boundary,
    )


def cut_shares(out, step, steps, held, results, sem, dims):
    z_size, y_size, x_size = dims
    groups, share, _ = results[0].shape
    pairs = out.shape[0] // (2 * share)
    row, col = lax.axis_index("row"), lax.axis_index("col")
    my_z, my_y = quotient(row, y_size), remainder(row, y_size)
    my_x, mine = quotient(col, 2), remainder(col, 2) == 0

    def copies(slot):
        return [
            pltpu.make_async_copy(ref.at[slot], result.at[slot], sem.at[i, slot])
            for i, (ref, result) in enumerate(zip(held, results))
        ]

    for i in range(pairs):
        group = step * pairs + i
        x = remainder(group, x_size)
        y = remainder(quotient(group, x_size), y_size)
        z = quotient(group, x_size * y_size)
        slot = ((y ^ my_y) * x_size + (x ^ my_x)) * z_size + (z ^ my_z)
        even = out[2 * i * share : (2 * i + 1) * share]
        odd = out[(2 * i + 1) * share : (2 * i + 2) * share]
        held[0][slot] = jnp.where(mine, odd, even).astype(BF16)
        held[1][slot] = jnp.where(mine, even, odd)
        for copy in copies(slot):
            copy.start()

    @pl.when(step == steps - 1)
    def _():
        for slot in range(groups):
            for copy in copies(slot):
                copy.wait()


def whole(*shape):
    return pl.BlockSpec(shape, lambda i: (0,) * len(shape))


def project_stiff(block_map, fetched, matrix, dims, row_blocks):
    local_subs, boundary, _ = matrix.shape
    depth = local_subs * boundary
    per_sub = boundary // BLK
    groups = dims[0] * dims[1] * dims[2]
    row_count, _, ratio, width, _ = fetched.shape
    modes = row_count * width
    share = modes // (2 * groups)
    chunk = modes // 2

    def kernel(
        map_ref, in_ref, m_ref, send_ref, keep_ref, qt_ref, t_ref, y_ref, s_ref, k_ref, t_sem, sem
    ):
        step = pl.program_id(0)
        copy_out = pltpu.make_async_copy(t_ref, qt_ref, t_sem.at[0])

        @pl.when(step == 0)
        def _():
            for s in range(local_subs):
                for a in range(per_sub):
                    tile_row = quotient(map_ref[s, a], row_blocks)
                    c = quotient(tile_row, ratio)
                    h = remainder(tile_row, ratio)
                    k = (s * per_sub + a) * BLK
                    for r in range(row_count):
                        t_ref[r * width : (r + 1) * width, k : k + BLK] = in_ref[r, c, h]
            copy_out.start()

        rows = pl.ds(pl.multiple_of(step * chunk, chunk), chunk)
        for s in range(local_subs):
            span = slice(s * boundary, (s + 1) * boundary)
            y_ref[:, span] = jnp.dot(
                t_ref[rows, span], m_ref[s], preferred_element_type=F32
            ).astype(BF16)
        out = lax.dot_general(
            y_ref[...], t_ref[...], (((1,), (1,)), ((), ())), preferred_element_type=F32
        )
        cut_shares(out, step, 2, (s_ref, k_ref), (send_ref, keep_ref), sem, dims)

        @pl.when(step == 1)
        def _():
            copy_out.wait()

    return pl.pallas_call(
        kernel,
        grid=(2,),
        in_specs=[SMEM, whole(*fetched.shape), whole(local_subs, boundary, boundary)],
        out_specs=[ANY, ANY, ANY],
        out_shape=[
            jax.ShapeDtypeStruct((groups, share, modes), BF16),
            jax.ShapeDtypeStruct((groups, share, modes), F32),
            jax.ShapeDtypeStruct((modes, depth), BF16),
        ],
        scratch_shapes=[
            pltpu.VMEM((modes, depth), BF16),
            pltpu.VMEM((chunk, depth), BF16),
            pltpu.VMEM((groups, share, modes), BF16),
            pltpu.VMEM((groups, share, modes), F32),
            pltpu.SemaphoreType.DMA((1,)),
            pltpu.SemaphoreType.DMA((2, groups)),
        ],
        name="project_stiff",
    )(block_map, fetched, matrix)


def mix_mass(qt, matrix, diagonal):
    modes, depth = qt.shape
    local_subs, boundary, _ = matrix.shape
    chunk = modes // 4

    def kernel(t_ref, m_ref, d_ref, y_ref):
        for s in range(local_subs):
            span = slice(s * boundary, (s + 1) * boundary)
            left = t_ref[:, span]
            y = jnp.dot(left, m_ref[s], preferred_element_type=F32)
            y_ref[:, span] = (y + left.astype(F32) * d_ref[s]).astype(BF16)

    rows = pl.BlockSpec((chunk, depth), lambda i: (i, 0))
    return pl.pallas_call(
        kernel,
        grid=(modes // chunk,),
        in_specs=[rows, whole(local_subs, boundary, boundary), whole(local_subs, 1, boundary)],
        out_specs=rows,
        out_shape=jax.ShapeDtypeStruct((modes, depth), BF16),
        name="mix_mass",
    )(qt, matrix, diagonal)


def project_mass(mixed, qt, dims):
    modes, depth = qt.shape
    groups = dims[0] * dims[1] * dims[2]
    share = modes // (2 * groups)
    chunk = modes // 2

    def kernel(y_ref, t_ref, send_ref, keep_ref, s_ref, k_ref, sem):
        out = lax.dot_general(
            y_ref[...], t_ref[...], (((1,), (1,)), ((), ())), preferred_element_type=F32
        )
        cut_shares(out, pl.program_id(0), 2, (s_ref, k_ref), (send_ref, keep_ref), sem, dims)

    return pl.pallas_call(
        kernel,
        grid=(2,),
        in_specs=[pl.BlockSpec((chunk, depth), lambda i: (i, 0)), whole(modes, depth)],
        out_specs=[ANY, ANY],
        out_shape=[
            jax.ShapeDtypeStruct((groups, share, modes), BF16),
            jax.ShapeDtypeStruct((groups, share, modes), F32),
        ],
        scratch_shapes=[
            pltpu.VMEM((groups, share, modes), BF16),
            pltpu.VMEM((groups, share, modes), F32),
            pltpu.SemaphoreType.DMA((2, groups)),
        ],
        name="project_mass",
    )(mixed, qt)


def swap(value, offset, device_count):
    return lax.ppermute(value, AXES, [(i, i ^ offset) for i in range(device_count)])


def reduce_shares(send, keep, sizes):
    got = swap(send, 1, sizes.devices)
    depth = sizes.devices // sizes.plane
    shape = (sizes.plane // 2, depth) + keep.shape[1:]
    keep, got = keep.reshape(shape), got.reshape(shape)
    summed = [keep[d] + got[d].astype(F32) for d in range(sizes.plane // 2)]
    total = summed[0]
    for d in range(1, sizes.plane // 2):
        got = swap(summed[d].astype(BF16), 2 * d, sizes.devices)
        total = total + got.astype(F32)
    result = total[0]
    for d in range(1, depth):
        got = swap(total[d].astype(BF16), d * sizes.plane, sizes.devices)
        result = result + got.astype(F32)
    return result


def spread_in_plane(blocks, sizes):
    near = list(blocks)
    for d in reversed(range(1, sizes.plane)):
        near[d] = swap(blocks[d], d, sizes.devices)
    return [jnp.stack([part[z] for part in near]) for z in range(sizes.devices // sizes.plane)]


def clear_tiles(table, sizes):
    shape = (sizes.row_blocks * BLK, sizes.col_blocks * BLK)

    def kernel(_table, stiff_ref, mass_ref, zero_ref, sem):
        zero_ref[...] = jnp.zeros_like(zero_ref)
        fills = [
            pltpu.make_async_copy(zero_ref, ref.at[pl.ds(i * BLK, BLK), :], sem.at[i, j])
            for i in range(sizes.row_blocks)
            for j, ref in enumerate((stiff_ref, mass_ref))
        ]
        for fill in fills:
            fill.start()
        for fill in fills:
            fill.wait()

    return pl.pallas_call(
        kernel,
        in_specs=[ANY],
        out_specs=[ANY, ANY],
        out_shape=[jax.ShapeDtypeStruct(shape, BF16), jax.ShapeDtypeStruct(shape, BF16)],
        scratch_shapes=[
            pltpu.VMEM((BLK, shape[1]), BF16),
            pltpu.SemaphoreType.DMA((sizes.row_blocks, 2)),
        ],
        name="clear_tiles",
    )(table)


def place(table, order, slots, arrived, stiff_tile, mass_tile, sizes):
    count = sizes.devices
    limit = sizes.row_blocks * sizes.col_blocks
    depth = len(arrived)
    height = 2 * BLK + EXTRA

    def kernel(*refs):
        table_ref, order_ref, slot_ref = refs[:3]
        in_refs = refs[3 : 3 + depth]
        stiff_ref, mass_ref, share_ref, held_ref, sums_ref, in_sem, sem = refs[-7:]
        me = lax.axis_index("row") * sizes.cols + lax.axis_index("col")
        loads = [
            pltpu.make_async_copy(
                ref, held_ref.at[pl.ds(z * sizes.plane, sizes.plane)], in_sem.at[z]
            )
            for z, ref in enumerate(in_refs)
        ]
        for load in loads:
            load.start()
        for load in loads:
            load.wait()

        def copies(j):
            slot = slot_ref[j]
            row = pl.multiple_of(quotient(slot, sizes.col_blocks) * BLK, BLK)
            col = pl.multiple_of(remainder(slot, sizes.col_blocks) * BLK, BLK)
            return [
                pltpu.make_async_copy(
                    sums_ref.at[j, pl.ds(i * BLK, BLK)],
                    ref.at[pl.ds(row, BLK), pl.ds(col, BLK)],
                    sem.at[j, i],
                )
                for i, ref in enumerate((stiff_ref, mass_ref))
            ]

        def last(j):
            ahead = slot_ref[jnp.minimum(j + 1, count - 1)]
            ends = jnp.logical_or(j == count - 1, ahead != slot_ref[j])
            return jnp.logical_and(slot_ref[j] < limit, ends)

        def one(j, total):
            block = held_ref[order_ref[j] ^ me, : 2 * BLK].astype(F32)
            same = jnp.logical_and(j > 0, slot_ref[jnp.maximum(j - 1, 0)] == slot_ref[j])
            total = jnp.where(same, total + block, block)
            sums_ref[j] = total.astype(BF16)

            @pl.when(last(j))
            def _():
                for copy in copies(j):
                    copy.start()

            return total

        lax.fori_loop(0, count, one, jnp.zeros((2 * BLK, BLK), F32))
        share_ref[...] = jnp.zeros_like(share_ref)

        def add(device, carry):
            share = table_ref[device, sizes.ratio + 1]

            @pl.when(share >= 0)
            def _():
                parts = held_ref[device ^ me, 2 * BLK : 2 * BLK + EXTRA].astype(F32)
                share_ref[share] += parts[0:1] + parts[1:2] + parts[2:3]

            return carry

        lax.fori_loop(0, count, add, 0)

        def wait(j, carry):
            @pl.when(last(j))
            def _():
                for copy in copies(j):
                    copy.wait()

            return carry

        lax.fori_loop(0, count, wait, 0)

    return pl.pallas_call(
        kernel,
        in_specs=[SMEM, SMEM, SMEM] + [ANY] * (depth + 2),
        out_specs=[ANY, ANY, VMEM],
        out_shape=[
            jax.ShapeDtypeStruct(stiff_tile.shape, BF16),
            jax.ShapeDtypeStruct(mass_tile.shape, BF16),
            jax.ShapeDtypeStruct((sizes.share_blocks, 1, BLK), F32),
        ],
        input_output_aliases={3 + depth: 0, 4 + depth: 1},
        scratch_shapes=[
            pltpu.VMEM((count, height, BLK), BF16),
            pltpu.VMEM((count, 2 * BLK, BLK), BF16),
            pltpu.SemaphoreType.DMA((depth,)),
            pltpu.SemaphoreType.DMA((count, 2)),
        ],
        name="place",
    )(table, order, slots, *arrived, stiff_tile, mass_tile)


def reduction(inv_interior, coupling, boundary_stiff, mass_interior, mass_boundary, block_map, modes):
    row_count = lax.axis_size("row")
    col_count = lax.axis_size("col")
    tile_cols, width = modes.shape
    tile_rows = tile_cols * col_count // row_count
    sizes = Sizes(
        devices=row_count * col_count,
        cols=col_count,
        ratio=row_count // col_count,
        row_blocks=tile_rows // BLK,
        col_blocks=tile_cols // BLK,
        share_blocks=tile_rows // BLK // col_count,
        plane=col_count // 2 * col_count,
    )
    x_size = col_count // 2
    y_size = x_size
    dims = (row_count // y_size, y_size, x_size)

    table = exchange(describe(block_map, sizes))
    turned = jnp.swapaxes(modes.reshape(sizes.col_blocks, BLK, width), 1, 2)
    wanted = pick_modes(table, turned, sizes.ratio)
    fetched = exchange(wanted)
    stiff, mass, diagonal, *blocks = condense(
        block_map, inv_interior, coupling, boundary_stiff, mass_interior, mass_boundary, sizes
    )
    spread = spread_in_plane(blocks, sizes)
    beside = swap(spread[1], sizes.plane, sizes.devices)
    stiff_tile, mass_tile = clear_tiles(table, sizes)
    late, fetched, stiff_tile, mass_tile = lax.optimization_barrier(
        (spread[2:], fetched, stiff_tile, mass_tile)
    )
    late = [swap(part, (2 + d) * sizes.plane, sizes.devices) for d, part in enumerate(late)]
    arrived = [spread[0], beside, *late]

    fetched = fetched.reshape(row_count, col_count, sizes.ratio, width, BLK)
    send, keep, qt = project_stiff(block_map, fetched, stiff, dims, sizes.row_blocks)
    reduced_stiff = reduce_shares(send, keep, sizes)
    mixed = mix_mass(qt, mass, diagonal)
    send, keep = project_mass(mixed, qt, dims)
    reduced_mass = reduce_shares(send, keep, sizes)

    slot = table[:, sizes.ratio]
    ids = jnp.arange(sizes.devices, dtype=jnp.int32)
    before = jnp.logical_or(
        slot[None, :] < slot[:, None],
        jnp.logical_and(slot[None, :] == slot[:, None], ids[None, :] < ids[:, None]),
    )
    rank = jnp.sum(before.astype(jnp.int32), axis=1)
    chosen = rank[None, :] == ids[:, None]
    order = jnp.sum(jnp.where(chosen, ids[None, :], 0), axis=1)
    slots = jnp.sum(jnp.where(chosen, slot[None, :], 0), axis=1)
    stiff_tile, mass_tile, mass_share = place(
        table, order, slots, arrived, stiff_tile, mass_tile, sizes
    )
    return stiff_tile, mass_tile, reduced_stiff, reduced_mass, mass_share.reshape(-1)


def solution(mesh):
    return jax.shard_map(
        reduction,
        mesh=mesh,
        in_specs=(
            P(AXES, None, None),
            P(AXES, None, None),
            P(AXES, None, None),
            P(AXES, None),
            P(AXES, None),
            P(AXES, None),
            P("col", "row"),
        ),
        out_specs=(P("row", "col"), P("row", "col"), P(AXES, None), P(AXES, None), P(AXES)),
        check_vma=False,
    )
```
